32 devices in a mesh: dp: 8 (over z, y), expert: 4 (over x, core).
Axes of the slice: x: 2, y: 2, z: 4, core: 2. Of those that a mesh axis runs over, the one named last changes fastest.
Arguments:
- tokens: bfloat16 [2, 32, 256, 1024], P(None, ('dp', 'expert')), may hold values from -6 to 6
- lengths: int32 [2, 32], P(None, ('dp', 'expert')), may hold values from 1 to 256, 5120 in all within a row
- routes: int32 [2, 32, 256, 2], P(None, ('dp', 'expert')), may hold values from 0 to 3, all different within a row; in each aligned block of 256 rows (0 to 255, 256 to 511, ..., all dimensions but the last counted through in order) at most 160 rows name the same one
- cotangent: float32 [2, 32, 256, 1024], P(None, ('dp', 'expert')), may hold values from -6 to 6
- step_count: int32 [1], replicated, may hold values from 1 to 20
- qkv_master: float32 [1024, 3072], P('dp'), may hold values from -0.1875 to 0.1875
- qkv_first: float32 [1024, 3072], P('dp'), may hold values from -128 to 128
- qkv_second: float32 [1024, 3072], P('dp'), may hold values from 491.5 to 7864
- proj_master: float32 [1024, 1024], P('dp'), may hold values from -1 to 1
- proj_first: float32 [1024, 1024], P('dp'), may hold values from -6 to 6
- proj_second: float32 [1024, 1024], P('dp'), may hold values from 2.949 to 49.15
- table_master: float32 [32, 16], P('dp'), may hold values from -4 to 4
- table_first: float32 [32, 16], P('dp'), may hold values from -128 to 128
- table_second: float32 [32, 16], P('dp'), may hold values from 491.5 to 7864
- gains_master: float32 [2, 1024], P(None, 'dp'), may hold values from 0.5 to 1.5
- gains_first: float32 [2, 1024], P(None, 'dp'), may hold values from -128 to 128
- gains_second: float32 [2, 1024], P(None, 'dp'), may hold values from 491.5 to 7864
- router_master: float32 [1024, 4], P('dp'), may hold values from -0.375 to 0.375
- router_first: float32 [1024, 4], P('dp'), may hold values from -192 to 192
- router_second: float32 [1024, 4], P('dp'), may hold values from 983 to 19660
- expand_master: float32 [4, 1024, 5632], P('expert', 'dp'), may hold values from -0.1875 to 0.1875
- expand_first: float32 [4, 1024, 5632], P('expert', 'dp'), may hold values from -6 to 6
- expand_second: float32 [4, 1024, 5632], P('expert', 'dp'), may hold values from 1.4745 to 24.575
- shrink_master: float32 [4, 2816, 1024], P('expert', 'dp'), may hold values from -0.3125 to 0.3125
- shrink_first: float32 [4, 2816, 1024], P('expert', 'dp'), may hold values from -6 to 6
- shrink_second: float32 [4, 2816, 1024], P('expert', 'dp'), may hold values from 0.73725 to 9.83
Outputs:
- layer_out: bfloat16 [2, 32, 256, 1024], P(None, ('dp', 'expert'))
- token_grad: float32 [2, 32, 256, 1024], P(None, ('dp', 'expert'))
- qkv_weight: float32 [1024, 3072], P('dp')
- qkv_mean: float32 [1024, 3072], P('dp')
- qkv_square: float32 [1024, 3072], P('dp')
- proj_weight: float32 [1024, 1024], P('dp')
- proj_mean: float32 [1024, 1024], P('dp')
- proj_square: float32 [1024, 1024], P('dp')
- table_weight: float32 [32, 16], P('dp')
- table_mean: float32 [32, 16], P('dp')
- table_square: float32 [32, 16], P('dp')
- gains_weight: float32 [2, 1024], P(None, 'dp')
- gains_mean: float32 [2, 1024], P(None, 'dp')
- gains_square: float32 [2, 1024], P(None, 'dp')
- router_weight: float32 [1024, 4], P('dp')
- router_mean: float32 [1024, 4], P('dp')
- router_square: float32 [1024, 4], P('dp')
- expand_weight: float32 [4, 1024, 5632], P('expert', 'dp')
- expand_mean: float32 [4, 1024, 5632], P('expert', 'dp')
- expand_square: float32 [4, 1024, 5632], P('expert', 'dp')
- shrink_weight: float32 [4, 2816, 1024], P('expert', 'dp')
- shrink_mean: float32 [4, 2816, 1024], P('expert', 'dp')
- shrink_square: float32 [4, 2816, 1024], P('expert', 'dp')
The draws below stay inside these ranges and needn't reach their ends.
Inputs may be any that keep to these rules, and one draw needn't show every extreme that they name: `routes`: each slot names two different experts. Among the 256 slots of one sequence of one micro-batch, no expert is named more than 160 times, a bound that some block reaches. The lengths of one micro-batch sum to 5120, and the longest is 256.
All inputs are finite; a program needn't handle non-finite values. No bound on the sum of `lengths` on one device may be relied on, other than what follows from the above.
Results may differ from the reference program's by a relative error of at most 0.014.
The reference program's roundings to bfloat16 on the way count: a program that leaves them out, or rounds other values in their place, can miss the bound.
Values may be sent and summed in bfloat16 or wider, within the bound.
No kernel may reach another device: no remote copies, remote signals or barrier semaphores. Data moves between devices by JAX's collectives and lax.ppermute only.
A program may use at most 320 MiB of HBM per device.

```python
import math
import jax
import jax.numpy as jnp
import numpy as np
from jax import lax

D = 1024
HEADS = 16
HEAD = 64
FF = 2816
BUCKETS = 32
MB = 2
SEQ = 256
SEQS = 32
EXPERTS = 4
CAP = 160


def shard_levels(stream_key, extent, pieces, smallest, largest):
    def one(position, blocks):
        heights = jax.random.uniform(jax.random.fold_in(jax.random.fold_in(stream_key, 6), position), (blocks,), jnp.float32, smallest / len(pieces), largest / len(pieces))
        return jnp.repeat(jnp.exp(heights), extent[position] // blocks).reshape((-1,) + (1,) * (len(extent) - position - 1))

    level = one(*pieces[0])
    for cut in pieces[1:]:
        level = level * one(*cut)
    return level


def profile(number_of, total, bound, lean):
    weights = [(1 << 20) // math.isqrt(grade ** lean) + 1 for grade in range(2, number_of + 1)]
    surplus, given = total - bound - (number_of - 1), [1] * (number_of - 1)
    while surplus > 0:
        movable = [i for i in range(number_of - 1) if given[i] < bound]
        mass, budget = sum([weights[i] for i in movable]), surplus
        for i in movable:
            addition = min(bound - given[i], max(1, budget * weights[i] // mass), surplus)
            given[i] = given[i] + addition
            surplus = surplus - addition
    return np.array([bound] + given)


def ragged_sizes(stream_key, amount, total, most, skew):
    if amount == 2:
        one = jax.random.randint(stream_key, (), max(1, total - most), min(most, total - 1) + 1)
        return jnp.stack([one, total - one])
    sizes = jnp.asarray(profile(amount, total, most, skew), jnp.int32)
    pairs = (amount - 1) // 2
    source_of, sink = sizes[1:1 + 2 * pairs:2], sizes[2:2 + 2 * pairs:2]
    slack = jnp.minimum(source_of - 1, most - sink)
    moved = jax.random.randint(jax.random.fold_in(stream_key, 1), (pairs,), 0, 1 << 20) % (slack + 1)
    sizes = sizes.at[1:1 + 2 * pairs:2].set(source_of - moved).at[2:2 + 2 * pairs:2].set(sink + moved)
    return sizes[jax.random.permutation(jax.random.fold_in(stream_key, 2), amount)]


def deal_out(key, own, number, rows, count, top, limit, slope):
    ranking = jax.random.permutation(key, count)
    crowded, ordinary = shares(count, rows * top, limit, slope, True), shares(count, rows * top, limit, slope, False)
    places = jnp.arange(count)

    def named(tallies, rotation):
        used = int((tallies > 0).sum())
        fixed = max(1, used // 4)
        shifted = fixed + (places - fixed + rotation * (used - fixed)) % max(1, count - fixed)
        return jnp.zeros((count,), jnp.int32).at[ranking[jnp.where(places < fixed, places, shifted)]].set(jnp.asarray(tallies, jnp.int32))

    tallies = jnp.where(number % 4 == 0, named(crowded, number // 4), named(ordinary, number - number // 4 - 1))
    mixed = jax.random.permutation(jax.random.fold_in(own, 3), count)
    giver, sink = mixed[0:count // 2 * 2:2], mixed[1:count // 2 * 2:2]
    margin = jnp.minimum(tallies[giver] - 1, limit - tallies[sink]) // 2
    margin = jnp.where((giver == ranking[0]) | (sink == ranking[0]) | (tallies[sink] == 0), 0, jnp.maximum(margin, 0))
    shifted = jax.random.randint(jax.random.fold_in(own, 4), (count // 2,), 0, 1 << 20) % (margin + 1)
    tallies = tallies.at[giver].add(-shifted).at[sink].add(shifted)
    items = jnp.searchsorted(jnp.cumsum(tallies), jnp.arange(rows * top), side="right").astype(jnp.int32)
    grid = items.reshape(top, rows).T
    grid = grid[jax.random.permutation(jax.random.fold_in(own, 1), rows)]
    rotation = jax.random.randint(jax.random.fold_in(own, 2), (rows, 1), 0, top)
    return jnp.take_along_axis(grid, (jnp.arange(top)[None, :] + rotation) % top, axis=1)


def shares(amount, total, limit, slope, full):
    loads = [(1 << 20) // math.isqrt(standing ** slope) + 1 for standing in range(1, amount + 1)]
    largest = limit if full else min(limit, max(-(-total // amount), total * loads[0] // sum(loads)))
    least = 1 if total - largest >= amount - 1 else 0
    holding, spare = [largest] + [least] * (amount - 1), total - largest - least * (amount - 1)
    while spare > 0:
        candidates = [i for i in range(1, amount) if holding[i] < largest] or [i for i in range(1, amount) if holding[i] < limit]
        whole, left = sum([loads[i] for i in candidates]), spare
        for i in candidates:
            extra = min(limit - holding[i], max(1, left * loads[i] // whole), spare)
            holding[i] = holding[i] + extra
            spare = spare - extra
    return np.array(holding)


def scatter_about(stream_key, extent, scale, bound, shards=(), kind=jnp.bfloat16):
    level = shard_levels(stream_key, extent, shards, -0.22, 0.18) if shards else 1.0
    array = jax.random.normal(stream_key, extent, jnp.float32) * scale * level
    return jnp.minimum(jnp.maximum(array, -bound), bound).astype(kind)


def setup_inputs(seed: int = 0) -> dict:
    splits = jax.random.split(jax.random.key(seed), 27)
    tokens = scatter_about(splits[0], (MB, SEQS, SEQ, D), 1.0, 6.0, ((1, 32),))
    lengths = jax.vmap(lambda own: ragged_sizes(own, SEQS, 5 * SEQ * SEQS // 8, SEQ, 1))(jax.random.split(splits[1], MB)).reshape((MB, SEQS)).astype(jnp.int32)
    routes_keys = jax.random.split(jax.random.fold_in(splits[2], 1), MB * SEQS * SEQ // SEQ)
    routes_turns = jax.random.permutation(jax.random.fold_in(splits[2], 3), MB * SEQS * SEQ // SEQ)
    routes = jax.vmap(lambda own, number: deal_out(jax.random.fold_in(splits[2], 2), own, number, SEQ, EXPERTS, 2, CAP, 2))(routes_keys, routes_turns).reshape((MB, SEQS, SEQ, 2))
    cotangent = scatter_about(splits[3], (MB, SEQS, SEQ, D), 1.0, 6.0, ((1, 32),), jnp.float32)
    step_count = jax.random.randint(splits[4], (1,), 1, 21).astype(jnp.int32)
    qkv_master = scatter_about(splits[5], (D, 3 * D), D ** -0.5, 0.1875, ((0, 8),), jnp.float32)
    qkv_first = scatter_about(splits[6], (D, 3 * D), (0.22 * (MB * SEQ * SEQS * 3 // 5) ** 0.5), 128.0, ((0, 8),), jnp.float32)
    qkv_second = jnp.clip(jnp.exp(math.log(7864.0) - 2.7725887 * jax.random.uniform(splits[7], (D, 3 * D), jnp.float32) ** shard_levels(splits[7], (D, 3 * D), ((0, 8),), -0.2, 0.2)), 491.5, 7864.0)
    proj_master = scatter_about(splits[8], (D, D), (D // 32) ** -0.5, 1.0, ((0, 8),), jnp.float32)
    proj_first = scatter_about(splits[9], (D, D), (0.017 * (MB * SEQ * SEQS * 3 // 5) ** 0.5), 6.0, ((0, 8),), jnp.float32)
    proj_second = jnp.clip(jnp.exp(math.log(49.15) - 2.8134108 * jax.random.uniform(splits[10], (D, D), jnp.float32) ** shard_levels(splits[10], (D, D), ((0, 8),), -0.2, 0.2)), 2.949, 49.15)
    table_master = scatter_about(splits[11], (BUCKETS, HEADS), 0.25, 4.0, ((0, 8),), jnp.float32)
    table_first = scatter_about(splits[12], (BUCKETS, HEADS), (0.22 * (MB * SEQ * SEQS * 3 // 5) ** 0.5), 128.0, ((0, 8),), jnp.float32)
    table_second = jnp.clip(jnp.exp(math.log(7864.0) - 2.7725887 * jax.random.uniform(splits[13], (BUCKETS, HEADS), jnp.float32) ** shard_levels(splits[13], (BUCKETS, HEADS), ((0, 8),), -0.2, 0.2)), 491.5, 7864.0)
    gains_master = jnp.clip(1.0 + 0.1 * jax.random.normal(splits[14], (2, D), jnp.float32), 0.5, 1.5)
    gains_first = scatter_about(splits[15], (2, D), (0.22 * (MB * SEQ * SEQS * 3 // 5) ** 0.5), 128.0, ((1, 8),), jnp.float32)
    gains_second = jnp.clip(jnp.exp(math.log(7864.0) - 2.7725887 * jax.random.uniform(splits[16], (2, D), jnp.float32) ** shard_levels(splits[16], (2, D), ((1, 8),), -0.2, 0.2)), 491.5, 7864.0)
    router_master = scatter_about(splits[17], (D, EXPERTS), (D // 4) ** -0.5, 0.375, ((0, 8),), jnp.float32)
    router_first = scatter_about(splits[18], (D, EXPERTS), (0.33 * (MB * SEQ * SEQS * 3 // 5) ** 0.5), 192.0, ((0, 8),), jnp.float32)
    router_second = jnp.clip(jnp.exp(math.log(19660.0) - 2.9957323 * jax.random.uniform(splits[19], (D, EXPERTS), jnp.float32) ** shard_levels(splits[19], (D, EXPERTS), ((0, 8),), -0.2, 0.2)), 983.0, 19660.0)
    expand_master = scatter_about(splits[20], (EXPERTS, D, 2 * FF), D ** -0.5, 0.1875, ((0, 4), (1, 8)), jnp.float32)
    expand_first = scatter_about(splits[21], (EXPERTS, D, 2 * FF), (0.017 * (MB * SEQ * SEQS * 6 // (5 * EXPERTS)) ** 0.5), 6.0, ((0, 4), (1, 8)), jnp.float32)
    expand_second = jnp.clip(jnp.exp(math.log(24.575) - 2.8134108 * jax.random.uniform(splits[22], (EXPERTS, D, 2 * FF), jnp.float32) ** shard_levels(splits[22], (EXPERTS, D, 2 * FF), ((0, 4), (1, 8)), -0.2, 0.2)), 1.4745, 24.575)
    shrink_master = scatter_about(splits[23], (EXPERTS, FF, D), (FF // 8) ** -0.5, 0.3125, ((0, 4), (1, 8)), jnp.float32)
    shrink_first = scatter_about(splits[24], (EXPERTS, FF, D), (0.011 * (MB * SEQ * SEQS * 6 // (5 * EXPERTS)) ** 0.5), 6.0, ((0, 4), (1, 8)), jnp.float32)
    shrink_second = jnp.clip(jnp.exp(math.log(9.83) - 2.5902672 * jax.random.uniform(splits[25], (EXPERTS, FF, D), jnp.float32) ** shard_levels(splits[25], (EXPERTS, FF, D), ((0, 4), (1, 8)), -0.2, 0.2)), 0.73725, 9.83)
    return dict(tokens=tokens, lengths=lengths, routes=routes, cotangent=cotangent, step_count=step_count, qkv_master=qkv_master, qkv_first=qkv_first, qkv_second=qkv_second, proj_master=proj_master, proj_first=proj_first, proj_second=proj_second, table_master=table_master, table_first=table_first, table_second=table_second, gains_master=gains_master, gains_first=gains_first, gains_second=gains_second, router_master=router_master, router_first=router_first, router_second=router_second, expand_master=expand_master, expand_first=expand_first, expand_second=expand_second, shrink_master=shrink_master, shrink_first=shrink_first, shrink_second=shrink_second)


HIGHEST = lax.Precision.HIGHEST
epsilon_norm = 1e-06
beta_first = 0.9
beta_second = 0.95
adam_floor = 1e-08
decay_rate = 0.1
rate_table = (0.03, 0.1, 0.3, 0.1, 0.03, 0.03, 0.03)

@jax.custom_vjp
def low(v):
    return lax.optimization_barrier(v.astype(jnp.bfloat16)).astype(jnp.float32)

@jax.custom_vjp
def low_back(v):
    return v

def low_keep(v):
    return (low(v), None)

def low_pass(kept, grad):
    return (grad,)

def back_keep(v):
    return (v, None)

def back_low(kept, grad):
    return (low(grad),)
low.defvjp(low_keep, low_pass)
low_back.defvjp(back_keep, back_low)

def bucket_table(length, buckets):
    places = np.arange(length)
    spread = np.maximum(places[:, None] - places[None, :], 0)
    exact_span = buckets // 2
    scaled = np.log(np.maximum(spread, 1) / exact_span) / np.log(128.0 / exact_span)
    farther = np.minimum(exact_span + (scaled * (buckets - exact_span)).astype(np.int64), buckets - 1)
    return np.where(spread < exact_span, spread, farther).astype(np.int32)

def bucket_onehot(length, buckets):
    table_ids = jnp.asarray(bucket_table(length, buckets))
    return (table_ids[:, :, None] == jnp.arange(buckets, dtype=jnp.int32)).astype(jnp.float32)

def normalize(values, weights):
    return values * lax.rsqrt(lax.optimization_barrier(jnp.mean(values * values, axis=-1, keepdims=True)) + epsilon_norm) * weights

def attend_group(inputs, qkv_mat, proj_mat, bias_all, gain_rows):
    row_block, seq_lengths = inputs
    seq_count, length, model_width = row_block.shape
    normed = low(normalize(row_block, gain_rows[0]))
    packed = low_back(low(jnp.einsum('psd,de->pse', normed, qkv_mat, precision=HIGHEST)))
    packed = packed.reshape(seq_count, length, 3, HEADS, HEAD)
    queries = packed[:, :, 0]
    key_rows = packed[:, :, 1]
    value_rows = packed[:, :, 2]
    raw_scores = low_back(jnp.einsum('pihd,pjhd->phij', queries, key_rows, precision=HIGHEST) * HEAD ** (-0.5))
    places = jnp.arange(length, dtype=jnp.int32)
    allowed = (places[None, :, None] >= places[None, None, :]) & (places[None, None, :] < seq_lengths[:, None, None])
    scores = jnp.where(allowed[:, None], raw_scores + bias_all[None], -1e+30)
    attn_probs = jax.nn.softmax(scores, axis=-1)
    mixed_heads = jnp.einsum('phij,pjhd->pihd', low(attn_probs), value_rows, precision=HIGHEST)
    mixed_heads = low_back(low(mixed_heads.reshape(seq_count, length, model_width)))
    return row_block + low_back(jnp.einsum('psd,de->pse', mixed_heads, proj_mat, precision=HIGHEST))

def slot_index(route_rows, live_rows):
    expert_ids = jnp.arange(EXPERTS, dtype=jnp.int32)
    hit_table = (route_rows[:, :, None] == expert_ids).astype(jnp.int32) * live_rows[:, None, None].astype(jnp.int32)
    per_row = lax.optimization_barrier(jnp.sum(hit_table, axis=1)).astype(jnp.int32)
    earlier = (jnp.cumsum(per_row, axis=0).astype(jnp.int32) - per_row).astype(jnp.int32)
    slot_rank = lax.optimization_barrier(jnp.sum(hit_table * earlier[:, None, :], axis=2)).astype(jnp.int32)
    return jnp.where(live_rows[:, None], route_rows * CAP + slot_rank, EXPERTS * CAP).astype(jnp.int32)

def expert_apply(inputs):
    row_block, expand_mat, shrink_mat = inputs
    pre_act = low_back(jnp.dot(row_block, expand_mat, precision=HIGHEST))
    hidden = low(jax.nn.gelu(pre_act[:, :FF]) * pre_act[:, FF:])
    return low_back(low(jnp.dot(hidden, shrink_mat, precision=HIGHEST)))

def fill_slots(index_rows, normed_rows):
    spread = jnp.broadcast_to(normed_rows[:, None, :], (SEQ, 2, D)).reshape(2 * SEQ, D)
    return jnp.zeros((EXPERTS * CAP, D), jnp.float32).at[index_rows.reshape(-1)].set(spread, mode='drop')

def pick_rows(table_rows, index_rows):
    return table_rows[index_rows]

def forward(tokens_in, lengths, routes, qkv_mat, proj_mat, table_vals, gain_rows, router_mat, expand_mat, shrink_mat):
    blocks = MB * SEQS
    places = jnp.arange(SEQ, dtype=jnp.int32)
    live_rows = places[None, :] < lengths.reshape(blocks)[:, None]
    live_float = live_rows.astype(jnp.float32)
    bias_all = jnp.einsum('ijb,bh->hij', bucket_onehot(SEQ, BUCKETS), table_vals, precision=HIGHEST)
    group_size = math.gcd(blocks, max(1, 4096 // SEQ))
    row_block = tokens_in.reshape(blocks // group_size, group_size, SEQ, D)
    seq_lengths = lengths.reshape(blocks // group_size, group_size)
    attended = lax.map(jax.checkpoint(lambda inputs: attend_group(inputs, qkv_mat, proj_mat, bias_all, gain_rows)), (row_block, seq_lengths))
    resid_state = attended.reshape(blocks, SEQ, D)
    normed = low(normalize(resid_state, gain_rows[1]))
    router_probs = jax.nn.softmax(jnp.einsum('bsd,de->bse', normed, router_mat, precision=HIGHEST), axis=-1)
    route_rows = routes.reshape(blocks, SEQ, 2)
    slot_ids = jax.vmap(slot_index)(route_rows, live_rows)
    buffer = low_back(jax.vmap(fill_slots)(slot_ids, normed))
    by_expert = buffer.reshape(blocks, EXPERTS, CAP, D).transpose(1, 0, 2, 3).reshape(EXPERTS, blocks * CAP, D)
    results = lax.map(jax.checkpoint(expert_apply), (by_expert, expand_mat, shrink_mat))
    results = results.reshape(EXPERTS, blocks, CAP, D).transpose(1, 0, 2, 3).reshape(blocks, EXPERTS * CAP, D)
    clipped = jnp.minimum(slot_ids, EXPERTS * CAP - 1)
    picked = jax.vmap(pick_rows)(results, clipped)
    choose = (route_rows[..., None] == jnp.arange(EXPERTS, dtype=jnp.int32)).astype(jnp.float32)
    gate_probs = lax.optimization_barrier(jnp.sum(router_probs[:, :, None, :] * choose, axis=-1)) * live_float[..., None]
    mixture = lax.optimization_barrier(jnp.sum(gate_probs[..., None] * picked, axis=2))
    return (live_float[..., None] * (resid_state + mixture)).reshape(MB, SEQS, SEQ, D)

def adam_update(master, first_old, second, gradient, counter, learn_rate):
    first_new = beta_first * first_old + (1.0 - beta_first) * gradient
    second_new = beta_second * second + (1.0 - beta_second) * gradient * gradient
    first_hat = first_new / (1.0 - beta_first ** counter)
    second_hat = second_new / (1.0 - beta_second ** counter)
    master_new = master - learn_rate * (first_hat / (jnp.sqrt(second_hat) + adam_floor) + decay_rate * master)
    return (master_new, first_new, second_new)

def reference(tokens, lengths, routes, cotangent, step_count, qkv_master, qkv_first, qkv_second, proj_master, proj_first, proj_second, table_master, table_first, table_second, gains_master, gains_first, gains_second, router_master, router_first, router_second, expand_master, expand_first, expand_second, shrink_master, shrink_first, shrink_second):
    masters = (qkv_master, proj_master, table_master, gains_master, router_master, expand_master, shrink_master)
    firsts = (qkv_first, proj_first, table_first, gains_first, router_first, expand_first, shrink_first)
    seconds = (qkv_second, proj_second, table_second, gains_second, router_second, expand_second, shrink_second)
    rounded = tuple((master.astype(jnp.bfloat16).astype(jnp.float32) for master in masters))
    tokens_float = tokens.astype(jnp.float32)

    def wrapped(tokens_in, qkv_mat, proj_mat, table_vals, gain_rows, router_mat, expand_mat, shrink_mat):
        return forward(tokens_in, lengths, routes, qkv_mat, proj_mat, table_vals, gain_rows, router_mat, expand_mat, shrink_mat)
    primal, pullback = jax.vjp(wrapped, tokens_float, rounded[0], rounded[1], rounded[2], rounded[3], rounded[4], rounded[5], rounded[6])
    gradients = pullback(cotangent.astype(jnp.float32))
    counter = step_count[0].astype(jnp.float32)
    fresh = []
    for master, first_old, second, gradient, learn_rate in zip(masters, firsts, seconds, gradients[1:], rate_table):
        fresh.append(adam_update(master, first_old, second, gradient, counter, learn_rate))
    return (primal.astype(jnp.bfloat16), gradients[0], fresh[0][0], fresh[0][1], fresh[0][2], fresh[1][0], fresh[1][1], fresh[1][2], fresh[2][0], fresh[2][1], fresh[2][2], fresh[3][0], fresh[3][1], fresh[3][2], fresh[4][0], fresh[4][1], fresh[4][2], fresh[5][0], fresh[5][1], fresh[5][2], fresh[6][0], fresh[6][1], fresh[6][2])
```

```python
import functools

import jax
import jax.numpy as jnp
import numpy as np
from jax import lax
from jax.experimental import pallas as pl
from jax.experimental.pallas import tpu as pltpu
from jax.sharding import PartitionSpec as P

HEAD = 64
FF = 2816
BUCKETS = 32
MB = 2
TILE = 256
PARTS = (6, 5)
CALLS = ((3, 3), (3, 2))
RING_LIMIT = 8

HIGHEST = lax.Precision.HIGHEST
f32 = jnp.float32
bf16 = jnp.bfloat16
epsilon_norm = 1e-06
beta_first = 0.9
beta_second = 0.95
adam_floor = 1e-08
decay_rate = 0.1
rate_table = (0.03, 0.1, 0.3, 0.1, 0.03, 0.03, 0.03)
tanh_scale = 0.7978845608028654
tanh_cubic = 0.044715


def dot_nn(a, b):
    return lax.dot_general(a, b, (((1,), (0,)), ((), ())), preferred_element_type=f32)


def dot_nt(a, b):
    return lax.dot_general(a, b, (((1,), (1,)), ((), ())), preferred_element_type=f32)


def dot_tn(a, b):
    return lax.dot_general(a, b, (((0,), (0,)), ((), ())), preferred_element_type=f32)


def distance_buckets(length):
    spread = np.arange(length)
    exact_span = BUCKETS // 2
    scaled = np.log(np.maximum(spread, 1) / exact_span) / np.log(128.0 / exact_span)
    farther = np.minimum(
        exact_span + (scaled * (BUCKETS - exact_span)).astype(np.int64), BUCKETS - 1
    )
    return np.where(spread < exact_span, spread, farther).astype(np.int32)


def ring_order(count):
    if count % 2:
        return list(range(count))
    return list(range(0, count, 2)) + list(range(count - 1, 0, -2))


class Ring:
    def __init__(self):
        self.count = lax.axis_size("dp")
        self.order = ring_order(self.count)
        self.me = lax.axis_index("dp")
        places = np.argsort(np.array(self.order))
        self.place = jnp.asarray(places, jnp.int32)[self.me]
        self.members = jnp.asarray(self.order, jnp.int32)

    def member(self, offset):
        return self.members[(self.place + offset) % self.count]

    def step(self, values, way):
        n, order = self.count, self.order
        pairs = [(order[i], order[(i + way) % n]) for i in range(n)]
        return lax.ppermute(values, "dp", pairs)

    def gather(self, block, way):
        if self.count > RING_LIMIT:
            whole = lax.all_gather(block, "dp", axis=0)
            return whole, [block] * self.count
        zeros = (0,) * block.ndim
        whole = jnp.zeros((self.count,) + block.shape, block.dtype)
        whole = lax.dynamic_update_slice(whole, block[None], (self.me,) + zeros)
        arrived = [block]
        for hop in range(1, self.count):
            block = self.step(block, way)
            arrived.append(block)
            whole = lax.dynamic_update_slice(
                whole, block[None], (self.member(-way * hop),) + zeros
            )
        return whole, arrived

    def scatter(self, shares, way):
        if self.count > RING_LIMIT:
            return lax.psum_scatter(shares, "dp", scatter_dimension=0).astype(f32)

        def own(offset):
            return lax.dynamic_index_in_dim(shares, self.member(offset), 0, keepdims=False)

        block = own(-way).astype(bf16)
        for hop in range(1, self.count):
            block = self.step(block, way)
            block = block.astype(f32) + own(-way * (hop + 1)).astype(f32)
            if hop < self.count - 1:
                block = block.astype(bf16)
        return block


def swap(values, axis, bit):
    count = lax.axis_size(axis)
    return lax.ppermute(values, axis, [(i, i ^ bit) for i in range(count)])


def gather_small(values):
    count = lax.axis_size("dp")
    rows = values[None]
    bit = 1
    while bit < count:
        rows = jnp.concatenate([rows, swap(rows, "dp", bit)], axis=0)
        bit *= 2
    return rows[jnp.arange(count) ^ lax.axis_index("dp")]


def sum_small(values):
    for axis in ("expert", "dp"):
        bit = 1
        while bit < lax.axis_size(axis):
            values = values + swap(values, axis, bit)
            bit *= 2
    return values


def head_probs(query, key, bias_row, length):
    seq = query.shape[0]
    scores = dot_nt(query, key) * HEAD ** (-0.5)
    bias = pltpu.roll(
        jnp.broadcast_to(bias_row, (seq, seq)), 0, 1, stride=1, stride_axis=0
    )
    row = lax.broadcasted_iota(jnp.int32, (seq, seq), 0)
    column = lax.broadcasted_iota(jnp.int32, (seq, seq), 1)
    scores = jnp.where((column <= row) & (column < length), scores + bias, -1e30)
    exps = jnp.exp(scores - jnp.max(scores, axis=1, keepdims=True))
    return exps / jnp.sum(exps, axis=1, keepdims=True)


def attend_kernel(lengths, query, key, value, bias_rows, mixed):
    length = lengths[pl.program_id(0)]
    for half in range(2):
        c = pl.ds(HEAD * half, HEAD)
        probs = head_probs(query[:, c], key[:, c], bias_rows[0, half : half + 1, :], length)
        mixed[:, c] = dot_nn(probs.astype(bf16), value[:, c]).astype(bf16)


def attend_back_kernel(
    lengths, query, key, value, bias_rows, grad, grad_query, grad_key, grad_value, sums
):
    seq = query.shape[0]
    length = lengths[pl.program_id(0)]
    for half in range(2):
        c = pl.ds(HEAD * half, HEAD)
        q, k, v, g = query[:, c], key[:, c], value[:, c], grad[:, c]
        probs = head_probs(q, k, bias_rows[0, half : half + 1, :], length)
        grad_value[:, c] = dot_tn(probs.astype(bf16), g).astype(bf16)
        grad_probs = dot_nt(g, v)
        scores = probs * (grad_probs - jnp.sum(probs * grad_probs, axis=1, keepdims=True))
        rounded = scores.astype(bf16)
        grad_query[:, c] = (dot_nn(rounded, k) * HEAD ** (-0.5)).astype(bf16)
        grad_key[:, c] = (dot_tn(rounded, q) * HEAD ** (-0.5)).astype(bf16)
        eight = scores[0:8, :]
        for t in range(1, seq // 8):
            eight = eight + pltpu.roll(scores[8 * t : 8 * t + 8, :], seq - 8 * t, 1)
        total = eight[0:1, :]
        for t in range(1, 8):
            total = total + pltpu.roll(eight, seq - t, 1)[t : t + 1, :]
        sums[0, 0, half : half + 1, :] = total
    sums[0, 0, 2:8, :] = jnp.zeros((6, seq), f32)


def attend(lengths, packed, bias_rows, seq):
    width = packed.shape[1] // 3
    pairs = width // (2 * HEAD)

    def window(part):
        return pl.BlockSpec((seq, 2 * HEAD), lambda m, h, _: (m, part * pairs + h))

    return pl.pallas_call(
        attend_kernel,
        grid_spec=pltpu.PrefetchScalarGridSpec(
            num_scalar_prefetch=1,
            grid=(packed.shape[0] // seq, pairs),
            in_specs=[window(0), window(1), window(2)]
            + [pl.BlockSpec((1, 8, seq), lambda m, h, _: (h, 0, 0))],
            out_specs=window(0),
        ),
        out_shape=jax.ShapeDtypeStruct((packed.shape[0], width), bf16),
        name="attend",
    )(lengths, packed, packed, packed, bias_rows)


def attend_back(lengths, packed, bias_rows, grad, seq):
    rows, width = grad.shape
    pairs = width // (2 * HEAD)

    def window(part):
        return pl.BlockSpec((seq, 2 * HEAD), lambda m, h, _: (m, part * pairs + h))

    return pl.pallas_call(
        attend_back_kernel,
        grid_spec=pltpu.PrefetchScalarGridSpec(
            num_scalar_prefetch=1,
            grid=(rows // seq, pairs),
            in_specs=[window(0), window(1), window(2)]
            + [pl.BlockSpec((1, 8, seq), lambda m, h, _: (h, 0, 0)), window(0)],
            out_specs=[window(0)] * 3
            + [pl.BlockSpec((1, 1, 8, seq), lambda m, h, _: (m, h, 0, 0))],
        ),
        out_shape=[jax.ShapeDtypeStruct((rows, width), bf16)] * 3
        + [jax.ShapeDtypeStruct((rows // seq, pairs, 8, seq), f32)],
        name="attend_back",
    )(lengths, packed, packed, packed, bias_rows, grad)


def hidden_kernel(*refs, first):
    rows_in, turned, grads_in = refs[0:2], refs[2:4], refs[4:6]
    gate_mat, up_mat, shrink_mat = refs[6:9]
    out = refs[9 if first else 13 :]
    gate_grad, up_grad, shrink_grad, hidden, pre_gate, pre_up = out
    size = rows_in[0].shape[0]
    for m in range(MB):
        r = pl.ds(m * size, size)
        gate = dot_nn(rows_in[m][...], gate_mat[...])
        up = dot_nn(rows_in[m][...], up_mat[...])
        grad = dot_nt(grads_in[m][...], shrink_mat[...])
        bent = jnp.tanh(tanh_scale * (gate + tanh_cubic * (gate * gate * gate)))
        half = 0.5 * (1.0 + bent)
        gelu = gate * half
        slope = half + gate * (0.5 * (1.0 - bent * bent)) * (
            tanh_scale * (1.0 + 3.0 * tanh_cubic * gate * gate)
        )
        hidden[r, :] = (gelu * up).astype(bf16)
        pre_gate[r, :] = (slope * up * grad).astype(bf16)
        pre_up[r, :] = (gelu * grad).astype(bf16)
    lower, upper = pl.ds(0, size), pl.ds(size, size)
    gate_grad[...] = (
        dot_nn(turned[0][...], pre_gate[lower, :]) + dot_nn(turned[1][...], pre_gate[upper, :])
    ).astype(bf16)
    up_grad[...] = (
        dot_nn(turned[0][...], pre_up[lower, :]) + dot_nn(turned[1][...], pre_up[upper, :])
    ).astype(bf16)
    shrink_grad[...] = (
        dot_tn(hidden[lower, :], grads_in[0][...]) + dot_tn(hidden[upper, :], grads_in[1][...])
    ).astype(bf16)


def hidden_call(rows_in, turned, grads_in, gate_mat, up_mat, shrink_mat, kept, place, inner, tiles):
    size, width = rows_in[0].shape
    once = pl.Buffered(1)

    def full(shape):
        return pl.BlockSpec(shape, lambda j: (0, 0), pipeline_mode=once)

    def columns(rows, start):
        return pl.BlockSpec((rows, TILE), lambda j: (0, start + j))

    first = kept is None
    begin = place + inner
    in_specs = (
        [full((size, width))] * 2
        + [full((width, size))] * 2
        + [full((size, width))] * 2
        + [columns(width, inner)] * 2
        + [pl.BlockSpec((TILE, width), lambda j: (begin + j, 0))]
        + ([] if first else [pl.BlockSpec(memory_space=pl.ANY)] * 4)
    )
    out_specs = (
        [columns(width, 0)] * 2
        + [pl.BlockSpec((TILE, width), lambda j: (begin + j, 0))]
        + [columns(MB * size, begin)] * 3
    )
    out_shape = (
        [jax.ShapeDtypeStruct((width, tiles * TILE), bf16)] * 2
        + [jax.ShapeDtypeStruct((FF, width), bf16)]
        + [jax.ShapeDtypeStruct((MB * size, FF), bf16)] * 3
    )
    return pl.pallas_call(
        functools.partial(hidden_kernel, first=first),
        grid=(tiles,),
        in_specs=in_specs,
        out_specs=out_specs,
        out_shape=out_shape,
        input_output_aliases={} if first else {9: 2, 10: 3, 11: 4, 12: 5},
        compiler_params=pltpu.CompilerParams(
            dimension_semantics=("arbitrary",), vmem_limit_bytes=48 << 20
        ),
        name="hidden",
    )(*rows_in, *turned, *grads_in, gate_mat, up_mat, shrink_mat, *(() if first else kept))


def result_kernel(hidden, pre_gate, pre_up, shrink_mat, *refs):
    parts = len(PARTS)
    mats, (result, grad, result_sum, grad_sum) = refs[: 2 * parts], refs[2 * parts :]
    j = pl.program_id(0)

    @pl.when(j == 0)
    def _():
        result_sum[...] = jnp.zeros_like(result_sum)
        grad_sum[...] = jnp.zeros_like(grad_sum)

    result_sum[...] += dot_nn(hidden[...], shrink_mat[...])
    start = 0
    for p in range(parts):

        @pl.when((j >= start) & (j < start + PARTS[p]))
        def _(p=p):
            grad_sum[...] += dot_nt(pre_gate[...], mats[2 * p][...]) + dot_nt(
                pre_up[...], mats[2 * p + 1][...]
            )

        start += PARTS[p]

    @pl.when(j == pl.num_programs(0) - 1)
    def _():
        result[...] = result_sum[...].astype(bf16)
        grad[...] = grad_sum[...].astype(bf16)


def result_call(m, hidden, pre_gate, pre_up, shrink_mat, mats):
    width = shrink_mat.shape[1]
    size = hidden.shape[0] // MB
    tiles = FF // TILE
    mat_specs = []
    start = 0
    for count in PARTS:
        spec = pl.BlockSpec(
            (width, TILE),
            lambda j, start=start, count=count: (0, jnp.clip(j - start, 0, count - 1)),
        )
        mat_specs += [spec, spec]
        start += count
    return pl.pallas_call(
        result_kernel,
        grid=(tiles,),
        in_specs=[pl.BlockSpec((size, TILE), lambda j: (m, j))] * 3
        + [pl.BlockSpec((TILE, width), lambda j: (j, 0))]
        + mat_specs,
        out_specs=[pl.BlockSpec((size, width), lambda j: (0, 0))] * 2,
        out_shape=[jax.ShapeDtypeStruct((size, width), bf16)] * 2,
        scratch_shapes=[pltpu.VMEM((size, width), f32)] * 2,
        compiler_params=pltpu.CompilerParams(
            dimension_semantics=("arbitrary",), vmem_limit_bytes=40 << 20
        ),
        name="result",
    )(hidden, pre_gate, pre_up, shrink_mat, *mats)


def inverse_root(values):
    return lax.rsqrt(jnp.mean(values * values, axis=-1, keepdims=True) + epsilon_norm)


def norm_back(values, gain, grad):
    root = inverse_root(values)
    scaled = grad * gain
    inner = jnp.mean(scaled * values, axis=-1, keepdims=True)
    grad_values = root * scaled - values * (root * root * root * inner)
    return grad_values, jnp.sum(grad * values * root, axis=0)


def adam_update(master, first_old, second, gradient, counter, learn_rate):
    first_new = beta_first * first_old + (1.0 - beta_first) * gradient
    second_new = beta_second * second + (1.0 - beta_second) * gradient * gradient
    first_hat = first_new / (1.0 - beta_first**counter)
    second_hat = second_new / (1.0 - beta_second**counter)
    master_new = master - learn_rate * (
        first_hat / (jnp.sqrt(second_hat) + adam_floor) + decay_rate * master
    )
    return (master_new, first_new, second_new)


def after(values, *earlier):
    return lax.optimization_barrier((values,) + earlier)[0]


def body(
    tokens,
    lengths,
    routes,
    cotangent,
    step_count,
    qkv_master,
    qkv_first,
    qkv_second,
    proj_master,
    proj_first,
    proj_second,
    table_master,
    table_first,
    table_second,
    gains_master,
    gains_first,
    gains_second,
    router_master,
    router_first,
    router_second,
    expand_master,
    expand_first,
    expand_second,
    shrink_master,
    shrink_first,
    shrink_second,
):
    experts = lax.axis_size("expert")
    devices = lax.axis_size("dp")
    length, width = tokens.shape[2], tokens.shape[3]
    heads = width // HEAD
    capacity = 5 * length // (2 * experts)
    slots = experts * capacity
    rows = MB * length
    ring = Ring()
    lower = lax.axis_index("expert") % 2 == 0

    def mine(values):
        half = values.shape[-1] // 2
        return jnp.where(lower, values[..., :half], values[..., half:])

    def other(values):
        half = values.shape[-1] // 2
        return jnp.where(lower, values[..., half:], values[..., :half])

    def joined(own, others):
        return jnp.where(
            lower,
            jnp.concatenate([own, others], axis=-1),
            jnp.concatenate([others, own], axis=-1),
        )

    small = jnp.concatenate(
        [table_master.reshape(-1), gains_master.reshape(-1), router_master.reshape(-1)]
    ).astype(bf16)
    small = gather_small(small)
    cut_one = table_master.size
    cut_two = cut_one + gains_master.size
    table_vals = small[:, :cut_one].reshape(BUCKETS, heads).astype(f32)
    gains = small[:, cut_one:cut_two].reshape(devices, 2, width // devices)
    gains = gains.transpose(1, 0, 2).reshape(2, width).astype(f32)
    router_mat = small[:, cut_two:].reshape(width, experts)

    def dense_gather(master, held_back=()):
        half = mine(master).astype(bf16)
        if held_back:
            half = after(half, *held_back)
        cut = half.shape[1] // 2
        left, arrived = ring.gather(half[:, :cut], 1)
        right, _ = ring.gather(half[:, cut:], -1)
        own = [left.reshape(width, cut), right.reshape(width, cut)]
        return own, [swap(piece, "expert", 1) for piece in own], arrived

    qkv_own, qkv_other, qkv_arrived = dense_gather(qkv_master)
    proj_own, proj_other, proj_arrived = dense_gather(proj_master, (qkv_arrived[2],))

    shrink_rows = shrink_master.shape[1]
    shrink_local = after(shrink_master[0].astype(bf16), qkv_arrived[4])
    cut = shrink_rows // 2
    shrink_top, shrink_arrived = ring.gather(shrink_local[:cut], 1)
    shrink_low, _ = ring.gather(shrink_local[cut:], -1)
    shrink_mat = jnp.concatenate([shrink_top, shrink_low], axis=1).reshape(FF, width)

    expand_local = expand_master[0]
    mats = []
    start = 0
    arrived = shrink_arrived
    for count in PARTS:
        stop = start + count * TILE
        gate_local = expand_local[:, start:stop].astype(bf16)
        up_local = expand_local[:, FF + start : FF + stop].astype(bf16)
        gate_local, up_local, _ = lax.optimization_barrier(
            (gate_local, up_local, arrived[devices // 2 + 1])
        )
        gate_mat, arrived = ring.gather(gate_local, 1)
        up_mat, _ = ring.gather(up_local, -1)
        mats += [gate_mat.reshape(width, stop - start), up_mat.reshape(width, stop - start)]
        start = stop

    distance = (-np.arange(length)) % length
    onehot = jnp.asarray(
        (distance_buckets(length)[distance][:, None] == np.arange(BUCKETS)).astype(np.float32)
    )
    bias_rows = jnp.einsum("cb,bh->hc", onehot, table_vals, precision=HIGHEST)
    bias_rows = jnp.pad(
        bias_rows.reshape(heads // 2, 2, length), ((0, 0), (0, 6), (0, 0))
    )
    length_now = lengths[:, 0]
    places = jnp.arange(length, dtype=jnp.int32)
    live = places[None, :] < length_now[:, None]
    live_float = live.astype(f32)
    live_rows = live_float.reshape(rows, 1)
    inputs = tokens.reshape(rows, width).astype(f32)
    root_one = inverse_root(inputs)
    normed_one = (inputs * root_one * gains[0]).astype(bf16)

    def times(values, own, others):
        own_part = jnp.concatenate([dot_nn(values, piece) for piece in own], axis=1)
        other_part = jnp.concatenate([dot_nn(values, piece) for piece in others], axis=1)
        return own_part, other_part

    own_part, other_part = times(normed_one, qkv_own, qkv_other)
    packed = joined(own_part.astype(bf16), other_part.astype(bf16))
    mixed = attend(length_now, packed, bias_rows, length)
    own_part, other_part = times(mixed, proj_own, proj_other)
    state = inputs + joined(own_part, other_part)
    normed_two = (state * inverse_root(state) * gains[1]).astype(bf16)

    route_rows = routes.reshape(MB, length, 2)
    expert_ids = jnp.arange(experts, dtype=jnp.int32)
    choose = (route_rows[..., None] == expert_ids).astype(f32)
    hits = choose * live_float[:, :, None, None]
    per_row = jnp.sum(hits, axis=2)
    before = jnp.asarray(np.tril(np.ones((length, length), np.float32), -1)).astype(bf16)
    earlier = jnp.einsum(
        "ts,mse->mte", before, per_row.astype(bf16), preferred_element_type=f32
    )
    rank = jnp.sum(hits * earlier[:, :, None, :], axis=3).astype(jnp.int32)
    slot_ids = jnp.where(live[:, :, None], route_rows * capacity + rank, slots)
    picks = jnp.arange(slots, dtype=jnp.int32)[None, None, :, None] == jnp.swapaxes(
        slot_ids, 1, 2
    )[:, :, None, :]
    picks = picks.astype(bf16)
    both = picks[:, 0] + picks[:, 1]
    logits = jnp.dot(normed_two, router_mat, preferred_element_type=f32)
    router_probs = jax.nn.softmax(logits, axis=-1).reshape(MB, length, experts)
    gate_probs = jnp.sum(router_probs[:, :, None, :] * choose, axis=-1)
    gate_probs = gate_probs * live_float[:, :, None]
    grad_out = cotangent.reshape(rows, width) * live_rows
    grad_rows = (
        gate_probs.transpose(2, 0, 1)[..., None] * grad_out.reshape(MB, length, width)[None]
    ).astype(bf16)

    def exchange(values):
        values = values.reshape(experts, capacity, width)
        values = lax.all_to_all(values, "expert", split_axis=0, concat_axis=0, tiled=True)
        return values.reshape(slots, width)

    expert_rows, expert_grads = [], []
    for m in range(MB):
        send = dot_nn(both[m], normed_two[m * length : (m + 1) * length]).astype(bf16)
        expert_rows.append(exchange(send))
        send = dot_nn(picks[m, 0], grad_rows[0, m]) + dot_nn(picks[m, 1], grad_rows[1, m])
        expert_grads.append(exchange(send.astype(bf16)))
    turned = [values.T for values in expert_rows]

    kept = None
    place = 0
    expand_shares = []
    for p, calls in enumerate(CALLS):
        inner = 0
        for tiles in calls:
            gate_grad, up_grad, *kept = hidden_call(
                expert_rows,
                turned,
                expert_grads,
                mats[2 * p],
                mats[2 * p + 1],
                shrink_mat,
                kept,
                place,
                inner,
                tiles,
            )
            expand_shares.append((gate_grad, up_grad))
            inner += tiles
        place += PARTS[p]
    shrink_grad, *acts = kept
    block = width // devices
    gate_done, up_done = [], []
    for gate_grad, up_grad in expand_shares:
        gate_done.append(ring.scatter(gate_grad.reshape(devices, block, -1), 1))
        up_done.append(ring.scatter(up_grad.reshape(devices, block, -1), -1))
    expand_grad = jnp.concatenate(gate_done + up_done, axis=1)
    shrink_grad = shrink_grad.reshape(devices, 2, cut, width)
    shrink_grad = jnp.concatenate(
        [ring.scatter(shrink_grad[:, 0], 1), ring.scatter(shrink_grad[:, 1], -1)], axis=0
    )

    picked, back = [], []
    for m in range(MB):
        result, grad = result_call(m, *acts, shrink_mat, mats)
        result, grad = exchange(result), exchange(grad)
        picked.append([dot_tn(picks[m, k], result) for k in range(2)])
        back.append(dot_tn(both[m], grad))
    picked = [jnp.concatenate([picked[m][k] for m in range(MB)], axis=0) for k in range(2)]
    back = jnp.concatenate(back, axis=0)

    gates = gate_probs.reshape(rows, 2)
    mixture = gates[:, 0:1] * picked[0] + gates[:, 1:2] * picked[1]
    layer_out = (live_rows * (state + mixture)).astype(bf16)
    grad_gates = jnp.stack([jnp.sum(grad_out * values, axis=-1) for values in picked], axis=-1)
    probs_flat = router_probs.reshape(rows, experts)
    grad_probs = jnp.sum(grad_gates[:, :, None] * choose.reshape(rows, 2, experts), axis=1)
    grad_logits = probs_flat * (
        grad_probs - jnp.sum(probs_flat * grad_probs, axis=-1, keepdims=True)
    )
    router_grad = jnp.einsum(
        "td,te->de", normed_two.astype(f32), grad_logits, precision=HIGHEST
    )
    router_float = router_mat.astype(f32)
    for e in range(experts):
        back = back + grad_logits[:, e : e + 1] * router_float[:, e]
    grad_norm, gains_two_grad = norm_back(state, gains[1], back)
    grad_state = grad_out + grad_norm
    grad_attn = grad_state.astype(bf16)

    def dense_scatter(left, right):
        sent = dot_tn(left, other(right)).astype(bf16)
        share = dot_tn(left, mine(right)) + swap(sent, "expert", 1).astype(f32)
        share = share.astype(bf16).reshape(devices, block, -1)
        half = share.shape[-1] // 2
        done = jnp.concatenate(
            [ring.scatter(share[..., :half], 1), ring.scatter(share[..., half:], -1)], axis=1
        )
        bit = 2
        while bit < experts:
            done = done + swap(done, "expert", bit)
            bit *= 2
        return joined(done, swap(done, "expert", 1))

    def times_back(values, own, others):
        total = None
        for part, pieces in ((mine(values), own), (other(values), others)):
            half = part.shape[1] // 2
            for piece, cols in zip(pieces, (part[:, :half], part[:, half:])):
                term = dot_nt(cols, piece)
                total = term if total is None else total + term
        return total

    proj_grad = dense_scatter(mixed, grad_attn)
    grad_mixed = times_back(grad_attn, proj_own, proj_other).astype(bf16)
    grad_query, grad_key, grad_value, sums = attend_back(
        length_now, packed, bias_rows, grad_mixed, length
    )
    table_grad = jnp.einsum(
        "hc,cb->bh",
        jnp.sum(sums, axis=0)[:, :2].reshape(heads, length),
        onehot,
        precision=HIGHEST,
    )
    grad_packed = jnp.concatenate([grad_query, grad_key, grad_value], axis=1)
    qkv_grad = dense_scatter(normed_one, grad_packed)
    grad_normed = times_back(grad_packed, qkv_own, qkv_other)
    grad_norm, gains_one_grad = norm_back(inputs, gains[0], grad_normed)
    token_grad = grad_state + grad_norm

    flat = jnp.concatenate(
        [
            table_grad.reshape(devices, -1),
            jnp.stack([gains_one_grad, gains_two_grad])
            .reshape(2, devices, block)
            .transpose(1, 0, 2)
            .reshape(devices, -1),
            router_grad.reshape(devices, -1),
        ],
        axis=1,
    )
    flat = sum_small(flat)[ring.me]
    table_grad = flat[:cut_one].reshape(table_master.shape)
    gains_grad = flat[cut_one:cut_two].reshape(gains_master.shape)
    router_grad = flat[cut_two:].reshape(router_master.shape)

    counter = step_count[0].astype(f32)
    states = (
        (qkv_master, qkv_first, qkv_second, qkv_grad),
        (proj_master, proj_first, proj_second, proj_grad),
        (table_master, table_first, table_second, table_grad),
        (gains_master, gains_first, gains_second, gains_grad),
        (router_master, router_first, router_second, router_grad),
        (expand_master, expand_first, expand_second, expand_grad[None]),
        (shrink_master, shrink_first, shrink_second, shrink_grad[None]),
    )
    fresh = []
    for (master, first_old, second, gradient), learn_rate in zip(states, rate_table):
        fresh += adam_update(master, first_old, second, gradient, counter, learn_rate)
    return (
        layer_out.reshape(MB, 1, length, width),
        token_grad.reshape(MB, 1, length, width),
        *fresh,
    )


def solution(mesh):
    sequences = P(None, ("dp", "expert"), None, None)
    over_rows = P("dp", None)
    over_columns = P(None, "dp")
    by_expert = P("expert", "dp", None)
    weights = (
        (over_rows,) * 9 + (over_columns,) * 3 + (over_rows,) * 3 + (by_expert,) * 6
    )
    return jax.shard_map(
        body,
        mesh=mesh,
        in_specs=(sequences, P(None, ("dp", "expert")), sequences, sequences, P()) + weights,
        out_specs=(sequences, sequences) + weights,
        check_vma=False,
    )
```

```python
import functools

import jax
import jax.numpy as jnp
import numpy as np
from jax import lax
from jax.experimental import pallas as pl
from jax.experimental.pallas import tpu as pltpu
from jax.sharding import PartitionSpec as P

HEAD = 64
FF = 2816
BUCKETS = 32
MB = 2
TILE = 256
PARTS = (6, 5)
RING_LIMIT = 8
GATE = 3

HIGHEST = lax.Precision.HIGHEST
f32 = jnp.float32
bf16 = jnp.bfloat16
epsilon_norm = 1e-06
beta_first = 0.9
beta_second = 0.95
adam_floor = 1e-08
decay_rate = 0.1
rate_table = (0.03, 0.1, 0.3, 0.1, 0.03, 0.03)
rate_expand = np.float32(0.03)
tanh_scale = 0.7978845608028654
tanh_cubic = 0.044715


def dot_nn(a, b):
    return lax.dot_general(a, b, (((1,), (0,)), ((), ())), preferred_element_type=f32)


def dot_nt(a, b):
    return lax.dot_general(a, b, (((1,), (1,)), ((), ())), preferred_element_type=f32)


def dot_tn(a, b):
    return lax.dot_general(a, b, (((0,), (0,)), ((), ())), preferred_element_type=f32)


def cost(seconds):
    return pl.CostEstimate(
        flops=int(seconds * 1e15), transcendentals=0, bytes_accessed=int(seconds * 3e12)
    )


def distance_buckets(length):
    spread = np.arange(length)
    exact_span = BUCKETS // 2
    scaled = np.log(np.maximum(spread, 1) / exact_span) / np.log(128.0 / exact_span)
    farther = np.minimum(
        exact_span + (scaled * (BUCKETS - exact_span)).astype(np.int64), BUCKETS - 1
    )
    return np.where(spread < exact_span, spread, farther).astype(np.int32)


def ring_order(count):
    if count % 2:
        return list(range(count))
    return list(range(0, count, 2)) + list(range(count - 1, 0, -2))


class Ring:
    def __init__(self):
        self.count = n = lax.axis_size("dp")
        self.order = ring_order(n)
        self.me = me = lax.axis_index("dp")
        if n % 2:
            place = me
        else:
            place = jnp.where(me % 2 == 0, me // 2, n - (me + 1) // 2)
        self.others = []
        for offset in range(1, n if n <= RING_LIMIT else 1):
            other = lax.rem(place + offset, n)
            if n % 2 == 0:
                other = jnp.where(other < n // 2, 2 * other, 2 * n - 1 - 2 * other)
            self.others.append(other)

    def member(self, offset):
        offset %= self.count
        return self.others[offset - 1] if offset else self.me

    def step(self, values, way):
        n, order = self.count, self.order
        pairs = [(order[i], order[(i + way) % n]) for i in range(n)]
        return lax.ppermute(values, "dp", pairs)

    def hop(self, blocks, gate):
        if gate is not None:
            blocks = lax.optimization_barrier((*blocks, gate))[:2]
        return lax.optimization_barrier((self.step(blocks[0], 1), self.step(blocks[1], -1)))

    def gather(self, left, right, marks=None, gates=()):
        if self.count > RING_LIMIT:
            return lax.all_gather(left, "dp", axis=0), lax.all_gather(right, "dp", axis=0)

        def placed(whole, block, member):
            index = (member,) + (0,) * block.ndim
            return lax.dynamic_update_slice(
                whole, block[None], index, allow_negative_indices=False
            )

        blocks = (left, right)
        wholes = [
            placed(jnp.zeros((self.count,) + block.shape, block.dtype), block, self.me)
            for block in blocks
        ]
        for hop in range(1, self.count):
            blocks = self.hop(blocks, gates[hop - 1] if hop <= len(gates) else None)
            if marks is not None:
                marks.append(blocks[0])
            wholes = [
                placed(whole, block, self.member(-way * hop))
                for whole, block, way in zip(wholes, blocks, (1, -1))
            ]
        return wholes

    def scatter(self, left, right, gates=(), marks=None):
        if self.count > RING_LIMIT:
            return [
                lax.psum_scatter(shares, "dp", scatter_dimension=0).astype(f32)
                for shares in (left, right)
            ]

        def own(shares, offset):
            return lax.dynamic_index_in_dim(
                shares, self.member(offset), 0, keepdims=False, allow_negative_indices=False
            )

        blocks = [own(shares, -way) for shares, way in ((left, 1), (right, -1))]
        for hop in range(1, self.count):
            blocks = self.hop(blocks, gates[hop - 1] if hop <= len(gates) else None)
            blocks = [
                block.astype(f32) + own(shares, -way * (hop + 1)).astype(f32)
                for block, shares, way in zip(blocks, (left, right), (1, -1))
            ]
            if hop < self.count - 1:
                blocks = [block.astype(bf16) for block in blocks]
            if marks is not None:
                marks.append(blocks[0])
        return blocks


def swap(values, axis, bit):
    count = lax.axis_size(axis)
    return lax.ppermute(values, axis, [(i, i ^ bit) for i in range(count)])


def gather_small(values):
    count = lax.axis_size("dp")
    rows = values[None]
    bit = 1
    marks = []
    while bit < count:
        rows = jnp.concatenate([rows, swap(rows, "dp", bit)], axis=0)
        marks.append(rows)
        bit *= 2
    return rows[jnp.arange(count) ^ lax.axis_index("dp")], marks


def sum_small(values):
    marks = []
    for axis in ("expert", "dp"):
        bit = 1
        while bit < lax.axis_size(axis):
            values = values + swap(values, axis, bit)
            marks.append(values)
            bit *= 2
    return values, marks


def head_probs(query, key, bias_row, length):
    seq = query.shape[0]
    scores = dot_nt(query, key) * HEAD ** (-0.5)
    bias = pltpu.roll(
        jnp.broadcast_to(bias_row, (seq, seq)), 0, 1, stride=1, stride_axis=0
    )
    row = lax.broadcasted_iota(jnp.int32, (seq, seq), 0)
    column = lax.broadcasted_iota(jnp.int32, (seq, seq), 1)
    scores = jnp.where((column <= row) & (column < length), scores + bias, -1e30)
    exps = jnp.exp(scores - jnp.max(scores, axis=1, keepdims=True))
    return exps / jnp.sum(exps, axis=1, keepdims=True)


def attend_kernel(info, query, key, value, bias_rows, mixed):
    length = info[pl.program_id(0)]
    for half in range(2):
        c = pl.ds(HEAD * half, HEAD)
        probs = head_probs(query[:, c], key[:, c], bias_rows[0, half : half + 1, :], length)
        mixed[:, c] = dot_nn(probs.astype(bf16), value[:, c]).astype(bf16)


def diagonal_sums(values):
    seq = values.shape[0]
    eight = values[0:8, :]
    for t in range(1, seq // 8):
        eight = eight + pltpu.roll(values[8 * t : 8 * t + 8, :], seq - 8 * t, 1)
    total = eight[0:1, :]
    for t in range(1, 8):
        total = total + pltpu.roll(eight, seq - t, 1)[t : t + 1, :]
    return total


def attend_back_kernel(info, query, key, value, bias_rows, grad, grad_packed, sums):
    seq = query.shape[0]
    h = pl.program_id(0)
    length, core = info[0], info[1]
    places = packed_places(h, pl.num_programs(0), core)
    offsets = [pl.multiple_of(place * 2 * HEAD, 2 * HEAD) for place in places]
    parts = [[], [], []]
    for half in range(2):
        c = pl.ds(HEAD * half, HEAD)
        q, k, v, g = query[:, c], key[:, c], value[:, c], grad[:, c]
        probs = head_probs(q, k, bias_rows[0, half : half + 1, :], length)
        grad_probs = dot_nt(g, v)
        scores = probs * (grad_probs - jnp.sum(probs * grad_probs, axis=1, keepdims=True))
        rounded = scores.astype(bf16)
        parts[0].append((dot_nn(rounded, k) * HEAD ** (-0.5)).astype(bf16))
        parts[1].append((dot_tn(rounded, q) * HEAD ** (-0.5)).astype(bf16))
        parts[2].append(dot_tn(probs.astype(bf16), g).astype(bf16))
        sums[0, half : half + 1, :] = diagonal_sums(scores)
    sums[0, 2:8, :] = jnp.zeros((6, seq), f32)
    for offset, part in zip(offsets, parts):
        grad_packed[:, pl.ds(offset, 2 * HEAD)] = jnp.concatenate(part, axis=1)


def packed_places(h, pairs, core):
    half, quarter = pairs // 2, pairs // 4
    base = jnp.where(h // half == core, 0, 3 * half)
    i = lax.rem(h, half)
    value = jnp.where(i < quarter, half + i, 2 * half + i)
    return base + i, base + half + quarter + i, base + value


def pair_window(seq, pairs, part):
    return pl.BlockSpec(
        (seq, 2 * HEAD), lambda m, h, info: (m, packed_places(h, pairs, info[MB])[part])
    )


def attend(info, packed, bias_rows, seq):
    width = packed.shape[1] // 3
    pairs = width // (2 * HEAD)
    return pl.pallas_call(
        attend_kernel,
        grid_spec=pltpu.PrefetchScalarGridSpec(
            num_scalar_prefetch=1,
            grid=(packed.shape[0] // seq, pairs),
            in_specs=[pair_window(seq, pairs, part) for part in range(3)]
            + [pl.BlockSpec((1, 8, seq), lambda m, h, _: (h, 0, 0))],
            out_specs=pl.BlockSpec((seq, 2 * HEAD), lambda m, h, _: (m, h)),
        ),
        out_shape=jax.ShapeDtypeStruct((packed.shape[0], width), bf16),
        cost_estimate=cost(20e-6),
        name="attend",
    )(info, packed, packed, packed, bias_rows)


def attend_back(m, info, packed, bias_rows, grad):
    seq, width = grad.shape
    pairs = width // (2 * HEAD)

    def window(part):
        return pl.BlockSpec(
            (seq, 2 * HEAD), lambda h, info: (m, packed_places(h, pairs, info[1])[part])
        )

    return pl.pallas_call(
        attend_back_kernel,
        grid_spec=pltpu.PrefetchScalarGridSpec(
            num_scalar_prefetch=1,
            grid=(pairs,),
            in_specs=[window(0), window(1), window(2)]
            + [
                pl.BlockSpec((1, 8, seq), lambda h, _: (h, 0, 0)),
                pl.BlockSpec((seq, 2 * HEAD), lambda h, _: (0, h)),
            ],
            out_specs=[
                pl.BlockSpec((seq, 3 * width), lambda h, _: (0, 0)),
                pl.BlockSpec((1, 8, seq), lambda h, _: (h, 0, 0)),
            ],
        ),
        out_shape=[
            jax.ShapeDtypeStruct((seq, 3 * width), bf16),
            jax.ShapeDtypeStruct((pairs, 8, seq), f32),
        ],
        cost_estimate=cost(16e-6),
        name="attend_back",
    )(jnp.stack([info[m], info[MB]]), packed, packed, packed, bias_rows, grad)


SLOT_LANE, GATE_LANE = 16, 18


def halves(values, core):
    half = values.shape[1] // 2
    turned = jnp.concatenate([values[:, half:], values[:, :half]], axis=1)
    return jnp.where(core == 0, values, turned)


def pick_table(slot, slots):
    lane = lax.broadcasted_iota(jnp.int32, (slot.shape[0], slots), 1).astype(f32)
    return jnp.where(lane == slot, 1.0, 0.0).astype(bf16)


def route_kernel(info, inputs, mixed, *refs, capacity):
    pieces, refs = refs[:4], refs[4:]
    gain, router, routes, cotangent, state, normed, aux, *outs = refs
    length, me, core = info[0], info[1], info[2]
    seq = inputs.shape[0]
    experts = len(outs)
    added = jnp.concatenate([dot_nn(mixed[...], piece[...]) for piece in pieces], axis=1)
    values = inputs[...].astype(f32) + halves(added, core)
    state[...] = values
    rows = (values * inverse_root(values) * gain[...]).astype(bf16)
    normed[...] = rows
    logits = dot_nn(rows, router[...])
    lane = lax.broadcasted_iota(jnp.int32, logits.shape, 1)
    logits = jnp.where(lane < experts, logits, -1e30)
    exps = jnp.exp(logits - jnp.max(logits, axis=1, keepdims=True))
    probs = exps / jnp.sum(exps, axis=1, keepdims=True)
    live = lax.broadcasted_iota(jnp.int32, (seq, 1), 0) < length
    named = [routes[:, k : k + 1] for k in range(2)]
    hits = [jnp.where((lane == name) & live, 1.0, 0.0) for name in named]
    before = lax.broadcasted_iota(jnp.int32, (seq, seq), 0) > lax.broadcasted_iota(
        jnp.int32, (seq, seq), 1
    )
    earlier = dot_nn(
        jnp.where(before, 1.0, 0.0).astype(bf16), (hits[0] + hits[1]).astype(bf16)
    )
    grad_out = jnp.where(live, cotangent[...], 0.0)
    kept = probs
    picks, grads = [], []
    for k in range(2):
        rank = jnp.sum(hits[k] * earlier, axis=1, keepdims=True)
        slot = ((named[k] ^ me) * capacity).astype(f32) + rank
        slot = jnp.where(live, slot, float(experts * capacity))
        gate = jnp.sum(hits[k] * probs, axis=1, keepdims=True)
        kept = jnp.where(lane == SLOT_LANE + k, slot, kept)
        kept = jnp.where(lane == GATE_LANE + k, gate, kept)
        picks.append(pick_table(slot, experts * capacity))
        grads.append((gate * grad_out).astype(bf16))
    aux[...] = kept
    sent = dot_tn(picks[0] + picks[1], rows).astype(bf16)
    sent_grads = (dot_tn(picks[0], grads[0]) + dot_tn(picks[1], grads[1])).astype(bf16)
    for d, out in enumerate(outs):
        out[:capacity, :] = sent[d * capacity : (d + 1) * capacity, :]
        out[capacity:, :] = sent_grads[d * capacity : (d + 1) * capacity, :]


def whole(shape):
    return pl.BlockSpec(shape, lambda i, _: (0,) * len(shape))


def part(m, shape):
    return pl.BlockSpec(shape, lambda i, _: (m,) + (0,) * (len(shape) - 1))


def proj_part(pieces):
    width = pieces[0].shape[0]
    return [pl.BlockSpec((width, width // 4), lambda i, _: (0, 3)) for _ in pieces]


def route(m, info, inputs, mixed, pieces, gain, router, routes, cotangent, experts, capacity):
    width = inputs.shape[1]
    seq = inputs.shape[0] // MB
    big = (seq, width)
    outs = [
        jax.ShapeDtypeStruct(big, f32),
        jax.ShapeDtypeStruct(big, bf16),
        jax.ShapeDtypeStruct((seq, 128), f32),
    ] + [jax.ShapeDtypeStruct((2 * capacity, width), bf16)] * experts
    return pl.pallas_call(
        functools.partial(route_kernel, capacity=capacity),
        grid_spec=pltpu.PrefetchScalarGridSpec(
            num_scalar_prefetch=1,
            grid=(1,),
            in_specs=[part(m, big), part(m, big)]
            + proj_part(pieces)
            + [whole(gain.shape), whole(router.shape), part(m, (seq, 2)), part(m, big)],
            out_specs=[whole(out.shape) for out in outs],
        ),
        out_shape=outs,
        cost_estimate=cost(8e-6),
        name="route",
    )(info, inputs, mixed, *pieces, gain, router, routes, cotangent)


def combine_kernel(info, aux, routes, state, cotangent, gain, router_rows, *refs, experts):
    pieces, blocks, refs = refs[:4], refs[4 : 4 + experts], refs[4 + experts :]
    layer_out, grad_state, grad_attn, grad_mixed, grad_logits, gain_grad = refs
    length, core = info[0], info[2]
    seq = state.shape[0]
    capacity = blocks[0].shape[0] // 2
    result = jnp.concatenate([block[:capacity, :] for block in blocks], axis=0)
    back = jnp.concatenate([block[capacity:, :] for block in blocks], axis=0)
    lane = lax.broadcasted_iota(jnp.int32, aux.shape, 1)
    probs = jnp.where(lane < experts, aux[...], 0.0)
    live = lax.broadcasted_iota(jnp.int32, (seq, 1), 0) < length
    grad_out = jnp.where(live, cotangent[...], 0.0)
    picks, mixture, grad_probs = [], 0.0, 0.0
    for k in range(2):
        picks.append(pick_table(aux[:, SLOT_LANE + k : SLOT_LANE + k + 1], experts * capacity))
        picked = dot_nn(picks[k], result)
        mixture = mixture + aux[:, GATE_LANE + k : GATE_LANE + k + 1] * picked
        grad_gate = jnp.sum(grad_out * picked, axis=1, keepdims=True)
        grad_probs = grad_probs + jnp.where(lane == routes[:, k : k + 1], grad_gate, 0.0)
    values = state[...]
    layer_out[...] = jnp.where(live, values + mixture, 0.0).astype(bf16)
    logits = probs * (grad_probs - jnp.sum(probs * grad_probs, axis=1, keepdims=True))
    grad_logits[...] = logits
    grad = dot_nn(picks[0] + picks[1], back)
    for e in range(experts):
        grad = grad + logits[:, e : e + 1] * router_rows[e : e + 1, :]
    grad_norm, gain_sum = norm_back(values, gain[...], grad)
    gain_grad[...] = gain_sum
    total = grad_out + grad_norm
    grad_state[...] = total
    turned = halves(total.astype(bf16), core)
    grad_attn[...] = turned
    quarter = turned.shape[1] // 4
    grad_mixed[...] = sum(
        dot_nt(turned[:, i * quarter : (i + 1) * quarter], pieces[i][...]) for i in range(4)
    ).astype(bf16)


def combine(m, info, aux, routes, state, cotangent, gain, router_rows, pieces, blocks):
    seq, width = state.shape
    big = (seq, width)
    outs = [
        jax.ShapeDtypeStruct(big, bf16),
        jax.ShapeDtypeStruct(big, f32),
        jax.ShapeDtypeStruct(big, bf16),
        jax.ShapeDtypeStruct(big, bf16),
        jax.ShapeDtypeStruct((seq, 128), f32),
        jax.ShapeDtypeStruct((1, width), f32),
    ]
    return pl.pallas_call(
        functools.partial(combine_kernel, experts=len(blocks)),
        grid_spec=pltpu.PrefetchScalarGridSpec(
            num_scalar_prefetch=1,
            grid=(1,),
            in_specs=[whole(aux.shape), part(m, (seq, 2)), whole(big), part(m, big)]
            + [whole(gain.shape), whole(router_rows.shape)]
            + proj_part(pieces)
            + [whole(blocks[0].shape)] * len(blocks),
            out_specs=[whole(out.shape) for out in outs],
        ),
        out_shape=outs,
        cost_estimate=cost(8e-6),
        name="combine",
    )(info, aux, routes, state, cotangent, gain, router_rows, *pieces, *blocks)


def enter_kernel(inputs, gain, *refs):
    pieces, (normed, packed) = refs[:4], refs[4:]
    values = inputs[...].astype(f32)
    rows = (values * inverse_root(values) * gain[...]).astype(bf16)
    normed[...] = rows
    span = pieces[0].shape[1] * 3 // 4
    for i, piece in enumerate(pieces):
        packed[:, i * span : (i + 1) * span] = dot_nn(rows, piece[:, :span]).astype(bf16)


def enter(inputs, gain, pieces):
    rows, width = inputs.shape
    return pl.pallas_call(
        enter_kernel,
        out_shape=[
            jax.ShapeDtypeStruct((rows, width), bf16),
            jax.ShapeDtypeStruct((rows, 3 * width), bf16),
        ],
        cost_estimate=cost(9e-6),
        compiler_params=pltpu.CompilerParams(vmem_limit_bytes=48 << 20),
        name="enter",
    )(inputs, gain, *pieces)


def leave_kernel(inputs, gain, *refs):
    pieces, packed, states, (out, gain_grad) = refs[:4], refs[4:6], refs[6:8], refs[8:]
    seq = packed[0].shape[0]
    span = pieces[0].shape[1] * 3 // 4
    total = 0.0
    for m in range(MB):
        r = pl.ds(m * seq, seq)
        grad = sum(
            dot_nt(packed[m][:, i * span : (i + 1) * span], piece[:, :span])
            for i, piece in enumerate(pieces)
        )
        grad_norm, gain_sum = norm_back(inputs[r, :].astype(f32), gain[...], grad)
        out[r, :] = states[m][...] + grad_norm
        total = total + gain_sum
    gain_grad[...] = total


def leave(inputs, gain, pieces, packed, states):
    return pl.pallas_call(
        leave_kernel,
        out_shape=[
            jax.ShapeDtypeStruct(inputs.shape, f32),
            jax.ShapeDtypeStruct(gain.shape, f32),
        ],
        cost_estimate=cost(12e-6),
        compiler_params=pltpu.CompilerParams(vmem_limit_bytes=48 << 20),
        name="leave",
    )(inputs, gain, *pieces, *packed, *states)


def expert_kernel(*refs, first, last, experts):
    blocks, refs = refs[: MB * experts], refs[MB * experts :]
    (gate_mat, up_mat, shrink_mat), refs = refs[:3], refs[3:]
    sums_in, turned = (), ()
    if not first:
        sums_in, turned, refs = refs[: 2 * MB], refs[2 * MB : 3 * MB], refs[3 * MB + 1 :]
    expand_grad, shrink_grad, *outs, hidden, pre = refs
    if last:
        outs, sums = outs[: MB * experts], outs[MB * experts :]
    else:
        sums = outs[: 2 * MB]
    if first:
        turned, outs = outs[2 * MB : 3 * MB], outs[: 2 * MB] + outs[3 * MB :]
    cap = blocks[0].shape[0] // 2
    size = experts * cap
    j = pl.program_id(0)

    @pl.when(j == 0)
    def _():
        for k, total in enumerate(sums):
            total[...] = jnp.zeros_like(total) if first else sums_in[k][...]
        if first:
            for m in range(MB):
                for d in range(experts):
                    turned[m][:, d * cap : (d + 1) * cap] = blocks[m * experts + d][:cap, :].T

    grads_in = []
    for m in range(MB):
        r = pl.ds(m * size, size)
        mine = blocks[m * experts : (m + 1) * experts]
        rows_in = jnp.concatenate([block[:cap, :] for block in mine], axis=0)
        grads_in.append(jnp.concatenate([block[cap:, :] for block in mine], axis=0))
        gate = dot_nn(rows_in, gate_mat[...])
        up = dot_nn(rows_in, up_mat[...])
        grad = dot_nt(grads_in[m], shrink_mat[...])
        bent = jnp.tanh(tanh_scale * (gate + tanh_cubic * (gate * gate * gate)))
        half = 0.5 * (1.0 + bent)
        gelu = gate * half
        slope = half + gate * (0.5 * (1.0 - bent * bent)) * (
            tanh_scale * (1.0 + 3.0 * tanh_cubic * gate * gate)
        )
        act = (gelu * up).astype(bf16)
        pre_gate = (slope * up * grad).astype(bf16)
        pre_up = (gelu * grad).astype(bf16)
        hidden[r, :] = act
        pre[r, :TILE] = pre_gate
        pre[r, TILE:] = pre_up
        sums[m][...] += dot_nn(act, shrink_mat[...])
        sums[MB + m][...] += dot_nt(pre_gate, gate_mat[...]) + dot_nt(pre_up, up_mat[...])
    lower, upper = pl.ds(0, size), pl.ds(size, size)
    expand_grad[...] = (
        dot_nn(turned[0][...], pre[lower, :]) + dot_nn(turned[1][...], pre[upper, :])
    ).astype(bf16)
    shrink_grad[...] = (
        dot_tn(hidden[lower, :], grads_in[0]) + dot_tn(hidden[upper, :], grads_in[1])
    ).astype(bf16)
    if last:

        @pl.when(j == pl.num_programs(0) - 1)
        def _():
            for m in range(MB):
                for d in range(experts):
                    out, r = outs[m * experts + d], pl.ds(d * cap, cap)
                    out[:cap, :] = sums[m][r, :].astype(bf16)
                    out[cap:, :] = sums[MB + m][r, :].astype(bf16)


def expert_call(blocks, mat, shrink_mat, kept, place, tiles, last):
    experts = len(blocks[0])
    pair, width = blocks[0][0].shape
    size = experts * pair // 2
    first = kept is None

    def full(shape, **options):
        return pl.BlockSpec(shape, lambda j: (0, 0), **options)

    def once(shape):
        return full(shape, pipeline_mode=pl.Buffered(1))

    shrink_tile = pl.BlockSpec((TILE, width), lambda j: (place + j, 0))
    if last:
        outs = [jax.ShapeDtypeStruct((pair, width), bf16)] * (MB * experts)
    else:
        outs = [jax.ShapeDtypeStruct((size, width), f32)] * (2 * MB)
        outs += [jax.ShapeDtypeStruct((width, size), bf16)] * MB
    return pl.pallas_call(
        functools.partial(expert_kernel, first=first, last=last, experts=experts),
        grid=(tiles,),
        in_specs=[once((pair, width))] * (MB * experts)
        + [
            pl.BlockSpec((width, TILE), lambda j: (0, j)),
            pl.BlockSpec((width, TILE), lambda j: (0, tiles + j)),
            shrink_tile,
        ]
        + (
            []
            if first
            else [once((size, width))] * (2 * MB)
            + [once((width, size))] * MB
            + [pl.BlockSpec(memory_space=pl.ANY)]
        ),
        out_specs=[pl.BlockSpec((width, 2 * TILE), lambda j: (0, j)), shrink_tile]
        + [full(out.shape) for out in outs],
        out_shape=[
            jax.ShapeDtypeStruct((width, 2 * tiles * TILE), bf16),
            jax.ShapeDtypeStruct((FF, width), bf16),
        ]
        + outs,
        scratch_shapes=([pltpu.VMEM((size, width), f32)] * (2 * MB) if last else [])
        + [pltpu.VMEM((MB * size, TILE), bf16), pltpu.VMEM((MB * size, 2 * TILE), bf16)],
        input_output_aliases={} if first else {MB * experts + 3 * MB + 3: 1},
        compiler_params=pltpu.CompilerParams(
            dimension_semantics=("arbitrary",), vmem_limit_bytes=58 << 20
        ),
        cost_estimate=cost(8.5e-6 * tiles),
        name="expert",
    )(
        *(block for side in blocks for block in side),
        mat,
        mat,
        shrink_mat,
        *(() if first else (*kept[1:], kept[0])),
    )


def adam_kernel(scales, master, first_old, second, gradient, *refs):
    master_out, first_out, second_out = refs[-3:]
    grad = gradient[...].astype(f32)
    first_new = beta_first * first_old[...] + (1.0 - beta_first) * grad
    second_new = beta_second * second[...] + (1.0 - beta_second) * grad * grad
    step = (first_new / scales[0]) / (jnp.sqrt(second_new / scales[1]) + adam_floor)
    master_out[...] = master[...] - scales[2] * (step + decay_rate * master[...])
    first_out[...] = first_new
    second_out[...] = second_new


def adam_expand(scales, states, gradient, kept, place, tiles):
    rows = states[0].shape[0]
    window = pl.BlockSpec((rows, TILE), lambda h, j, _: (0, h * (FF // TILE) + place + j))
    first = kept is None
    return pl.pallas_call(
        adam_kernel,
        grid_spec=pltpu.PrefetchScalarGridSpec(
            num_scalar_prefetch=1,
            grid=(2, tiles),
            in_specs=[window] * 3
            + [pl.BlockSpec((rows, TILE), lambda h, j, _: (0, 2 * j + h))]
            + ([] if first else [pl.BlockSpec(memory_space=pl.ANY)] * 3),
            out_specs=[window] * 3,
        ),
        out_shape=[jax.ShapeDtypeStruct(states[0].shape, f32)] * 3,
        input_output_aliases={} if first else {5: 0, 6: 1, 7: 2},
        cost_estimate=cost(1.5e-6 * tiles),
        name="adam",
    )(scales, *states, gradient, *(() if first else kept))


def inverse_root(values):
    return lax.rsqrt(jnp.mean(values * values, axis=-1, keepdims=True) + epsilon_norm)


def norm_back(values, gain, grad):
    root = inverse_root(values)
    scaled = grad * gain
    inner = jnp.mean(scaled * values, axis=-1, keepdims=True)
    grad_values = root * scaled - values * (root * root * root * inner)
    return grad_values, jnp.sum(grad * values * root, axis=0, keepdims=True)


def adam_update(master, first_old, second, gradient, counter, learn_rate):
    first_new = beta_first * first_old + (1.0 - beta_first) * gradient
    second_new = beta_second * second + (1.0 - beta_second) * gradient * gradient
    first_hat = first_new / (1.0 - beta_first**counter)
    second_hat = second_new / (1.0 - beta_second**counter)
    master_new = master - learn_rate * (
        first_hat / (jnp.sqrt(second_hat) + adam_floor) + decay_rate * master
    )
    return (master_new, first_new, second_new)


def after(values, *earlier):
    return lax.optimization_barrier((values,) + earlier)[0]


def body(
    tokens,
    lengths,
    routes,
    cotangent,
    step_count,
    qkv_master,
    qkv_first,
    qkv_second,
    proj_master,
    proj_first,
    proj_second,
    table_master,
    table_first,
    table_second,
    gains_master,
    gains_first,
    gains_second,
    router_master,
    router_first,
    router_second,
    expand_master,
    expand_first,
    expand_second,
    shrink_master,
    shrink_first,
    shrink_second,
):
    experts = lax.axis_size("expert")
    devices = lax.axis_size("dp")
    length, width = tokens.shape[2], tokens.shape[3]
    heads = width // HEAD
    capacity = 5 * length // (2 * experts)
    slots = experts * capacity
    rows = MB * length
    ring = Ring()
    lower = lax.axis_index("expert") % 2 == 0

    def mine(values):
        half = values.shape[-1] // 2
        return jnp.where(lower, values[..., :half], values[..., half:])

    def joined(own, others):
        return [jnp.where(lower, own, others), jnp.where(lower, others, own)]

    small = jnp.concatenate(
        [table_master.reshape(-1), gains_master.reshape(-1), router_master.reshape(-1)]
    ).astype(bf16)
    small, small_marks = gather_small(small)
    cut_one = table_master.size
    cut_two = cut_one + gains_master.size
    table_vals = small[:, :cut_one].reshape(BUCKETS, heads).astype(f32)
    gains = small[:, cut_one:cut_two].reshape(devices, 2, width // devices)
    gains = gains.transpose(1, 0, 2).reshape(2, width).astype(f32)
    router_mat = small[:, cut_two:].reshape(width, experts)

    half, quarter = width // 2, width // 4
    query_half, key_half, value_half = (
        mine(qkv_master[:, i * width : (i + 1) * width]) for i in range(3)
    )
    proj_half = mine(proj_master)
    marks = [query_half]
    dense_own = ring.gather(
        jnp.concatenate(
            [query_half, value_half[:, :quarter], proj_half[:, :quarter]], axis=1
        ).astype(bf16),
        jnp.concatenate(
            [key_half, value_half[:, quarter:], proj_half[:, quarter:]], axis=1
        ).astype(bf16),
        marks,
        (None, *small_marks),
    )
    dense_own = [piece.reshape(width, width) for piece in dense_own]
    dense_other = [swap(piece, "expert", 1) for piece in dense_own]
    dense = dense_own + dense_other

    expand_local = expand_master[0]
    mats = []
    start = 0
    for count in PARTS:
        stop = start + count * TILE
        local = jnp.concatenate(
            [expand_local[:, start:stop], expand_local[:, FF + start : FF + stop]], axis=1
        )
        local = local.astype(bf16)
        if start == 0:
            local = after(local, marks[min(GATE, len(marks) - 1)])
        mats.append(lax.all_gather(local, "dp", axis=0, tiled=True))
        start = stop

    distance = (-np.arange(length)) % length
    onehot = jnp.asarray(
        (distance_buckets(length)[distance][:, None] == np.arange(BUCKETS)).astype(np.float32)
    )
    bias_rows = jnp.einsum("cb,bh->hc", onehot, table_vals, precision=HIGHEST)
    bias_rows = jnp.pad(
        bias_rows.reshape(heads // 2, 2, length), ((0, 0), (0, 6), (0, 0))
    )
    length_now = lengths[:, 0]
    me = lax.axis_index("expert")
    core = lax.rem(me, 2)
    info = jnp.concatenate([length_now, core[None]])
    inputs = tokens.reshape(rows, width)
    normed_one, packed = enter(inputs, gains[0:1], dense)
    mixed = attend(info, packed, bias_rows, length)

    route_rows = routes.reshape(rows, 2)
    gradient = cotangent.reshape(rows, width)
    router_lanes = jnp.pad(router_mat, ((0, 0), (0, 128 - experts)))

    def exchange(blocks):
        return [blocks[0]] + [swap(blocks[d], "expert", d) for d in range(1, experts)]

    infos = [jnp.stack([length_now[m], me, core]) for m in range(MB)]
    state, normed_two, aux, expert_rows = [], [], [], []
    for m in range(MB):
        state_now, normed_now, aux_now, *sent = route(
            m,
            infos[m],
            inputs,
            mixed,
            dense,
            gains[1:2],
            router_lanes,
            route_rows,
            gradient,
            experts,
            capacity,
        )
        state.append(state_now)
        normed_two.append(normed_now)
        aux.append(aux_now)
        expert_rows.append(exchange(sent))

    cut = shrink_master.shape[1] // 2
    shrink_local = shrink_master[0].astype(bf16)
    marks_shrink = [shrink_local]
    shrink_mat = ring.gather(
        shrink_local[:cut],
        shrink_local[cut:],
        marks_shrink,
        (marks[-1], packed, mixed, state[1]),
    )
    shrink_mat = jnp.concatenate([piece[:, None] for piece in shrink_mat], axis=1)
    shrink_mat = shrink_mat.reshape(FF, width)
    kept = None
    place = 0
    block = width // devices
    expand_grads = []
    for p, tiles in enumerate(PARTS):
        last = p == len(PARTS) - 1
        share, *kept = expert_call(
            expert_rows, mats[p], shrink_mat, kept, place, tiles, last
        )
        expand_grads.append(lax.psum_scatter(share, "dp", scatter_dimension=0, tiled=True))
        place += tiles
    shrink_grad, *sums = kept
    shrink_grad = shrink_grad.reshape(devices, 2, cut, width)

    router_rows = router_mat.astype(f32).T
    returned = [exchange(sums[m * experts : (m + 1) * experts]) for m in range(MB)]
    counter = step_count[0].astype(f32)
    scales = jnp.stack([1.0 - beta_first**counter, 1.0 - beta_second**counter, rate_expand])
    expand_states = (expand_master[0], expand_first[0], expand_second[0])
    expand_new = adam_expand(scales, expand_states, expand_grads[0], None, 0, PARTS[0])
    shrink_gates = [None, None, None]
    combined, backs = [], []
    for m in range(MB):
        blocks = returned[m]
        if m > 0:
            blocks = lax.optimization_barrier((*blocks, backs[-1][0]))[:-1]
        combined.append(
            combine(
                m,
                infos[m],
                aux[m],
                route_rows,
                state[m],
                gradient,
                gains[1:2],
                router_rows,
                dense,
                blocks,
            )
        )
        grad_mixed = combined[m][3]
        if m == MB - 1:
            grad_mixed = after(grad_mixed, expand_new[0])
        backs.append(attend_back(m, info, packed, bias_rows, grad_mixed))
        shrink_gates += [combined[m][1], backs[m][0]]
    layer_out, grad_state, grad_attn, _, grad_logits, gain_sums = (
        jnp.stack(values) for values in zip(*combined)
    )
    shrink_grad = jnp.concatenate(
        ring.scatter(shrink_grad[:, 0], shrink_grad[:, 1], shrink_gates), axis=0
    )
    gains_two_grad = jnp.sum(gain_sums, axis=(0, 1))
    router_grad = jnp.einsum(
        "mtd,mte->de",
        jnp.stack(normed_two).astype(f32),
        grad_logits[:, :, :experts],
        precision=HIGHEST,
    )
    grad_attn = grad_attn.reshape(rows, width)
    grad_packed, sums = (jnp.concatenate(values) for values in zip(*backs))

    def shared(left, right):
        middle = right.shape[1] // 2
        sent = swap(dot_tn(left, right[:, middle:]).astype(bf16), "expert", 1)
        share = dot_tn(left, right[:, :middle]) + sent.astype(f32)
        share = share.astype(bf16).reshape(devices, block, middle)
        return share[..., : middle // 2], share[..., middle // 2 :]

    proj_share = shared(mixed, grad_attn)
    qkv_share = shared(normed_one, grad_packed)
    table_grad = jnp.einsum(
        "hc,cb->bh",
        jnp.sum(sums.reshape(MB, heads // 2, 8, length), axis=0)[:, :2].reshape(heads, length),
        onehot,
        precision=HIGHEST,
    )
    token_grad, gains_one_grad = leave(
        inputs,
        gains[0:1],
        dense,
        [back[0] for back in backs],
        [values[1] for values in combined],
    )

    flat = jnp.concatenate(
        [
            table_grad.reshape(devices, -1),
            jnp.stack([gains_one_grad[0], gains_two_grad])
            .reshape(2, devices, block)
            .transpose(1, 0, 2)
            .reshape(devices, -1),
            router_grad.reshape(devices, -1),
        ],
        axis=1,
    )
    flat, small_marks = sum_small(flat)
    flat = flat[ring.me]
    table_grad = flat[:cut_one].reshape(table_master.shape)
    gains_grad = flat[cut_one:cut_two].reshape(gains_master.shape)
    router_grad = flat[cut_two:].reshape(router_master.shape)

    done = ring.scatter(
        *(
            jnp.concatenate([qkv_part, proj_part], axis=-1)
            for qkv_part, proj_part in zip(qkv_share, proj_share)
        ),
        (None, token_grad, *small_marks),
    )
    done = jnp.concatenate(done, axis=1)
    bit = 2
    while bit < experts:
        done = done.astype(bf16)
        done = done.astype(f32) + swap(done, "expert", bit).astype(f32)
        bit *= 2
    others = swap(done, "expert", 1)

    def columns(*spans):
        own, other = (
            jnp.concatenate([side[:, start:stop] for start, stop in spans], axis=1)
            for side in (done, others)
        )
        return joined(own, other)

    qkv_grad = jnp.concatenate(
        columns((0, half))
        + columns((width, width + half))
        + columns((half, half + quarter), (width + half, width + half + quarter)),
        axis=1,
    )
    proj_grad = jnp.concatenate(
        columns((half + quarter, width), (width + half + quarter, 2 * width)), axis=1
    )
    states = (
        (qkv_master, qkv_first, qkv_second, qkv_grad),
        (proj_master, proj_first, proj_second, proj_grad),
        (table_master, table_first, table_second, table_grad),
        (gains_master, gains_first, gains_second, gains_grad),
        (router_master, router_first, router_second, router_grad),
        (shrink_master, shrink_first, shrink_second, shrink_grad[None]),
    )
    fresh = []
    for (master, first_old, second, gradient), learn_rate in zip(states, rate_table):
        fresh.append(adam_update(master, first_old, second, gradient, counter, learn_rate))
    kept = adam_expand(scales, expand_states, expand_grads[1], expand_new, PARTS[0], PARTS[1])
    fresh.insert(5, tuple(value[None] for value in kept))
    fresh = [value for group in fresh for value in group]
    return (
        layer_out.reshape(MB, 1, length, width),
        token_grad.reshape(MB, 1, length, width),
        *fresh,
    )


def solution(mesh):
    sequences = P(None, ("dp", "expert"), None, None)
    over_rows = P("dp", None)
    over_columns = P(None, "dp")
    by_expert = P("expert", "dp", None)
    weights = (
        (over_rows,) * 9 + (over_columns,) * 3 + (over_rows,) * 3 + (by_expert,) * 6
    )
    return jax.shard_map(
        body,
        mesh=mesh,
        in_specs=(sequences, P(None, ("dp", "expert")), sequences, sequences, P()) + weights,
        out_specs=(sequences, sequences) + weights,
        check_vma=False,
    )
```

```python
import functools

import jax
import jax.numpy as jnp
import numpy as np
from jax import lax
from jax.experimental import pallas as pl
from jax.experimental.pallas import tpu as pltpu
from jax.sharding import PartitionSpec as P

HEAD = 64
FF = 2816
BUCKETS = 32
MB = 2
TILE = 256
PARTS = (7, 4)
RING_LIMIT = 8
GATE = 4

HIGHEST = lax.Precision.HIGHEST
f32 = jnp.float32
bf16 = jnp.bfloat16
epsilon_norm = 1e-06
beta_first = 0.9
beta_second = 0.95
adam_floor = 1e-08
decay_rate = 0.1
rate_table = (0.03, 0.1, 0.3, 0.1, 0.03, 0.03)
rate_expand = np.float32(0.03)
tanh_scale = 0.7978845608028654
tanh_cubic = 0.044715


def dot_nn(a, b):
    return lax.dot_general(a, b, (((1,), (0,)), ((), ())), preferred_element_type=f32)


def dot_nt(a, b):
    return lax.dot_general(a, b, (((1,), (1,)), ((), ())), preferred_element_type=f32)


def dot_tn(a, b):
    return lax.dot_general(a, b, (((0,), (0,)), ((), ())), preferred_element_type=f32)


def cost(seconds):
    return pl.CostEstimate(
        flops=int(seconds * 1e15), transcendentals=0, bytes_accessed=int(seconds * 3e12)
    )


def distance_buckets(length):
    spread = np.arange(length)
    exact_span = BUCKETS // 2
    scaled = np.log(np.maximum(spread, 1) / exact_span) / np.log(128.0 / exact_span)
    farther = np.minimum(
        exact_span + (scaled * (BUCKETS - exact_span)).astype(np.int64), BUCKETS - 1
    )
    return np.where(spread < exact_span, spread, farther).astype(np.int32)


def ring_order(count):
    if count % 2:
        return list(range(count))
    return list(range(0, count, 2)) + list(range(count - 1, 0, -2))


class Ring:
    def __init__(self):
        self.count = n = lax.axis_size("dp")
        self.order = ring_order(n)
        self.me = me = lax.axis_index("dp")
        if n % 2:
            place = me
        else:
            place = jnp.where(me % 2 == 0, me // 2, n - (me + 1) // 2)
        self.others = []
        for offset in range(1, n if n <= RING_LIMIT else 1):
            other = lax.rem(place + offset, n)
            if n % 2 == 0:
                other = jnp.where(other < n // 2, 2 * other, 2 * n - 1 - 2 * other)
            self.others.append(other)

    def member(self, offset):
        offset %= self.count
        return self.others[offset - 1] if offset else self.me

    def step(self, values, way):
        n, order = self.count, self.order
        pairs = [(order[i], order[(i + way) % n]) for i in range(n)]
        return lax.ppermute(values, "dp", pairs)


class Moving:
    def __init__(self, ring, blocks):
        self.ring = ring
        self.ahead, self.behind = list(blocks), list(blocks)
        self.hops = 0
        self.arrived = [[(0, 0, block)] for block in blocks]

    def advance(self, gate=None):
        self.hops += 1
        hop, count = self.hops, len(self.ahead)
        ahead, behind = self.ahead, self.behind
        cuts = [0] * count
        if hop == self.ring.count // 2:
            cuts = [block.shape[0] // 2 for block in ahead]
            ahead = [block[:cut] for block, cut in zip(ahead, cuts)]
            behind = [block[cut:] for block, cut in zip(behind, cuts)]
        blocks = (*ahead, *behind)
        if gate is not None:
            blocks = lax.optimization_barrier((*blocks, gate))[:-1]
        blocks = lax.optimization_barrier(
            tuple(self.ring.step(block, 1 if k < count else -1) for k, block in enumerate(blocks))
        )
        self.ahead, self.behind = blocks[:count], blocks[count:]
        for k in range(count):
            self.arrived[k].append((-hop, 0, self.ahead[k]))
            self.arrived[k].append((hop, cuts[k], self.behind[k]))
        return blocks[0]

    def placed(self, k):
        block = self.arrived[k][0][2]
        whole = jnp.zeros((self.ring.count,) + block.shape, block.dtype)
        for offset, row, block in self.arrived[k]:
            index = (self.ring.member(offset), row) + (0,) * (block.ndim - 1)
            whole = lax.dynamic_update_slice(
                whole, block[None], index, allow_negative_indices=False
            )
        return whole


class Scattering:
    def __init__(self, ring, top, bottom):
        self.ring, self.groups, self.hops = ring, (top, bottom), 0
        self.alone = ring.count > RING_LIMIT
        self.blocks = [top[0][0]]
        if not self.alone:
            self.add(None)

    def add(self, received):
        self.blocks = add_shares(received, self.groups, self.hops, self.ring)

    def start(self, *gates):
        if not self.alone:
            blocks = after(list(self.blocks), *gates)
            self.received = [self.ring.step(block, way) for block, way in zip(blocks, (1, -1))]

    def settle(self, *gates):
        if self.alone:
            return gates[0]
        self.hops += 1
        self.add(after(self.received, *gates))
        return self.blocks[0]

    def finish(self):
        if not self.alone:
            return self.blocks
        return [
            jnp.concatenate(
                [
                    lax.psum_scatter(
                        shares[:, r * i : r * (i + 1), c * j : c * (j + 1)],
                        "dp",
                        scatter_dimension=0,
                    ).astype(f32)
                    for shares, r, c, i, j in group
                ],
                axis=1,
            )
            for group in self.groups
        ]


def add_kernel(members, *refs, counts, rows, hop, last):
    received, refs = (refs[:2], refs[2:]) if hop else ((), refs)
    ways = 1 if last else 2
    for way in range(ways):
        start_row = 0
        for g in range(2):
            if hop == 0 and g != way:
                continue
            windows, refs = refs[: counts[g]], refs[counts[g] :]
            start = 0
            for window in windows:
                span = pl.ds(start, window.shape[-1])
                value = window[0].astype(f32)
                for side in (0, 1) if last else (way,):
                    if hop > 1:
                        value = value + received[side][pl.ds(start_row, rows[g]), span].astype(f32)
                    elif hop == 1 and side == g:
                        value = value + received[side][:, span].astype(f32)
                if last:
                    out, r = refs_out(refs, 2)[g], pl.ds(0, rows[g])
                elif hop == 0:
                    out, r = refs_out(refs, 2)[way], pl.ds(0, rows[g])
                else:
                    out, r = refs_out(refs, 2)[way], pl.ds(start_row, rows[g])
                out[r, span] = value.astype(out.dtype)
                start += window.shape[-1]
            start_row += rows[g]


def refs_out(refs, count):
    return refs[len(refs) - count :]


def add_shares(received, groups, hop, ring):
    last = hop == ring.count // 2
    rows = [group[0][1] for group in groups]
    widths = [sum(window[2] for window in group) for group in groups]
    distance = ring.count // 2 - hop
    members = [ring.member(distance), ring.member(-distance)]
    in_specs, operands = [], []
    for block in received or ():
        in_specs.append(pl.BlockSpec(block.shape, lambda i, _: (0, 0)))
        operands.append(block)
    for way in range(1 if last else 2):
        for g, group in enumerate(groups):
            if hop == 0 and g != way:
                continue
            for shares, r, c, row, column in group:
                in_specs.append(
                    pl.BlockSpec(
                        (1, r, c),
                        lambda i, members, way=way, row=row, column=column: (
                            members[way],
                            row,
                            column,
                        ),
                    )
                )
                operands.append(shares)
    if last:
        outs = [jax.ShapeDtypeStruct(shape, f32) for shape in zip(rows, widths)]
    elif hop == 0:
        outs = [jax.ShapeDtypeStruct(shape, bf16) for shape in zip(rows, widths)]
    else:
        outs = [jax.ShapeDtypeStruct((sum(rows), widths[0]), bf16)] * 2
    return pl.pallas_call(
        functools.partial(
            add_kernel, counts=[len(group) for group in groups], rows=rows, hop=hop, last=last
        ),
        grid_spec=pltpu.PrefetchScalarGridSpec(
            num_scalar_prefetch=1,
            grid=(1,),
            in_specs=in_specs,
            out_specs=[pl.BlockSpec(out.shape, lambda i, _: (0, 0)) for out in outs],
        ),
        out_shape=outs,
        cost_estimate=cost(3e-6),
        name="add_shares",
    )(jnp.stack(members), *operands)


def swap(values, axis, bit):
    count = lax.axis_size(axis)
    return lax.ppermute(values, axis, [(i, i ^ bit) for i in range(count)])


def gather_small(values):
    count = lax.axis_size("dp")
    rows = values[None]
    bit = 1
    marks = []
    while bit < count:
        rows = jnp.concatenate([rows, swap(rows, "dp", bit)], axis=0)
        marks.append(rows)
        bit *= 2
    return rows[jnp.arange(count) ^ lax.axis_index("dp")], marks


def sum_small(values):
    marks = []
    for axis in ("expert", "dp"):
        bit = 1
        while bit < lax.axis_size(axis):
            values = values + swap(values, axis, bit)
            marks.append(values)
            bit *= 2
    return values, marks


def head_probs(query, key, bias_row, length):
    seq = query.shape[0]
    scores = dot_nt(query, key) * HEAD ** (-0.5)
    bias = pltpu.roll(
        jnp.broadcast_to(bias_row, (seq, seq)), 0, 1, stride=1, stride_axis=0
    )
    row = lax.broadcasted_iota(jnp.int32, (seq, seq), 0)
    column = lax.broadcasted_iota(jnp.int32, (seq, seq), 1)
    scores = jnp.where((column <= row) & (column < length), scores + bias, -1e30)
    exps = jnp.exp(scores - jnp.max(scores, axis=1, keepdims=True))
    return exps / jnp.sum(exps, axis=1, keepdims=True)


def attend_kernel(info, query, key, value, bias_rows, mixed):
    length = info[0]
    for half in range(2):
        c = pl.ds(HEAD * half, HEAD)
        probs = head_probs(query[:, c], key[:, c], bias_rows[0, half : half + 1, :], length)
        mixed[:, c] = dot_nn(probs.astype(bf16), value[:, c]).astype(bf16)


def diagonal_sums(values):
    seq = values.shape[0]
    eight = values[0:8, :]
    for t in range(1, seq // 8):
        eight = eight + pltpu.roll(values[8 * t : 8 * t + 8, :], seq - 8 * t, 1)
    total = eight[0:1, :]
    for t in range(1, 8):
        total = total + pltpu.roll(eight, seq - t, 1)[t : t + 1, :]
    return total


def attend_back_kernel(info, query, key, value, bias_rows, grad, *refs):
    grad_packed, sums = refs[-2:]
    seq = query.shape[0]
    h = pl.program_id(0)
    length, core = info[0], info[1]
    places = packed_places(h, pl.num_programs(0), core)
    offsets = [pl.multiple_of(place * 2 * HEAD, 2 * HEAD) for place in places]
    parts = [[], [], []]
    for half in range(2):
        c = pl.ds(HEAD * half, HEAD)
        q, k, v, g = query[:, c], key[:, c], value[:, c], grad[:, c]
        probs = head_probs(q, k, bias_rows[0, half : half + 1, :], length)
        grad_probs = dot_nt(g, v)
        scores = probs * (grad_probs - jnp.sum(probs * grad_probs, axis=1, keepdims=True))
        rounded = scores.astype(bf16)
        parts[0].append((dot_nn(rounded, k) * HEAD ** (-0.5)).astype(bf16))
        parts[1].append((dot_tn(rounded, q) * HEAD ** (-0.5)).astype(bf16))
        parts[2].append(dot_tn(probs.astype(bf16), g).astype(bf16))
        sums[0, half : half + 1, :] = diagonal_sums(scores)
    sums[0, 2:8, :] = jnp.zeros((6, seq), f32)
    for offset, part in zip(offsets, parts):
        grad_packed[:, pl.ds(offset, 2 * HEAD)] = jnp.concatenate(part, axis=1)


def packed_places(h, pairs, core):
    half = pairs // 2
    first = jnp.where(h // half == core, 0, 3 * half) + lax.rem(h, half)
    return first, first + half, first + 2 * half


def pair_windows(m, seq, pairs):
    return [
        pl.BlockSpec(
            (seq, 2 * HEAD),
            lambda h, info, part=part: (m, packed_places(h, pairs, info[1])[part]),
        )
        for part in range(3)
    ]


def attend(m, info, packed, bias_rows, seq):
    width = packed.shape[1] // 3
    pairs = width // (2 * HEAD)
    return pl.pallas_call(
        attend_kernel,
        grid_spec=pltpu.PrefetchScalarGridSpec(
            num_scalar_prefetch=1,
            grid=(pairs,),
            in_specs=pair_windows(m, seq, pairs)
            + [pl.BlockSpec((1, 8, seq), lambda h, _: (h, 0, 0))],
            out_specs=pl.BlockSpec((seq, 2 * HEAD), lambda h, _: (0, h)),
        ),
        out_shape=jax.ShapeDtypeStruct((seq, width), bf16),
        cost_estimate=cost(10e-6),
        name="attend",
    )(info, packed, packed, packed, bias_rows)


def attend_back(m, info, packed, bias_rows, grad, kept):
    seq, width = grad.shape
    pairs = width // (2 * HEAD)

    return pl.pallas_call(
        attend_back_kernel,
        grid_spec=pltpu.PrefetchScalarGridSpec(
            num_scalar_prefetch=1,
            grid=(pairs,),
            in_specs=pair_windows(m, seq, pairs)
            + [
                pl.BlockSpec((1, 8, seq), lambda h, _: (h, 0, 0)),
                pl.BlockSpec((seq, 2 * HEAD), lambda h, _: (0, h)),
            ]
            + [pl.BlockSpec(memory_space=pl.ANY) for _ in kept],
            out_specs=[
                pl.BlockSpec((seq, 3 * width), lambda h, _: (m, 0)),
                pl.BlockSpec((1, 8, seq), lambda h, _: (h, 0, 0)),
            ],
        ),
        out_shape=[
            jax.ShapeDtypeStruct(packed.shape, bf16),
            jax.ShapeDtypeStruct((pairs, 8, seq), f32),
        ],
        input_output_aliases={6: 0} if kept else {},
        cost_estimate=cost(16e-6),
        name="attend_back",
    )(info, packed, packed, packed, bias_rows, grad, *kept)


SLOT_LANE, GATE_LANE = 16, 18


def halves(values, core):
    half = values.shape[1] // 2
    turned = jnp.concatenate([values[:, half:], values[:, :half]], axis=1)
    return jnp.where(core == 0, values, turned)


def pick_table(slot, slots):
    lane = lax.broadcasted_iota(jnp.int32, (slot.shape[0], slots), 1).astype(f32)
    return jnp.where(lane == slot, 1.0, 0.0).astype(bf16)


def route_kernel(info, inputs, mixed, *refs, capacity):
    pieces, refs = refs[:2], refs[2:]
    gain, router, routes, cotangent, state, normed, aux, out = refs
    length, core = info[0], info[1]
    seq = inputs.shape[0]
    experts = out.shape[0] // (2 * capacity)
    added = jnp.concatenate([dot_nn(mixed[...], piece[...]) for piece in pieces], axis=1)
    values = inputs[...].astype(f32) + halves(added, core)
    state[...] = values
    rows = (values * inverse_root(values) * gain[...]).astype(bf16)
    normed[...] = rows
    logits = dot_nn(rows, router[...])
    lane = lax.broadcasted_iota(jnp.int32, logits.shape, 1)
    logits = jnp.where(lane < experts, logits, -1e30)
    exps = jnp.exp(logits - jnp.max(logits, axis=1, keepdims=True))
    probs = exps / jnp.sum(exps, axis=1, keepdims=True)
    live = lax.broadcasted_iota(jnp.int32, (seq, 1), 0) < length
    named = [routes[:, k : k + 1] for k in range(2)]
    hits = [jnp.where((lane == name) & live, 1.0, 0.0) for name in named]
    before = lax.broadcasted_iota(jnp.int32, (seq, seq), 0) > lax.broadcasted_iota(
        jnp.int32, (seq, seq), 1
    )
    earlier = dot_nn(
        jnp.where(before, 1.0, 0.0).astype(bf16), (hits[0] + hits[1]).astype(bf16)
    )
    grad_out = jnp.where(live, cotangent[...], 0.0)
    kept = probs
    picks, grads = [], []
    for k in range(2):
        rank = jnp.sum(hits[k] * earlier, axis=1, keepdims=True)
        slot = (named[k] * capacity).astype(f32) + rank
        slot = jnp.where(live, slot, float(experts * capacity))
        gate = jnp.sum(hits[k] * probs, axis=1, keepdims=True)
        kept = jnp.where(lane == SLOT_LANE + k, slot, kept)
        kept = jnp.where(lane == GATE_LANE + k, gate, kept)
        picks.append(pick_table(slot, experts * capacity))
        grads.append((gate * grad_out).astype(bf16))
    aux[...] = kept
    sent = dot_tn(picks[0] + picks[1], rows).astype(bf16)
    sent_grads = (dot_tn(picks[0], grads[0]) + dot_tn(picks[1], grads[1])).astype(bf16)
    for e in range(experts):
        r = slice(e * capacity, (e + 1) * capacity)
        out[pl.ds(2 * e * capacity, capacity), :] = sent[r, :]
        out[pl.ds((2 * e + 1) * capacity, capacity), :] = sent_grads[r, :]


def whole(shape):
    return pl.BlockSpec(shape, lambda i, _: (0,) * len(shape))


def part(m, shape):
    return pl.BlockSpec(shape, lambda i, _: (m,) + (0,) * (len(shape) - 1))


def proj_part(pieces):
    width = pieces[0].shape[0]
    return [pl.BlockSpec((width, width // 2), lambda i, _: (0, 3)) for _ in pieces]


def route(m, info, inputs, mixed, pieces, gain, router, routes, cotangent, experts, capacity):
    width = inputs.shape[1]
    seq = inputs.shape[0] // MB
    big = (seq, width)
    outs = [
        jax.ShapeDtypeStruct(big, f32),
        jax.ShapeDtypeStruct(big, bf16),
        jax.ShapeDtypeStruct((seq, 128), f32),
        jax.ShapeDtypeStruct((2 * experts * capacity, width), bf16),
    ]
    return pl.pallas_call(
        functools.partial(route_kernel, capacity=capacity),
        grid_spec=pltpu.PrefetchScalarGridSpec(
            num_scalar_prefetch=1,
            grid=(1,),
            in_specs=[part(m, big), whole(big)]
            + proj_part(pieces)
            + [whole(gain.shape), whole(router.shape), part(m, (seq, 2)), part(m, big)],
            out_specs=[whole(out.shape) for out in outs],
        ),
        out_shape=outs,
        cost_estimate=cost(8e-6),
        name="route",
    )(info, inputs, mixed, *pieces, gain, router, routes, cotangent)


def combine_kernel(info, aux, routes, state, cotangent, gain, router_rows, *refs, experts):
    pieces, blocks, refs = refs[:2], refs[2], refs[3:]
    layer_out, grad_state, grad_attn, grad_mixed, grad_logits, gain_grad = refs
    length, core = info[0], info[1]
    seq = state.shape[0]
    capacity = blocks.shape[0] // (2 * experts)
    result, back = split_blocks(blocks, experts)
    lane = lax.broadcasted_iota(jnp.int32, aux.shape, 1)
    probs = jnp.where(lane < experts, aux[...], 0.0)
    live = lax.broadcasted_iota(jnp.int32, (seq, 1), 0) < length
    grad_out = jnp.where(live, cotangent[...], 0.0)
    picks, mixture, grad_probs = [], 0.0, 0.0
    for k in range(2):
        picks.append(pick_table(aux[:, SLOT_LANE + k : SLOT_LANE + k + 1], experts * capacity))
        picked = dot_nn(picks[k], result)
        mixture = mixture + aux[:, GATE_LANE + k : GATE_LANE + k + 1] * picked
        grad_gate = jnp.sum(grad_out * picked, axis=1, keepdims=True)
        grad_probs = grad_probs + jnp.where(lane == routes[:, k : k + 1], grad_gate, 0.0)
    values = state[...]
    layer_out[...] = jnp.where(live, values + mixture, 0.0).astype(bf16)
    logits = probs * (grad_probs - jnp.sum(probs * grad_probs, axis=1, keepdims=True))
    grad_logits[...] = logits
    grad = dot_nn(picks[0] + picks[1], back)
    for e in range(experts):
        grad = grad + logits[:, e : e + 1] * router_rows[e : e + 1, :]
    grad_norm, gain_sum = norm_back(values, gain[...], grad)
    gain_grad[...] = gain_sum
    total = grad_out + grad_norm
    grad_state[...] = total
    turned = halves(total.astype(bf16), core)
    grad_attn[...] = turned
    half = turned.shape[1] // 2
    grad_mixed[...] = (
        dot_nt(turned[:, :half], pieces[0][...]) + dot_nt(turned[:, half:], pieces[1][...])
    ).astype(bf16)


def combine(m, info, aux, routes, state, cotangent, gain, router_rows, pieces, blocks, experts):
    seq, width = state.shape
    big = (seq, width)
    outs = [
        jax.ShapeDtypeStruct(big, bf16),
        jax.ShapeDtypeStruct(big, f32),
        jax.ShapeDtypeStruct(big, bf16),
        jax.ShapeDtypeStruct(big, bf16),
        jax.ShapeDtypeStruct((seq, 128), f32),
        jax.ShapeDtypeStruct((1, width), f32),
    ]
    return pl.pallas_call(
        functools.partial(combine_kernel, experts=experts),
        grid_spec=pltpu.PrefetchScalarGridSpec(
            num_scalar_prefetch=1,
            grid=(1,),
            in_specs=[whole(aux.shape), part(m, (seq, 2)), whole(big), part(m, big)]
            + [whole(gain.shape), whole(router_rows.shape)]
            + proj_part(pieces)
            + [whole(blocks.shape)],
            out_specs=[whole(out.shape) for out in outs],
        ),
        out_shape=outs,
        cost_estimate=cost(8e-6),
        name="combine",
    )(info, aux, routes, state, cotangent, gain, router_rows, *pieces, blocks)


def enter_kernel(inputs, gain, *refs):
    pieces, (normed, packed) = refs[:2], refs[2:]
    values = inputs[...].astype(f32)
    rows = (values * inverse_root(values) * gain[...]).astype(bf16)
    normed[...] = rows
    span = pieces[0].shape[1] * 3 // 4
    for i, piece in enumerate(pieces):
        packed[:, i * span : (i + 1) * span] = dot_nn(rows, piece[:, :span]).astype(bf16)


def enter(inputs, gain, pieces):
    rows, width = inputs.shape
    return pl.pallas_call(
        enter_kernel,
        out_shape=[
            jax.ShapeDtypeStruct((rows, width), bf16),
            jax.ShapeDtypeStruct((rows, 3 * width), bf16),
        ],
        cost_estimate=cost(9e-6),
        compiler_params=pltpu.CompilerParams(vmem_limit_bytes=48 << 20),
        name="enter",
    )(inputs, gain, *pieces)


def leave_kernel(inputs, gain, *refs):
    pieces, (packed, *states), (out, gain_grad) = refs[:2], refs[2 : 3 + MB], refs[3 + MB :]
    seq = states[0].shape[0]
    span = pieces[0].shape[1] * 3 // 4
    total = 0.0
    for m in range(MB):
        r = pl.ds(m * seq, seq)
        grad = sum(
            dot_nt(packed[r, i * span : (i + 1) * span], piece[:, :span])
            for i, piece in enumerate(pieces)
        )
        grad_norm, gain_sum = norm_back(inputs[r, :].astype(f32), gain[...], grad)
        out[r, :] = states[m][...] + grad_norm
        total = total + gain_sum
    gain_grad[...] = total


def leave(inputs, gain, pieces, packed, states):
    return pl.pallas_call(
        leave_kernel,
        out_shape=[
            jax.ShapeDtypeStruct(inputs.shape, f32),
            jax.ShapeDtypeStruct(gain.shape, f32),
        ],
        cost_estimate=cost(12e-6),
        compiler_params=pltpu.CompilerParams(vmem_limit_bytes=48 << 20),
        name="leave",
    )(inputs, gain, *pieces, packed, *states)


def activations(rows_in, grads_in, gate_mat, up_mat, shrink_mat):
    gate = dot_nn(rows_in, gate_mat[...])
    up = dot_nn(rows_in, up_mat[...])
    grad = dot_nt(grads_in, shrink_mat[...])
    bent = jnp.tanh(tanh_scale * (gate + tanh_cubic * (gate * gate * gate)))
    half = 0.5 * (1.0 + bent)
    gelu = gate * half
    slope = half + gate * (0.5 * (1.0 - bent * bent)) * (
        tanh_scale * (1.0 + 3.0 * tanh_cubic * gate * gate)
    )
    return (gelu * up).astype(bf16), (slope * up * grad).astype(bf16), (gelu * grad).astype(bf16)


def split_blocks(blocks, experts):
    cap = blocks.shape[0] // (2 * experts)
    return (
        jnp.concatenate(
            [blocks[pl.ds((2 * e + i) * cap, cap), :] for e in range(experts)], axis=0
        )
        for i in range(2)
    )


def weight_grads(turned, hidden, pre, grads_in):
    expand_grad = sum(dot_nn(turned[m][...], pre[m][...]) for m in range(MB))
    shrink_grad = sum(dot_tn(hidden[m][...], grads_in[m]) for m in range(MB))
    return expand_grad.astype(bf16), shrink_grad.astype(bf16)


def first_kernel(members, *refs, experts, pieces):
    blocks, refs = refs[:MB], refs[MB:]
    mats, refs = refs[:pieces], refs[pieces:]
    (shrink_mat, expand_grad, shrink_grad), refs = refs[:3], refs[3:]
    sums, turned, refs = refs[: 2 * MB], refs[2 * MB : 3 * MB], refs[3 * MB :]
    hidden, pre, mats_whole = refs[:MB], refs[MB : 2 * MB], refs[2 * MB :]
    cap = blocks[0].shape[0] // (2 * experts)
    if pieces == 2:
        gate_mat, up_mat = mats
    else:
        gate_mat, up_mat = mats_whole
        for k, piece in enumerate(mats):
            count = piece.shape[0]
            r = pl.ds(pl.multiple_of(members[k % (pieces // 2)], count), count)
            mats_whole[k // (pieces // 2)][r, :] = piece[...]

    @pl.when(pl.program_id(0) == 0)
    def _():
        for total in sums:
            total[...] = jnp.zeros_like(total)
        for m in range(MB):
            for e in range(experts):
                rows_now = blocks[m][pl.ds(2 * e * cap, cap), :]
                turned[m][:, e * cap : (e + 1) * cap] = rows_now.T

    grads_in = []
    for m in range(MB):
        rows_in, grads = split_blocks(blocks[m], experts)
        grads_in.append(grads)
        act, pre_gate, pre_up = activations(rows_in, grads, gate_mat, up_mat, shrink_mat)
        hidden[m][...] = act
        pre[m][:, :TILE] = pre_gate
        pre[m][:, TILE:] = pre_up
        sums[2 * m][...] += dot_nn(act, shrink_mat[...])
        sums[2 * m + 1][...] += dot_nt(pre_gate, gate_mat[...]) + dot_nt(pre_up, up_mat[...])
    expand_grad[...], shrink_grad[...] = weight_grads(turned, hidden, pre, grads_in)


def full(shape, **options):
    return pl.BlockSpec(shape, lambda j, *_: (0, 0), **options)


def once(shape):
    return full(shape, pipeline_mode=pl.Buffered(1))


def column_tiles(rows, place=0, size=TILE):
    return pl.BlockSpec((rows, size), lambda j, *_: (0, place + j))


def row_tiles(width, place):
    return pl.BlockSpec((TILE, width), lambda j, *_: (place + j, 0))


def expert_first(blocks, mat, members, shrink_mat, tiles, experts):
    height, width = blocks[0].shape
    size = height // 2
    if isinstance(mat, list):
        mat_specs = [
            column_tiles(piece.shape[0], place) for place in (0, tiles) for piece in mat
        ]
        mat, whole_mats = mat * 2, [pltpu.VMEM((width, TILE), bf16)] * 2
    else:
        mat_specs = [column_tiles(width), column_tiles(width, tiles)]
        mat, whole_mats = [mat, mat], []
    return pl.pallas_call(
        functools.partial(first_kernel, experts=experts, pieces=len(mat)),
        grid_spec=pltpu.PrefetchScalarGridSpec(
            num_scalar_prefetch=1,
            grid=(tiles,),
            in_specs=[once((height, width))] * MB + mat_specs + [row_tiles(width, 0)],
            out_specs=[column_tiles(width, 0, 2 * TILE), row_tiles(width, 0)]
            + [full((size, width))] * (2 * MB)
            + [full((width, size))] * MB,
            scratch_shapes=[pltpu.VMEM((size, TILE), bf16)] * MB
            + [pltpu.VMEM((size, 2 * TILE), bf16)] * MB
            + whole_mats,
        ),
        out_shape=[
            jax.ShapeDtypeStruct((width, 2 * tiles * TILE), bf16),
            jax.ShapeDtypeStruct((FF, width), bf16),
        ]
        + [jax.ShapeDtypeStruct((size, width), f32)] * (2 * MB)
        + [jax.ShapeDtypeStruct((width, size), bf16)] * MB,
        compiler_params=pltpu.CompilerParams(
            dimension_semantics=("arbitrary",), vmem_limit_bytes=58 << 20
        ),
        cost_estimate=cost(8.5e-6 * tiles),
        name="expert",
    )(members, *blocks, *mat, shrink_mat)


def last_kernel(*refs, experts):
    blocks, gate_mat, up_mat, shrink_mat, result_in, grad_in, out, hidden, pre, result, grad = refs
    cap = blocks.shape[0] // (2 * experts)
    j = pl.program_id(0)

    @pl.when(j == 0)
    def _():
        result[...] = result_in[...]
        grad[...] = grad_in[...]

    rows_in, grads = split_blocks(blocks, experts)
    act, pre_gate, pre_up = activations(rows_in, grads, gate_mat, up_mat, shrink_mat)
    hidden[...] = act
    pre[:, :TILE] = pre_gate
    pre[:, TILE:] = pre_up
    result[...] += dot_nn(act, shrink_mat[...])
    grad[...] += dot_nt(pre_gate, gate_mat[...]) + dot_nt(pre_up, up_mat[...])

    @pl.when(j == pl.num_programs(0) - 1)
    def _():
        for e in range(experts):
            r = pl.ds(e * cap, cap)
            out[pl.ds(2 * e * cap, cap), :] = result[r, :].astype(bf16)
            out[pl.ds((2 * e + 1) * cap, cap), :] = grad[r, :].astype(bf16)


def expert_last(blocks, mat, shrink_mat, sums, place, tiles, experts):
    height, width = blocks.shape
    size = height // 2
    return pl.pallas_call(
        functools.partial(last_kernel, experts=experts),
        grid=(tiles,),
        in_specs=[once((height, width))]
        + [column_tiles(width), column_tiles(width, tiles), row_tiles(width, place)]
        + [once((size, width))] * 2,
        out_specs=[
            full((height, width)),
            pl.BlockSpec((size, TILE), lambda j: (0, j)),
            pl.BlockSpec((size, 2 * TILE), lambda j: (0, j)),
        ],
        out_shape=[
            jax.ShapeDtypeStruct((height, width), bf16),
            jax.ShapeDtypeStruct((size, tiles * TILE), bf16),
            jax.ShapeDtypeStruct((size, 2 * tiles * TILE), bf16),
        ],
        scratch_shapes=[pltpu.VMEM((size, width), f32)] * 2,
        compiler_params=pltpu.CompilerParams(
            dimension_semantics=("arbitrary",), vmem_limit_bytes=40 << 20
        ),
        cost_estimate=cost(3.0e-6 * tiles),
        name="expert_last",
    )(blocks, mat, mat, shrink_mat, *sums)


def weights_kernel(*refs, experts):
    turned, hidden, pre, refs = refs[:MB], refs[MB : 2 * MB], refs[2 * MB : 3 * MB], refs[3 * MB :]
    blocks, (_, expand_grad, shrink_grad) = refs[:MB], refs[MB:]
    grads_in = []
    for m in range(MB):
        _, grads = split_blocks(blocks[m], experts)
        grads_in.append(grads)
    expand_grad[...], shrink_grad[...] = weight_grads(turned, hidden, pre, grads_in)


def expert_weights(turned, hidden, pre, blocks, shrink_grad, place, tiles, experts):
    height, width = blocks[0].shape
    size = height // 2
    return pl.pallas_call(
        functools.partial(weights_kernel, experts=experts),
        grid=(tiles,),
        in_specs=[once((width, size))] * MB
        + [column_tiles(size)] * MB
        + [column_tiles(size, 0, 2 * TILE)] * MB
        + [once((height, width))] * MB
        + [pl.BlockSpec(memory_space=pl.ANY)],
        out_specs=[column_tiles(width, 0, 2 * TILE), row_tiles(width, place)],
        out_shape=[
            jax.ShapeDtypeStruct((width, 2 * tiles * TILE), bf16),
            jax.ShapeDtypeStruct((FF, width), bf16),
        ],
        input_output_aliases={4 * MB: 1},
        compiler_params=pltpu.CompilerParams(
            dimension_semantics=("arbitrary",), vmem_limit_bytes=40 << 20
        ),
        cost_estimate=cost(3.0e-6 * tiles),
        name="expert_weights",
    )(*turned, *hidden, *pre, *blocks, shrink_grad)


def adam_kernel(scales, master, first_old, second, gradient, *refs):
    master_out, first_out, second_out = refs[-3:]
    grad = gradient[...].astype(f32)
    first_new = beta_first * first_old[...] + (1.0 - beta_first) * grad
    second_new = beta_second * second[...] + (1.0 - beta_second) * grad * grad
    step = (first_new / scales[0]) / (jnp.sqrt(second_new / scales[1]) + adam_floor)
    master_out[...] = master[...] - scales[2] * (step + decay_rate * master[...])
    first_out[...] = first_new
    second_out[...] = second_new


def adam_expand(scales, states, gradient, kept, place, tiles):
    rows = states[0].shape[0]
    window = pl.BlockSpec((rows, TILE), lambda h, j, _: (0, h * (FF // TILE) + place + j))
    first = kept is None
    return pl.pallas_call(
        adam_kernel,
        grid_spec=pltpu.PrefetchScalarGridSpec(
            num_scalar_prefetch=1,
            grid=(2, tiles),
            in_specs=[window] * 3
            + [pl.BlockSpec((rows, TILE), lambda h, j, _: (0, 2 * j + h))]
            + ([] if first else [pl.BlockSpec(memory_space=pl.ANY)] * 3),
            out_specs=[window] * 3,
        ),
        out_shape=[jax.ShapeDtypeStruct(states[0].shape, f32)] * 3,
        input_output_aliases={} if first else {5: 0, 6: 1, 7: 2},
        cost_estimate=cost(1.5e-6 * tiles),
        name="adam",
    )(scales, *states, gradient, *(() if first else kept))


def inverse_root(values):
    return lax.rsqrt(jnp.mean(values * values, axis=-1, keepdims=True) + epsilon_norm)


def norm_back(values, gain, grad):
    root = inverse_root(values)
    scaled = grad * gain
    inner = jnp.mean(scaled * values, axis=-1, keepdims=True)
    grad_values = root * scaled - values * (root * root * root * inner)
    return grad_values, jnp.sum(grad * values * root, axis=0, keepdims=True)


def adam_update(master, first_old, second, gradient, counter, learn_rate):
    first_new = beta_first * first_old + (1.0 - beta_first) * gradient
    second_new = beta_second * second + (1.0 - beta_second) * gradient * gradient
    first_hat = first_new / (1.0 - beta_first**counter)
    second_hat = second_new / (1.0 - beta_second**counter)
    master_new = master - learn_rate * (
        first_hat / (jnp.sqrt(second_hat) + adam_floor) + decay_rate * master
    )
    return (master_new, first_new, second_new)


def after(values, *earlier):
    if isinstance(values, list):
        return list(lax.optimization_barrier((*values, *earlier))[: len(values)])
    return lax.optimization_barrier((values,) + earlier)[0]


def body(
    tokens,
    lengths,
    routes,
    cotangent,
    step_count,
    qkv_master,
    qkv_first,
    qkv_second,
    proj_master,
    proj_first,
    proj_second,
    table_master,
    table_first,
    table_second,
    gains_master,
    gains_first,
    gains_second,
    router_master,
    router_first,
    router_second,
    expand_master,
    expand_first,
    expand_second,
    shrink_master,
    shrink_first,
    shrink_second,
):
    experts = lax.axis_size("expert")
    devices = lax.axis_size("dp")
    length, width = tokens.shape[2], tokens.shape[3]
    heads = width // HEAD
    capacity = 5 * length // (2 * experts)
    slots = experts * capacity
    rows = MB * length
    ring = Ring()
    lower = lax.axis_index("expert") % 2 == 0

    def mine(values):
        half = values.shape[-1] // 2
        return jnp.where(lower, values[..., :half], values[..., half:])

    def joined(own, others):
        return [jnp.where(lower, own, others), jnp.where(lower, others, own)]

    small = jnp.concatenate(
        [table_master.reshape(-1), gains_master.reshape(-1), router_master.reshape(-1)]
    ).astype(bf16)
    small, small_marks = gather_small(small)
    cut_one = table_master.size
    cut_two = cut_one + gains_master.size
    table_vals = small[:, :cut_one].reshape(BUCKETS, heads).astype(f32)
    gains = small[:, cut_one:cut_two].reshape(devices, 2, width // devices)
    gains = gains.transpose(1, 0, 2).reshape(2, width).astype(f32)
    router_mat = small[:, cut_two:].reshape(width, experts)

    half = width // 2
    dense_half = jnp.concatenate(
        [mine(qkv_master[:, i * width : (i + 1) * width]) for i in range(3)] + [mine(proj_master)],
        axis=1,
    ).astype(bf16)
    if devices > RING_LIMIT:
        dense_own = lax.all_gather(dense_half, "dp", axis=0, tiled=True)
    else:
        moving = Moving(ring, [dense_half])
        for hop in range(devices // 2):
            moving.advance(small_marks[hop - 1] if 0 < hop <= len(small_marks) else None)
        dense_own = moving.placed(0).reshape(width, 2 * width)
    dense = [dense_own, swap(dense_own, "expert", 1)]

    ends = np.cumsum((0, *PARTS)) * TILE

    def expand_part(p):
        start, stop = ends[p], ends[p + 1]
        return [
            expand_master[0][:, start + shift : stop + shift].astype(bf16) for shift in (0, FF)
        ]

    shrink_rows = shrink_master.shape[1]
    cut = shrink_rows // 2
    first_local, last_local = (jnp.concatenate(expand_part(p), axis=1) for p in range(2))
    shrink_local = shrink_master[0].astype(bf16)
    mark = dense[1]
    if devices <= RING_LIMIT:
        moving = Moving(ring, [first_local, shrink_local])
        mark = moving.advance(mark)

    distance = (-np.arange(length)) % length
    onehot = jnp.asarray(
        (distance_buckets(length)[distance][:, None] == np.arange(BUCKETS)).astype(np.float32)
    )
    bias_rows = jnp.einsum("cb,bh->hc", onehot, table_vals, precision=HIGHEST)
    bias_rows = jnp.pad(
        bias_rows.reshape(heads // 2, 2, length), ((0, 0), (0, 6), (0, 0))
    )
    length_now = lengths[:, 0]
    me = lax.axis_index("expert")
    core = lax.rem(me, 2)
    infos = [jnp.stack([length_now[m], core]) for m in range(MB)]
    inputs = tokens.reshape(rows, width)
    normed_one, packed = enter(inputs, gains[0:1], dense)

    route_rows = routes.reshape(rows, 2)
    gradient = cotangent.reshape(rows, width)
    router_lanes = jnp.pad(router_mat, ((0, 0), (0, 128 - experts)))

    def exchange(blocks):
        blocks = blocks.reshape(experts, 2 * capacity, width)
        blocks = lax.all_to_all(blocks, "expert", split_axis=0, concat_axis=0, tiled=True)
        return blocks.reshape(2 * slots, width)

    mixed, state, normed_two, aux, expert_rows = [], [], [], [], []
    for m in range(MB):
        source = packed if m == 0 else after(packed, state[-1], mark)
        mixed.append(attend(m, infos[m], source, bias_rows, length))
        state_now, normed_now, aux_now, sent = route(
            m,
            infos[m],
            inputs,
            mixed[m],
            dense,
            gains[1:2],
            router_lanes,
            route_rows,
            gradient,
            experts,
            capacity,
        )
        state.append(state_now)
        normed_two.append(normed_now)
        aux.append(aux_now)
        expert_rows.append(exchange(sent))

    if devices > RING_LIMIT:
        first_mat = lax.all_gather(first_local, "dp", axis=0, tiled=True)
        members = jnp.zeros((1,), jnp.int32)
        shrink_mat = lax.all_gather(shrink_local, "dp", axis=0, tiled=True)
    else:
        gates = {2: state[0], 3: expert_rows[0], 4: expert_rows[1]}
        for hop in range(2, devices // 2 + 1):
            mark = moving.advance(gates.get(hop))
            if hop == GATE:
                last_local = after(last_local, mark)
        first_mat = [piece for _, _, piece in moving.arrived[0]]
        members = jnp.stack(
            [
                ring.member(offset) * first_local.shape[0] + row
                for offset, row, _ in moving.arrived[0]
            ]
        )
        shrink_mat = moving.placed(1).reshape(FF, width)
    last_mat = lax.all_gather(last_local, "dp", axis=0, tiled=True)

    block = width // devices
    share, shrink_grad, *middle = expert_first(
        expert_rows, first_mat, members, shrink_mat, PARTS[0], experts
    )
    expand_grads = [lax.psum_scatter(share, "dp", scatter_dimension=0, tiled=True)]
    returned, hidden, pre = [], [], []
    for m in range(MB):
        blocks, hidden_now, pre_now = expert_last(
            expert_rows[m] if m == 0 else after(expert_rows[m], returned[-1]),
            last_mat,
            shrink_mat,
            middle[2 * m : 2 * m + 2],
            PARTS[0],
            PARTS[1],
            experts,
        )
        hidden.append(hidden_now)
        pre.append(pre_now)
        returned.append(blocks)
    returned = [exchange(blocks) for blocks in returned]
    share, shrink_grad = expert_weights(
        middle[2 * MB :], hidden, pre, expert_rows, shrink_grad, *PARTS, experts
    )
    shrink_grad = shrink_grad.reshape(devices, 2 * cut, width)

    router_rows = router_mat.astype(f32).T
    counter = step_count[0].astype(f32)
    scales = jnp.stack([1.0 - beta_first**counter, 1.0 - beta_second**counter, rate_expand])
    expand_states = (expand_master[0], expand_first[0], expand_second[0])
    def shared(left, right, *earlier):
        middle = right.shape[1] // 2
        sent = swap(dot_tn(left, right[:, middle:]).astype(bf16), "expert", 1)
        share = dot_tn(after(left, *earlier), right[:, :middle]) + sent.astype(f32)
        return share.astype(bf16).reshape(devices, block, middle)

    last_share = share.reshape(devices, block, -1)
    scattering = Scattering(
        ring,
        [(last_share, block, last_share.shape[2], 0, 0)],
        [(shrink_grad, cut, width, i, 0) for i in range(2)],
    )
    combined, sums = [], []
    grad_packed = ()
    scattering.start(share, returned[0])
    mark = share
    for m in range(MB):
        blocks = after(returned[m], mark)
        combined.append(
            combine(
                m,
                infos[m],
                aux[m],
                route_rows,
                state[m],
                gradient,
                gains[1:2],
                router_rows,
                dense,
                blocks,
                experts,
            )
        )
        grad_mixed = combined[m][3]
        if m == MB - 1:
            grad_attn = jnp.concatenate([values[2] for values in combined], axis=0)
            proj_share = shared(jnp.concatenate(mixed, axis=0), grad_attn)
            grad_mixed = after(grad_mixed, proj_share)
        *grad_packed, sums_now = attend_back(
            m, infos[m], packed, bias_rows, grad_mixed, grad_packed
        )
        sums.append(sums_now)
        if m == 0:
            mark = scattering.settle(sums_now)
            scattering.start(returned[1])
    mark = scattering.settle(combined[1][1])
    scattering.start()
    (grad_packed,) = grad_packed
    layer_out, _, _, _, grad_logits, gain_sums = (jnp.stack(values) for values in zip(*combined))
    gains_two_grad = jnp.sum(gain_sums, axis=(0, 1))
    router_grad = jnp.einsum(
        "mtd,mte->de",
        jnp.stack(normed_two).astype(f32),
        grad_logits[:, :, :experts],
        precision=HIGHEST,
    )
    qkv_share = shared(normed_one, grad_packed, mark)
    expand_new = adam_expand(
        scales, expand_states, after(expand_grads[0], qkv_share), None, 0, PARTS[0]
    )
    dense_scattering = Scattering(
        ring,
        *(
            [
                (qkv_share, block // 2, 3 * half, i, 0),
                (proj_share, block // 2, half, i, 0),
            ]
            for i in range(2)
        ),
    )
    dense_scattering.start()
    table_grad = jnp.einsum(
        "hc,cb->bh",
        (sums[0] + sums[1])[:, :2].reshape(heads, length),
        onehot,
        precision=HIGHEST,
    )
    token_grad, gains_one_grad = leave(
        inputs,
        gains[0:1],
        dense,
        after(grad_packed, dense_scattering.blocks[0]),
        [values[1] for values in combined],
    )

    flat = jnp.concatenate(
        [
            table_grad.reshape(devices, -1),
            jnp.stack([gains_one_grad[0], gains_two_grad])
            .reshape(2, devices, block)
            .transpose(1, 0, 2)
            .reshape(devices, -1),
            router_grad.reshape(devices, -1),
        ],
        axis=1,
    )
    flat, small_marks = sum_small(flat)
    flat = flat[ring.me]
    table_grad = flat[:cut_one].reshape(table_master.shape)
    gains_grad = flat[cut_one:cut_two].reshape(gains_master.shape)
    router_grad = flat[cut_two:].reshape(router_master.shape)

    if devices <= RING_LIMIT:
        mark = dense_scattering.settle(token_grad)
        scattering.settle(token_grad)
        scattering.start()
        for hop in range(2, devices // 2 + 1):
            dense_scattering.start(small_marks[hop - 2])
            if hop == 3:
                scattering.settle(mark)
            mark = dense_scattering.settle(expand_new[0])
    done = dense_scattering.finish()
    done = jnp.concatenate(done, axis=0)
    last_grad, shrink_grad = scattering.finish()
    expand_grads.append(last_grad)
    shrink_grad = jnp.concatenate([shrink_grad[:, :width], shrink_grad[:, width:]], axis=0)
    bit = 2
    while bit < experts:
        done = done.astype(bf16)
        done = done.astype(f32) + swap(done, "expert", bit).astype(f32)
        bit *= 2
    others = swap(done, "expert", 1)

    parts = [
        joined(done[:, i * half : (i + 1) * half], others[:, i * half : (i + 1) * half])
        for i in range(4)
    ]
    qkv_grad = jnp.concatenate(parts[0] + parts[1] + parts[2], axis=1)
    proj_grad = jnp.concatenate(parts[3], axis=1)

    states = (
        (qkv_master, qkv_first, qkv_second, qkv_grad),
        (proj_master, proj_first, proj_second, proj_grad),
        (table_master, table_first, table_second, table_grad),
        (gains_master, gains_first, gains_second, gains_grad),
        (router_master, router_first, router_second, router_grad),
        (shrink_master, shrink_first, shrink_second, shrink_grad[None]),
    )
    fresh = []
    for (master, first_old, second, gradient), learn_rate in zip(states, rate_table):
        fresh.append(adam_update(master, first_old, second, gradient, counter, learn_rate))
    kept = adam_expand(scales, expand_states, expand_grads[1], expand_new, PARTS[0], PARTS[1])
    fresh.insert(5, tuple(value[None] for value in kept))
    fresh = [value for group in fresh for value in group]
    return (
        layer_out.reshape(MB, 1, length, width),
        token_grad.reshape(MB, 1, length, width),
        *fresh,
    )


def solution(mesh):
    sequences = P(None, ("dp", "expert"), None, None)
    over_rows = P("dp", None)
    over_columns = P(None, "dp")
    by_expert = P("expert", "dp", None)
    weights = (
        (over_rows,) * 9 + (over_columns,) * 3 + (over_rows,) * 3 + (by_expert,) * 6
    )
    return jax.shard_map(
        body,
        mesh=mesh,
        in_specs=(sequences, P(None, ("dp", "expert")), sequences, sequences, P()) + weights,
        out_specs=(sequences, sequences) + weights,
        check_vma=False,
    )
```

```python
import functools

import jax
import jax.numpy as jnp
import numpy as np
from jax import lax
from jax.experimental import pallas as pl
from jax.experimental.pallas import tpu as pltpu
from jax.sharding import PartitionSpec as P

HEAD = 64
FF = 2816
BUCKETS = 32
MB = 2
TILE = 256
PARTS = (7, 4)
RING_LIMIT = 8
GATE = 4

HIGHEST = lax.Precision.HIGHEST
f32 = jnp.float32
bf16 = jnp.bfloat16
epsilon_norm = 1e-06
beta_first = 0.9
beta_second = 0.95
adam_floor = 1e-08
decay_rate = 0.1
rate_table = (0.03, 0.1, 0.3, 0.1, 0.03, 0.03)
rate_expand = np.float32(0.03)
tanh_scale = 0.7978845608028654
tanh_cubic = 0.044715


def dot_nn(a, b):
    return lax.dot_general(a, b, (((1,), (0,)), ((), ())), preferred_element_type=f32)


def dot_nt(a, b):
    return lax.dot_general(a, b, (((1,), (1,)), ((), ())), preferred_element_type=f32)


def dot_tn(a, b):
    return lax.dot_general(a, b, (((0,), (0,)), ((), ())), preferred_element_type=f32)


def cost(seconds):
    return pl.CostEstimate(
        flops=int(seconds * 1e15), transcendentals=0, bytes_accessed=int(seconds * 3e12)
    )


def distance_buckets(length):
    spread = np.arange(length)
    exact_span = BUCKETS // 2
    scaled = np.log(np.maximum(spread, 1) / exact_span) / np.log(128.0 / exact_span)
    farther = np.minimum(
        exact_span + (scaled * (BUCKETS - exact_span)).astype(np.int64), BUCKETS - 1
    )
    return np.where(spread < exact_span, spread, farther).astype(np.int32)


def ring_order(count):
    if count % 2:
        return list(range(count))
    return list(range(0, count, 2)) + list(range(count - 1, 0, -2))


class Ring:
    def __init__(self):
        self.count = n = lax.axis_size("dp")
        self.order = ring_order(n)
        self.me = me = lax.axis_index("dp")
        if n % 2:
            place = me
        else:
            place = jnp.where(me % 2 == 0, me // 2, n - (me + 1) // 2)
        self.others = []
        for offset in range(1, n if n <= RING_LIMIT else 1):
            other = lax.rem(place + offset, n)
            if n % 2 == 0:
                other = jnp.where(other < n // 2, 2 * other, 2 * n - 1 - 2 * other)
            self.others.append(other)

    def member(self, offset):
        offset %= self.count
        return self.others[offset - 1] if offset else self.me

    def step(self, values, way):
        n, order = self.count, self.order
        pairs = [(order[i], order[(i + way) % n]) for i in range(n)]
        return lax.ppermute(values, "dp", pairs)


class Moving:
    def __init__(self, ring, blocks):
        self.ring = ring
        self.ahead, self.behind = list(blocks), list(blocks)
        self.hops = 0
        self.arrived = [[(0, 0, block)] for block in blocks]

    def advance(self, gate=None):
        self.hops += 1
        hop, count = self.hops, len(self.ahead)
        ahead, behind = self.ahead, self.behind
        cuts = [0] * count
        if hop == self.ring.count // 2:
            cuts = [block.shape[0] // 2 for block in ahead]
            ahead = [block[:cut] for block, cut in zip(ahead, cuts)]
            behind = [block[cut:] for block, cut in zip(behind, cuts)]
        blocks = (*ahead, *behind)
        if gate is not None:
            blocks = lax.optimization_barrier((*blocks, gate))[:-1]
        blocks = lax.optimization_barrier(
            tuple(self.ring.step(block, 1 if k < count else -1) for k, block in enumerate(blocks))
        )
        self.ahead, self.behind = blocks[:count], blocks[count:]
        for k in range(count):
            self.arrived[k].append((-hop, 0, self.ahead[k]))
            self.arrived[k].append((hop, cuts[k], self.behind[k]))
        return blocks[0]

    def placed(self, k):
        block = self.arrived[k][0][2]
        whole = jnp.zeros((self.ring.count,) + block.shape, block.dtype)
        for offset, row, block in self.arrived[k]:
            index = (self.ring.member(offset), row) + (0,) * (block.ndim - 1)
            whole = lax.dynamic_update_slice(
                whole, block[None], index, allow_negative_indices=False
            )
        return whole


class Scattering:
    def __init__(self, ring, top, bottom):
        self.ring, self.groups, self.hops = ring, (top, bottom), 0
        self.alone = ring.count > RING_LIMIT
        self.blocks = [top[0][0]]
        if not self.alone:
            self.add(None)

    def add(self, received, gates=()):
        self.blocks = add_shares(received, self.groups, self.hops, self.ring, gates)

    def start(self, *gates):
        if not self.alone:
            blocks = after(list(self.blocks), *gates)
            self.received = [self.ring.step(block, way) for block, way in zip(blocks, (1, -1))]

    def settle(self, *gates):
        if self.alone:
            return gates[0]
        self.hops += 1
        self.add(self.received, gates)
        return self.blocks[0]

    def finish(self):
        if not self.alone:
            return self.blocks
        return [
            jnp.concatenate(
                [
                    lax.psum_scatter(
                        shares[:, r * i : r * (i + 1), c * j : c * (j + 1)],
                        "dp",
                        scatter_dimension=0,
                    ).astype(f32)
                    for shares, r, c, i, j in group
                ],
                axis=1,
            )
            for group in self.groups
        ]


def add_kernel(members, *refs, counts, rows, hop, last):
    received, refs = (refs[:2], refs[2:]) if hop else ((), refs)
    ways = 1 if last else 2
    for way in range(ways):
        start_row = 0
        for g in range(2):
            if hop == 0 and g != way:
                continue
            windows, refs = refs[: counts[g]], refs[counts[g] :]
            start = 0
            for window in windows:
                span = pl.ds(start, window.shape[-1])
                value = window[0].astype(f32)
                for side in (0, 1) if last else (way,):
                    if hop > 1:
                        value = value + received[side][pl.ds(start_row, rows[g]), span].astype(f32)
                    elif hop == 1 and side == g:
                        value = value + received[side][:, span].astype(f32)
                if last:
                    out, r = refs_out(refs, 2)[g], pl.ds(0, rows[g])
                elif hop == 0:
                    out, r = refs_out(refs, 2)[way], pl.ds(0, rows[g])
                else:
                    out, r = refs_out(refs, 2)[way], pl.ds(start_row, rows[g])
                out[r, span] = value.astype(out.dtype)
                start += window.shape[-1]
            start_row += rows[g]


def refs_out(refs, count):
    return refs[len(refs) - count :]


def add_shares(received, groups, hop, ring, gates):
    last = hop == ring.count // 2
    rows = [group[0][1] for group in groups]
    widths = [sum(window[2] for window in group) for group in groups]
    distance = ring.count // 2 - hop
    members = [ring.member(distance), ring.member(-distance)]
    in_specs, operands = [], []
    for block in received or ():
        in_specs.append(pl.BlockSpec(block.shape, lambda i, _: (0, 0)))
        operands.append(block)
    for way in range(1 if last else 2):
        for g, group in enumerate(groups):
            if hop == 0 and g != way:
                continue
            for shares, r, c, row, column in group:
                in_specs.append(
                    pl.BlockSpec(
                        (1, r, c),
                        lambda i, members, way=way, row=row, column=column: (
                            members[way],
                            row,
                            column,
                        ),
                    )
                )
                operands.append(shares)
    in_specs += [pl.BlockSpec(memory_space=pl.ANY) for _ in gates]
    operands += gates
    if last:
        outs = [jax.ShapeDtypeStruct(shape, f32) for shape in zip(rows, widths)]
    elif hop == 0:
        outs = [jax.ShapeDtypeStruct(shape, bf16) for shape in zip(rows, widths)]
    else:
        outs = [jax.ShapeDtypeStruct((sum(rows), widths[0]), bf16)] * 2
    return pl.pallas_call(
        functools.partial(
            add_kernel, counts=[len(group) for group in groups], rows=rows, hop=hop, last=last
        ),
        grid_spec=pltpu.PrefetchScalarGridSpec(
            num_scalar_prefetch=1,
            grid=(1,),
            in_specs=in_specs,
            out_specs=[pl.BlockSpec(out.shape, lambda i, _: (0, 0)) for out in outs],
        ),
        out_shape=outs,
        cost_estimate=cost(3e-6),
        name="add_shares",
    )(jnp.stack(members), *operands)


def swap(values, axis, bit):
    count = lax.axis_size(axis)
    return lax.ppermute(values, axis, [(i, i ^ bit) for i in range(count)])


def gather_small(values):
    count = lax.axis_size("dp")
    rows = values[None]
    bit = 1
    marks = []
    while bit < count:
        rows = jnp.concatenate([rows, swap(rows, "dp", bit)], axis=0)
        marks.append(rows)
        bit *= 2
    return rows[jnp.arange(count) ^ lax.axis_index("dp")], marks


def sum_small(values):
    marks = []
    for axis in ("expert", "dp"):
        bit = 1
        while bit < lax.axis_size(axis):
            values = values + swap(values, axis, bit)
            marks.append(values)
            bit *= 2
    return values, marks


def head_probs(query, key, bias_row, length):
    seq = query.shape[0]
    scores = dot_nt(query, key) * HEAD ** (-0.5)
    bias = pltpu.roll(
        jnp.broadcast_to(bias_row, (seq, seq)), 0, 1, stride=1, stride_axis=0
    )
    row = lax.broadcasted_iota(jnp.int32, (seq, seq), 0)
    column = lax.broadcasted_iota(jnp.int32, (seq, seq), 1)
    scores = jnp.where((column <= row) & (column < length), scores + bias, -1e30)
    exps = jnp.exp(scores - jnp.max(scores, axis=1, keepdims=True))
    return exps / jnp.sum(exps, axis=1, keepdims=True)


def attend_kernel(info, query, key, value, bias_rows, mixed):
    length = info[0]
    for half in range(2):
        c = pl.ds(HEAD * half, HEAD)
        probs = head_probs(query[:, c], key[:, c], bias_rows[0, half : half + 1, :], length)
        mixed[:, c] = dot_nn(probs.astype(bf16), value[:, c]).astype(bf16)


def diagonal_sums(values):
    seq = values.shape[0]
    eight = values[0:8, :]
    for t in range(1, seq // 8):
        eight = eight + pltpu.roll(values[8 * t : 8 * t + 8, :], seq - 8 * t, 1)
    total = eight[0:1, :]
    for t in range(1, 8):
        total = total + pltpu.roll(eight, seq - t, 1)[t : t + 1, :]
    return total


def attend_back_kernel(info, query, key, value, bias_rows, grad, *refs):
    grad_packed, sums = refs[-2:]
    seq = query.shape[0]
    h = pl.program_id(0)
    length, core = info[0], info[1]
    places = packed_places(h, pl.num_programs(0), core)
    offsets = [pl.multiple_of(place * 2 * HEAD, 2 * HEAD) for place in places]
    parts = [[], [], []]
    for half in range(2):
        c = pl.ds(HEAD * half, HEAD)
        q, k, v, g = query[:, c], key[:, c], value[:, c], grad[:, c]
        probs = head_probs(q, k, bias_rows[0, half : half + 1, :], length)
        grad_probs = dot_nt(g, v)
        scores = probs * (grad_probs - jnp.sum(probs * grad_probs, axis=1, keepdims=True))
        rounded = scores.astype(bf16)
        parts[0].append((dot_nn(rounded, k) * HEAD ** (-0.5)).astype(bf16))
        parts[1].append((dot_tn(rounded, q) * HEAD ** (-0.5)).astype(bf16))
        parts[2].append(dot_tn(probs.astype(bf16), g).astype(bf16))
        sums[0, half : half + 1, :] = diagonal_sums(scores)
    sums[0, 2:8, :] = jnp.zeros((6, seq), f32)
    for offset, part in zip(offsets, parts):
        grad_packed[:, pl.ds(offset, 2 * HEAD)] = jnp.concatenate(part, axis=1)


def packed_places(h, pairs, core):
    half = pairs // 2
    first = jnp.where(h // half == core, 0, 3 * half) + lax.rem(h, half)
    return first, first + half, first + 2 * half


def pair_windows(m, seq, pairs):
    return [
        pl.BlockSpec(
            (seq, 2 * HEAD),
            lambda h, info, part=part: (m, packed_places(h, pairs, info[1])[part]),
        )
        for part in range(3)
    ]


def attend(m, info, packed, bias_rows, seq):
    width = packed.shape[1] // 3
    pairs = width // (2 * HEAD)
    return pl.pallas_call(
        attend_kernel,
        grid_spec=pltpu.PrefetchScalarGridSpec(
            num_scalar_prefetch=1,
            grid=(pairs,),
            in_specs=pair_windows(m, seq, pairs)
            + [pl.BlockSpec((1, 8, seq), lambda h, _: (h, 0, 0))],
            out_specs=pl.BlockSpec((seq, 2 * HEAD), lambda h, _: (0, h)),
        ),
        out_shape=jax.ShapeDtypeStruct((seq, width), bf16),
        cost_estimate=cost(10e-6),
        name="attend",
    )(info, packed, packed, packed, bias_rows)


def attend_back(m, info, packed, bias_rows, grad, kept):
    seq, width = grad.shape
    pairs = width // (2 * HEAD)

    return pl.pallas_call(
        attend_back_kernel,
        grid_spec=pltpu.PrefetchScalarGridSpec(
            num_scalar_prefetch=1,
            grid=(pairs,),
            in_specs=pair_windows(m, seq, pairs)
            + [
                pl.BlockSpec((1, 8, seq), lambda h, _: (h, 0, 0)),
                pl.BlockSpec((seq, 2 * HEAD), lambda h, _: (0, h)),
            ]
            + [pl.BlockSpec(memory_space=pl.ANY) for _ in kept],
            out_specs=[
                pl.BlockSpec((seq, 3 * width), lambda h, _: (m, 0)),
                pl.BlockSpec((1, 8, seq), lambda h, _: (h, 0, 0)),
            ],
        ),
        out_shape=[
            jax.ShapeDtypeStruct(packed.shape, bf16),
            jax.ShapeDtypeStruct((pairs, 8, seq), f32),
        ],
        input_output_aliases={6: 0} if kept else {},
        cost_estimate=cost(16e-6),
        name="attend_back",
    )(info, packed, packed, packed, bias_rows, grad, *kept)


SLOT_LANE, GATE_LANE = 16, 18


def halves(values, core):
    half = values.shape[1] // 2
    turned = jnp.concatenate([values[:, half:], values[:, :half]], axis=1)
    return jnp.where(core == 0, values, turned)


def pick_table(slot, slots):
    lane = lax.broadcasted_iota(jnp.int32, (slot.shape[0], slots), 1).astype(f32)
    return jnp.where(lane == slot, 1.0, 0.0).astype(bf16)


def route_kernel(info, inputs, mixed, *refs, capacity):
    pieces, refs = refs[:2], refs[2:]
    gain, router, routes, cotangent, state, normed, aux, out = refs
    length, core = info[0], info[1]
    seq = inputs.shape[0]
    experts = out.shape[0] // (2 * capacity)
    added = jnp.concatenate([dot_nn(mixed[...], piece[...]) for piece in pieces], axis=1)
    values = inputs[...].astype(f32) + halves(added, core)
    state[...] = values
    rows = (values * inverse_root(values) * gain[...]).astype(bf16)
    normed[...] = rows
    logits = dot_nn(rows, router[...])
    lane = lax.broadcasted_iota(jnp.int32, logits.shape, 1)
    logits = jnp.where(lane < experts, logits, -1e30)
    exps = jnp.exp(logits - jnp.max(logits, axis=1, keepdims=True))
    probs = exps / jnp.sum(exps, axis=1, keepdims=True)
    live = lax.broadcasted_iota(jnp.int32, (seq, 1), 0) < length
    named = [routes[:, k : k + 1] for k in range(2)]
    hits = [jnp.where((lane == name) & live, 1.0, 0.0) for name in named]
    before = lax.broadcasted_iota(jnp.int32, (seq, seq), 0) > lax.broadcasted_iota(
        jnp.int32, (seq, seq), 1
    )
    earlier = dot_nn(
        jnp.where(before, 1.0, 0.0).astype(bf16), (hits[0] + hits[1]).astype(bf16)
    )
    grad_out = jnp.where(live, cotangent[...], 0.0)
    kept = probs
    picks, grads = [], []
    for k in range(2):
        rank = jnp.sum(hits[k] * earlier, axis=1, keepdims=True)
        slot = (named[k] * capacity).astype(f32) + rank
        slot = jnp.where(live, slot, float(experts * capacity))
        gate = jnp.sum(hits[k] * probs, axis=1, keepdims=True)
        kept = jnp.where(lane == SLOT_LANE + k, slot, kept)
        kept = jnp.where(lane == GATE_LANE + k, gate, kept)
        picks.append(pick_table(slot, experts * capacity))
        grads.append((gate * grad_out).astype(bf16))
    aux[...] = kept
    sent = dot_tn(picks[0] + picks[1], rows).astype(bf16)
    sent_grads = (dot_tn(picks[0], grads[0]) + dot_tn(picks[1], grads[1])).astype(bf16)
    for e in range(experts):
        r = slice(e * capacity, (e + 1) * capacity)
        out[pl.ds(2 * e * capacity, capacity), :] = sent[r, :]
        out[pl.ds((2 * e + 1) * capacity, capacity), :] = sent_grads[r, :]


def whole(shape):
    return pl.BlockSpec(shape, lambda i, _: (0,) * len(shape))


def part(m, shape):
    return pl.BlockSpec(shape, lambda i, _: (m,) + (0,) * (len(shape) - 1))


def proj_part(pieces):
    width = pieces[0].shape[0]
    return [pl.BlockSpec((width, width // 2), lambda i, _: (0, 3)) for _ in pieces]


def route(m, info, inputs, mixed, pieces, gain, router, routes, cotangent, experts, capacity):
    width = inputs.shape[1]
    seq = inputs.shape[0] // MB
    big = (seq, width)
    outs = [
        jax.ShapeDtypeStruct(big, f32),
        jax.ShapeDtypeStruct(big, bf16),
        jax.ShapeDtypeStruct((seq, 128), f32),
        jax.ShapeDtypeStruct((2 * experts * capacity, width), bf16),
    ]
    return pl.pallas_call(
        functools.partial(route_kernel, capacity=capacity),
        grid_spec=pltpu.PrefetchScalarGridSpec(
            num_scalar_prefetch=1,
            grid=(1,),
            in_specs=[part(m, big), whole(big)]
            + proj_part(pieces)
            + [whole(gain.shape), whole(router.shape), part(m, (seq, 2)), part(m, big)],
            out_specs=[whole(out.shape) for out in outs],
        ),
        out_shape=outs,
        cost_estimate=cost(8e-6),
        name="route",
    )(info, inputs, mixed, *pieces, gain, router, routes, cotangent)


def combine_kernel(info, aux, routes, state, cotangent, gain, router_rows, *refs, experts):
    pieces, blocks, refs = refs[:2], refs[2], refs[3:]
    layer_out, grad_state, grad_attn, grad_mixed, grad_logits, gain_grad = refs
    length, core = info[0], info[1]
    seq = state.shape[0]
    capacity = blocks.shape[0] // (2 * experts)
    result, back = split_blocks(blocks, experts)
    lane = lax.broadcasted_iota(jnp.int32, aux.shape, 1)
    probs = jnp.where(lane < experts, aux[...], 0.0)
    live = lax.broadcasted_iota(jnp.int32, (seq, 1), 0) < length
    grad_out = jnp.where(live, cotangent[...], 0.0)
    picks, mixture, grad_probs = [], 0.0, 0.0
    for k in range(2):
        picks.append(pick_table(aux[:, SLOT_LANE + k : SLOT_LANE + k + 1], experts * capacity))
        picked = dot_nn(picks[k], result)
        mixture = mixture + aux[:, GATE_LANE + k : GATE_LANE + k + 1] * picked
        grad_gate = jnp.sum(grad_out * picked, axis=1, keepdims=True)
        grad_probs = grad_probs + jnp.where(lane == routes[:, k : k + 1], grad_gate, 0.0)
    values = state[...]
    layer_out[...] = jnp.where(live, values + mixture, 0.0).astype(bf16)
    logits = probs * (grad_probs - jnp.sum(probs * grad_probs, axis=1, keepdims=True))
    grad_logits[...] = logits
    grad = dot_nn(picks[0] + picks[1], back)
    for e in range(experts):
        grad = grad + logits[:, e : e + 1] * router_rows[e : e + 1, :]
    grad_norm, gain_sum = norm_back(values, gain[...], grad)
    gain_grad[...] = gain_sum
    total = grad_out + grad_norm
    grad_state[...] = total
    turned = halves(total.astype(bf16), core)
    grad_attn[...] = turned
    half = turned.shape[1] // 2
    grad_mixed[...] = (
        dot_nt(turned[:, :half], pieces[0][...]) + dot_nt(turned[:, half:], pieces[1][...])
    ).astype(bf16)


def combine(m, info, aux, routes, state, cotangent, gain, router_rows, pieces, blocks, experts):
    seq, width = state.shape
    big = (seq, width)
    outs = [
        jax.ShapeDtypeStruct(big, bf16),
        jax.ShapeDtypeStruct(big, f32),
        jax.ShapeDtypeStruct(big, bf16),
        jax.ShapeDtypeStruct(big, bf16),
        jax.ShapeDtypeStruct((seq, 128), f32),
        jax.ShapeDtypeStruct((1, width), f32),
    ]
    return pl.pallas_call(
        functools.partial(combine_kernel, experts=experts),
        grid_spec=pltpu.PrefetchScalarGridSpec(
            num_scalar_prefetch=1,
            grid=(1,),
            in_specs=[whole(aux.shape), part(m, (seq, 2)), whole(big), part(m, big)]
            + [whole(gain.shape), whole(router_rows.shape)]
            + proj_part(pieces)
            + [whole(blocks.shape)],
            out_specs=[whole(out.shape) for out in outs],
        ),
        out_shape=outs,
        cost_estimate=cost(8e-6),
        name="combine",
    )(info, aux, routes, state, cotangent, gain, router_rows, *pieces, blocks)


def enter_kernel(inputs, gain, *refs):
    pieces, (normed, packed) = refs[:2], refs[2:]
    values = inputs[...].astype(f32)
    rows = (values * inverse_root(values) * gain[...]).astype(bf16)
    normed[...] = rows
    span = pieces[0].shape[1] * 3 // 4
    for i, piece in enumerate(pieces):
        packed[:, i * span : (i + 1) * span] = dot_nn(rows, piece[:, :span]).astype(bf16)


def enter(inputs, gain, pieces):
    rows, width = inputs.shape
    return pl.pallas_call(
        enter_kernel,
        out_shape=[
            jax.ShapeDtypeStruct((rows, width), bf16),
            jax.ShapeDtypeStruct((rows, 3 * width), bf16),
        ],
        cost_estimate=cost(9e-6),
        compiler_params=pltpu.CompilerParams(vmem_limit_bytes=48 << 20),
        name="enter",
    )(inputs, gain, *pieces)


def leave_kernel(inputs, gain, *refs):
    pieces, (packed, *states), (_, out, gain_grad) = refs[:2], refs[2 : 3 + MB], refs[3 + MB :]
    seq = states[0].shape[0]
    span = pieces[0].shape[1] * 3 // 4
    total = 0.0
    for m in range(MB):
        r = pl.ds(m * seq, seq)
        grad = sum(
            dot_nt(packed[r, i * span : (i + 1) * span], piece[:, :span])
            for i, piece in enumerate(pieces)
        )
        grad_norm, gain_sum = norm_back(inputs[r, :].astype(f32), gain[...], grad)
        out[r, :] = states[m][...] + grad_norm
        total = total + gain_sum
    gain_grad[...] = total


def leave(inputs, gain, pieces, packed, states, gate):
    operands = (inputs, gain, *pieces, packed, *states)
    return pl.pallas_call(
        leave_kernel,
        in_specs=[pl.BlockSpec(memory_space=pltpu.VMEM) for _ in operands]
        + [pl.BlockSpec(memory_space=pl.ANY)],
        out_shape=[
            jax.ShapeDtypeStruct(inputs.shape, f32),
            jax.ShapeDtypeStruct(gain.shape, f32),
        ],
        cost_estimate=cost(12e-6),
        compiler_params=pltpu.CompilerParams(vmem_limit_bytes=48 << 20),
        name="leave",
    )(*operands, gate)


def activations(rows_in, grads_in, gate_mat, up_mat, shrink_mat):
    gate = dot_nn(rows_in, gate_mat[...])
    up = dot_nn(rows_in, up_mat[...])
    grad = dot_nt(grads_in, shrink_mat[...])
    bent = jnp.tanh(tanh_scale * (gate + tanh_cubic * (gate * gate * gate)))
    half = 0.5 * (1.0 + bent)
    gelu = gate * half
    slope = half + gate * (0.5 * (1.0 - bent * bent)) * (
        tanh_scale * (1.0 + 3.0 * tanh_cubic * gate * gate)
    )
    return (gelu * up).astype(bf16), (slope * up * grad).astype(bf16), (gelu * grad).astype(bf16)


def split_blocks(blocks, experts):
    cap = blocks.shape[0] // (2 * experts)
    return (
        jnp.concatenate(
            [blocks[pl.ds((2 * e + i) * cap, cap), :] for e in range(experts)], axis=0
        )
        for i in range(2)
    )


def weight_grads(turned, hidden, pre, grads_in):
    expand_grad = sum(dot_nn(turned[m][...], pre[m][...]) for m in range(MB))
    shrink_grad = sum(dot_tn(hidden[m][...], grads_in[m]) for m in range(MB))
    return expand_grad.astype(bf16), shrink_grad.astype(bf16)


def first_kernel(members, *refs, experts, pieces):
    blocks, refs = refs[:MB], refs[MB:]
    mats, refs = refs[:pieces], refs[pieces:]
    (shrink_mat, expand_grad, shrink_grad), refs = refs[:3], refs[3:]
    sums, turned, refs = refs[: 2 * MB], refs[2 * MB : 3 * MB], refs[3 * MB :]
    hidden, pre, mats_whole = refs[:MB], refs[MB : 2 * MB], refs[2 * MB :]
    cap = blocks[0].shape[0] // (2 * experts)
    if pieces == 2:
        gate_mat, up_mat = mats
    else:
        gate_mat, up_mat = mats_whole
        for k, piece in enumerate(mats):
            count = piece.shape[0]
            r = pl.ds(pl.multiple_of(members[k % (pieces // 2)], count), count)
            mats_whole[k // (pieces // 2)][r, :] = piece[...]

    @pl.when(pl.program_id(0) == 0)
    def _():
        for total in sums:
            total[...] = jnp.zeros_like(total)
        for m in range(MB):
            for e in range(experts):
                rows_now = blocks[m][pl.ds(2 * e * cap, cap), :]
                turned[m][:, e * cap : (e + 1) * cap] = rows_now.T

    grads_in = []
    for m in range(MB):
        rows_in, grads = split_blocks(blocks[m], experts)
        grads_in.append(grads)
        act, pre_gate, pre_up = activations(rows_in, grads, gate_mat, up_mat, shrink_mat)
        hidden[m][...] = act
        pre[m][:, :TILE] = pre_gate
        pre[m][:, TILE:] = pre_up
        sums[2 * m][...] += dot_nn(act, shrink_mat[...])
        sums[2 * m + 1][...] += dot_nt(pre_gate, gate_mat[...]) + dot_nt(pre_up, up_mat[...])
    expand_grad[...], shrink_grad[...] = weight_grads(turned, hidden, pre, grads_in)


def full(shape, **options):
    return pl.BlockSpec(shape, lambda j, *_: (0, 0), **options)


def once(shape):
    return full(shape, pipeline_mode=pl.Buffered(1))


def column_tiles(rows, place=0, size=TILE):
    return pl.BlockSpec((rows, size), lambda j, *_: (0, place + j))


def row_tiles(width, place):
    return pl.BlockSpec((TILE, width), lambda j, *_: (place + j, 0))


def expert_first(blocks, mat, members, shrink_mat, tiles, experts):
    height, width = blocks[0].shape
    size = height // 2
    if isinstance(mat, list):
        mat_specs = [
            column_tiles(piece.shape[0], place) for place in (0, tiles) for piece in mat
        ]
        mat, whole_mats = mat * 2, [pltpu.VMEM((width, TILE), bf16)] * 2
    else:
        mat_specs = [column_tiles(width), column_tiles(width, tiles)]
        mat, whole_mats = [mat, mat], []
    return pl.pallas_call(
        functools.partial(first_kernel, experts=experts, pieces=len(mat)),
        grid_spec=pltpu.PrefetchScalarGridSpec(
            num_scalar_prefetch=1,
            grid=(tiles,),
            in_specs=[once((height, width))] * MB + mat_specs + [row_tiles(width, 0)],
            out_specs=[column_tiles(width, 0, 2 * TILE), row_tiles(width, 0)]
            + [full((size, width))] * (2 * MB)
            + [full((width, size))] * MB,
            scratch_shapes=[pltpu.VMEM((size, TILE), bf16)] * MB
            + [pltpu.VMEM((size, 2 * TILE), bf16)] * MB
            + whole_mats,
        ),
        out_shape=[
            jax.ShapeDtypeStruct((width, 2 * tiles * TILE), bf16),
            jax.ShapeDtypeStruct((FF, width), bf16),
        ]
        + [jax.ShapeDtypeStruct((size, width), f32)] * (2 * MB)
        + [jax.ShapeDtypeStruct((width, size), bf16)] * MB,
        compiler_params=pltpu.CompilerParams(
            dimension_semantics=("arbitrary",), vmem_limit_bytes=58 << 20
        ),
        cost_estimate=cost(8.5e-6 * tiles),
        name="expert",
    )(members, *blocks, *mat, shrink_mat)


def last_kernel(*refs, experts):
    blocks, gate_mat, up_mat, shrink_mat, result_in, grad_in, out, hidden, pre, result, grad = refs
    cap = blocks.shape[0] // (2 * experts)
    j = pl.program_id(0)

    @pl.when(j == 0)
    def _():
        result[...] = result_in[...]
        grad[...] = grad_in[...]

    rows_in, grads = split_blocks(blocks, experts)
    act, pre_gate, pre_up = activations(rows_in, grads, gate_mat, up_mat, shrink_mat)
    hidden[...] = act
    pre[:, :TILE] = pre_gate
    pre[:, TILE:] = pre_up
    result[...] += dot_nn(act, shrink_mat[...])
    grad[...] += dot_nt(pre_gate, gate_mat[...]) + dot_nt(pre_up, up_mat[...])

    @pl.when(j == pl.num_programs(0) - 1)
    def _():
        for e in range(experts):
            r = pl.ds(e * cap, cap)
            out[pl.ds(2 * e * cap, cap), :] = result[r, :].astype(bf16)
            out[pl.ds((2 * e + 1) * cap, cap), :] = grad[r, :].astype(bf16)


def expert_last(blocks, mat, shrink_mat, sums, place, tiles, experts):
    height, width = blocks.shape
    size = height // 2
    return pl.pallas_call(
        functools.partial(last_kernel, experts=experts),
        grid=(tiles,),
        in_specs=[once((height, width))]
        + [column_tiles(width), column_tiles(width, tiles), row_tiles(width, place)]
        + [once((size, width))] * 2,
        out_specs=[
            full((height, width)),
            pl.BlockSpec((size, TILE), lambda j: (0, j)),
            pl.BlockSpec((size, 2 * TILE), lambda j: (0, j)),
        ],
        out_shape=[
            jax.ShapeDtypeStruct((height, width), bf16),
            jax.ShapeDtypeStruct((size, tiles * TILE), bf16),
            jax.ShapeDtypeStruct((size, 2 * tiles * TILE), bf16),
        ],
        scratch_shapes=[pltpu.VMEM((size, width), f32)] * 2,
        compiler_params=pltpu.CompilerParams(
            dimension_semantics=("arbitrary",), vmem_limit_bytes=40 << 20
        ),
        cost_estimate=cost(3.0e-6 * tiles),
        name="expert_last",
    )(blocks, mat, mat, shrink_mat, *sums)


def weights_kernel(*refs, experts):
    turned, hidden, pre, refs = refs[:MB], refs[MB : 2 * MB], refs[2 * MB : 3 * MB], refs[3 * MB :]
    blocks, (_, expand_grad, shrink_grad) = refs[:MB], refs[MB:]
    grads_in = []
    for m in range(MB):
        _, grads = split_blocks(blocks[m], experts)
        grads_in.append(grads)
    expand_grad[...], shrink_grad[...] = weight_grads(turned, hidden, pre, grads_in)


def expert_weights(turned, hidden, pre, blocks, shrink_grad, place, tiles, experts):
    height, width = blocks[0].shape
    size = height // 2
    return pl.pallas_call(
        functools.partial(weights_kernel, experts=experts),
        grid=(tiles,),
        in_specs=[once((width, size))] * MB
        + [column_tiles(size)] * MB
        + [column_tiles(size, 0, 2 * TILE)] * MB
        + [once((height, width))] * MB
        + [pl.BlockSpec(memory_space=pl.ANY)],
        out_specs=[column_tiles(width, 0, 2 * TILE), row_tiles(width, place)],
        out_shape=[
            jax.ShapeDtypeStruct((width, 2 * tiles * TILE), bf16),
            jax.ShapeDtypeStruct((FF, width), bf16),
        ],
        input_output_aliases={4 * MB: 1},
        compiler_params=pltpu.CompilerParams(
            dimension_semantics=("arbitrary",), vmem_limit_bytes=40 << 20
        ),
        cost_estimate=cost(3.0e-6 * tiles),
        name="expert_weights",
    )(*turned, *hidden, *pre, *blocks, shrink_grad)


def adam_kernel(scales, master, first_old, second, gradient, *refs):
    master_out, first_out, second_out = refs[-3:]
    grad = gradient[...].astype(f32)
    first_new = beta_first * first_old[...] + (1.0 - beta_first) * grad
    second_new = beta_second * second[...] + (1.0 - beta_second) * grad * grad
    step = (first_new / scales[0]) / (jnp.sqrt(second_new / scales[1]) + adam_floor)
    master_out[...] = master[...] - scales[2] * (step + decay_rate * master[...])
    first_out[...] = first_new
    second_out[...] = second_new


def adam_expand(scales, states, gradient, kept, place, tiles):
    rows = states[0].shape[0]
    window = pl.BlockSpec((rows, TILE), lambda h, j, _: (0, h * (FF // TILE) + place + j))
    first = kept is None
    return pl.pallas_call(
        adam_kernel,
        grid_spec=pltpu.PrefetchScalarGridSpec(
            num_scalar_prefetch=1,
            grid=(2, tiles),
            in_specs=[window] * 3
            + [pl.BlockSpec((rows, TILE), lambda h, j, _: (0, 2 * j + h))]
            + ([] if first else [pl.BlockSpec(memory_space=pl.ANY)] * 3),
            out_specs=[window] * 3,
        ),
        out_shape=[jax.ShapeDtypeStruct(states[0].shape, f32)] * 3,
        input_output_aliases={} if first else {5: 0, 6: 1, 7: 2},
        cost_estimate=cost(1.5e-6 * tiles),
        name="adam",
    )(scales, *states, gradient, *(() if first else kept))


def inverse_root(values):
    return lax.rsqrt(jnp.mean(values * values, axis=-1, keepdims=True) + epsilon_norm)


def norm_back(values, gain, grad):
    root = inverse_root(values)
    scaled = grad * gain
    inner = jnp.mean(scaled * values, axis=-1, keepdims=True)
    grad_values = root * scaled - values * (root * root * root * inner)
    return grad_values, jnp.sum(grad * values * root, axis=0, keepdims=True)


def adam_update(master, first_old, second, gradient, counter, learn_rate):
    first_new = beta_first * first_old + (1.0 - beta_first) * gradient
    second_new = beta_second * second + (1.0 - beta_second) * gradient * gradient
    first_hat = first_new / (1.0 - beta_first**counter)
    second_hat = second_new / (1.0 - beta_second**counter)
    master_new = master - learn_rate * (
        first_hat / (jnp.sqrt(second_hat) + adam_floor) + decay_rate * master
    )
    return (master_new, first_new, second_new)


def after(values, *earlier):
    if isinstance(values, list):
        return list(lax.optimization_barrier((*values, *earlier))[: len(values)])
    return lax.optimization_barrier((values,) + earlier)[0]


def body(
    tokens,
    lengths,
    routes,
    cotangent,
    step_count,
    qkv_master,
    qkv_first,
    qkv_second,
    proj_master,
    proj_first,
    proj_second,
    table_master,
    table_first,
    table_second,
    gains_master,
    gains_first,
    gains_second,
    router_master,
    router_first,
    router_second,
    expand_master,
    expand_first,
    expand_second,
    shrink_master,
    shrink_first,
    shrink_second,
):
    experts = lax.axis_size("expert")
    devices = lax.axis_size("dp")
    length, width = tokens.shape[2], tokens.shape[3]
    heads = width // HEAD
    capacity = 5 * length // (2 * experts)
    slots = experts * capacity
    rows = MB * length
    ring = Ring()
    lower = lax.axis_index("expert") % 2 == 0

    def mine(values):
        half = values.shape[-1] // 2
        return jnp.where(lower, values[..., :half], values[..., half:])

    def joined(own, others):
        return [jnp.where(lower, own, others), jnp.where(lower, others, own)]

    small = jnp.concatenate(
        [table_master.reshape(-1), gains_master.reshape(-1), router_master.reshape(-1)]
    ).astype(bf16)
    small, small_marks = gather_small(small)
    cut_one = table_master.size
    cut_two = cut_one + gains_master.size
    table_vals = small[:, :cut_one].reshape(BUCKETS, heads).astype(f32)
    gains = small[:, cut_one:cut_two].reshape(devices, 2, width // devices)
    gains = gains.transpose(1, 0, 2).reshape(2, width).astype(f32)
    router_mat = small[:, cut_two:].reshape(width, experts)

    half = width // 2
    dense_half = jnp.concatenate(
        [mine(qkv_master[:, i * width : (i + 1) * width]) for i in range(3)] + [mine(proj_master)],
        axis=1,
    ).astype(bf16)
    if devices > RING_LIMIT:
        dense_own = lax.all_gather(dense_half, "dp", axis=0, tiled=True)
    else:
        moving = Moving(ring, [dense_half])
        for hop in range(devices // 2):
            moving.advance(small_marks[hop - 1] if 0 < hop <= len(small_marks) else None)
        dense_own = moving.placed(0).reshape(width, 2 * width)
    dense = [dense_own, swap(dense_own, "expert", 1)]

    ends = np.cumsum((0, *PARTS)) * TILE

    def expand_part(p):
        start, stop = ends[p], ends[p + 1]
        return [
            expand_master[0][:, start + shift : stop + shift].astype(bf16) for shift in (0, FF)
        ]

    shrink_rows = shrink_master.shape[1]
    cut = shrink_rows // 2
    first_local, last_local = (jnp.concatenate(expand_part(p), axis=1) for p in range(2))
    shrink_local = shrink_master[0].astype(bf16)
    mark = dense[1]
    if devices <= RING_LIMIT:
        moving = Moving(ring, [first_local, shrink_local])
        mark = moving.advance(mark)

    distance = (-np.arange(length)) % length
    onehot = jnp.asarray(
        (distance_buckets(length)[distance][:, None] == np.arange(BUCKETS)).astype(np.float32)
    )
    bias_rows = jnp.einsum("cb,bh->hc", onehot, table_vals, precision=HIGHEST)
    bias_rows = jnp.pad(
        bias_rows.reshape(heads // 2, 2, length), ((0, 0), (0, 6), (0, 0))
    )
    length_now = lengths[:, 0]
    me = lax.axis_index("expert")
    core = lax.rem(me, 2)
    infos = [jnp.stack([length_now[m], core]) for m in range(MB)]
    inputs = tokens.reshape(rows, width)
    normed_one, packed = enter(inputs, gains[0:1], dense)

    route_rows = routes.reshape(rows, 2)
    gradient = cotangent.reshape(rows, width)
    router_lanes = jnp.pad(router_mat, ((0, 0), (0, 128 - experts)))

    def exchange(blocks):
        blocks = blocks.reshape(experts, 2 * capacity, width)
        blocks = lax.all_to_all(blocks, "expert", split_axis=0, concat_axis=0, tiled=True)
        return blocks.reshape(2 * slots, width)

    mixed, state, normed_two, aux, expert_rows = [], [], [], [], []
    for m in range(MB):
        source = packed if m == 0 else after(packed, state[-1], mark)
        mixed.append(attend(m, infos[m], source, bias_rows, length))
        state_now, normed_now, aux_now, sent = route(
            m,
            infos[m],
            inputs,
            mixed[m],
            dense,
            gains[1:2],
            router_lanes,
            route_rows,
            gradient,
            experts,
            capacity,
        )
        state.append(state_now)
        normed_two.append(normed_now)
        aux.append(aux_now)
        if m > 0 and devices <= RING_LIMIT:
            sent = after(sent, moving.advance(state[0]), expert_rows[0])
        expert_rows.append(exchange(sent))

    if devices > RING_LIMIT:
        first_mat = lax.all_gather(first_local, "dp", axis=0, tiled=True)
        members = jnp.zeros((1,), jnp.int32)
        shrink_mat = lax.all_gather(shrink_local, "dp", axis=0, tiled=True)
    else:
        for hop in range(3, devices // 2 + 1):
            mark = moving.advance({3: state[1], 4: expert_rows[1]}.get(hop))
            if hop == GATE:
                last_local = after(last_local, mark)
        first_mat = [piece for _, _, piece in moving.arrived[0]]
        members = jnp.stack(
            [
                ring.member(offset) * first_local.shape[0] + row
                for offset, row, _ in moving.arrived[0]
            ]
        )
        shrink_mat = moving.placed(1).reshape(FF, width)
    last_mat = lax.all_gather(last_local, "dp", axis=0, tiled=True)

    block = width // devices
    share, shrink_grad, *middle = expert_first(
        expert_rows, first_mat, members, shrink_mat, PARTS[0], experts
    )
    expand_grads = [lax.psum_scatter(share, "dp", scatter_dimension=0, tiled=True)]
    returned, hidden, pre = [], [], []
    for m in range(MB):
        blocks, hidden_now, pre_now = expert_last(
            expert_rows[m] if m == 0 else after(expert_rows[m], returned[-1]),
            last_mat,
            shrink_mat,
            middle[2 * m : 2 * m + 2],
            PARTS[0],
            PARTS[1],
            experts,
        )
        hidden.append(hidden_now)
        pre.append(pre_now)
        returned.append(blocks)
    returned = [exchange(blocks) for blocks in returned]
    share, shrink_grad = expert_weights(
        middle[2 * MB :], hidden, pre, expert_rows, shrink_grad, *PARTS, experts
    )
    shrink_grad = shrink_grad.reshape(devices, 2 * cut, width)

    router_rows = router_mat.astype(f32).T
    counter = step_count[0].astype(f32)
    scales = jnp.stack([1.0 - beta_first**counter, 1.0 - beta_second**counter, rate_expand])
    expand_states = (expand_master[0], expand_first[0], expand_second[0])
    def shared(left, right):
        middle = right.shape[1] // 2
        sent = swap(dot_tn(left, right[:, middle:]).astype(bf16), "expert", 1)
        share = dot_tn(left, right[:, :middle]) + sent.astype(f32)
        return share.astype(bf16).reshape(devices, block, middle)

    last_share = share.reshape(devices, block, -1)
    scattering = Scattering(
        ring,
        [(last_share, block, last_share.shape[2], 0, 0)],
        [(shrink_grad, cut, width, i, 0) for i in range(2)],
    )
    combined, sums = [], []
    grad_packed = ()
    scattering.start(share, returned[0])
    mark = share
    for m in range(MB):
        blocks = after(returned[m], mark)
        combined.append(
            combine(
                m,
                infos[m],
                aux[m],
                route_rows,
                state[m],
                gradient,
                gains[1:2],
                router_rows,
                dense,
                blocks,
                experts,
            )
        )
        grad_mixed = combined[m][3]
        if m == MB - 1:
            grad_attn = jnp.concatenate([values[2] for values in combined], axis=0)
            proj_share = shared(jnp.concatenate(mixed, axis=0), grad_attn)
            grad_mixed = after(grad_mixed, proj_share)
        *grad_packed, sums_now = attend_back(
            m, infos[m], packed, bias_rows, grad_mixed, grad_packed
        )
        sums.append(sums_now)
        if m == 0:
            mark = scattering.settle(sums_now)
            scattering.start(returned[1])
    (grad_packed,) = grad_packed
    layer_out, _, _, _, grad_logits, gain_sums = (jnp.stack(values) for values in zip(*combined))
    gains_two_grad = jnp.sum(gain_sums, axis=(0, 1))
    router_grad = jnp.einsum(
        "mtd,mte->de",
        jnp.stack(normed_two).astype(f32),
        grad_logits[:, :, :experts],
        precision=HIGHEST,
    )
    qkv_share = shared(normed_one, grad_packed)
    expand_new = adam_expand(
        scales, expand_states, after(expand_grads[0], qkv_share), None, 0, PARTS[0]
    )
    dense_scattering = Scattering(
        ring,
        *(
            [
                (qkv_share, block // 2, 3 * half, i, 0),
                (proj_share, block // 2, half, i, 0),
            ]
            for i in range(2)
        ),
    )
    dense_scattering.start()
    table_grad = jnp.einsum(
        "hc,cb->bh",
        (sums[0] + sums[1])[:, :2].reshape(heads, length),
        onehot,
        precision=HIGHEST,
    )
    token_grad, gains_one_grad = leave(
        inputs,
        gains[0:1],
        dense,
        grad_packed,
        [values[1] for values in combined],
        dense_scattering.blocks[0],
    )

    flat = jnp.concatenate(
        [
            table_grad.reshape(devices, -1),
            jnp.stack([gains_one_grad[0], gains_two_grad])
            .reshape(2, devices, block)
            .transpose(1, 0, 2)
            .reshape(devices, -1),
            router_grad.reshape(devices, -1),
        ],
        axis=1,
    )
    flat, small_marks = sum_small(flat)
    flat = flat[ring.me]
    table_grad = flat[:cut_one].reshape(table_master.shape)
    gains_grad = flat[cut_one:cut_two].reshape(gains_master.shape)
    router_grad = flat[cut_two:].reshape(router_master.shape)

    if devices <= RING_LIMIT:
        scattering.settle(dense_scattering.blocks[0])
        scattering.start()
        mark = dense_scattering.settle(token_grad)
        scattering.settle(mark)
        scattering.start()
        for hop in range(2, devices // 2 + 1):
            dense_scattering.start(small_marks[hop - 2])
            if hop == 4:
                scattering.settle(mark)
            mark = dense_scattering.settle(*expand_new[:1] if hop == 2 else ())
    done = dense_scattering.finish()
    done = jnp.concatenate(done, axis=0)
    last_grad, shrink_grad = scattering.finish()
    expand_grads.append(last_grad)
    shrink_grad = jnp.concatenate([shrink_grad[:, :width], shrink_grad[:, width:]], axis=0)
    bit = 2
    while bit < experts:
        done = done.astype(bf16)
        done = done.astype(f32) + swap(done, "expert", bit).astype(f32)
        bit *= 2
    others = swap(done, "expert", 1)

    parts = [
        joined(done[:, i * half : (i + 1) * half], others[:, i * half : (i + 1) * half])
        for i in range(4)
    ]
    qkv_grad = jnp.concatenate(parts[0] + parts[1] + parts[2], axis=1)
    proj_grad = jnp.concatenate(parts[3], axis=1)

    states = (
        (qkv_master, qkv_first, qkv_second, qkv_grad),
        (proj_master, proj_first, proj_second, proj_grad),
        (table_master, table_first, table_second, table_grad),
        (gains_master, gains_first, gains_second, gains_grad),
        (router_master, router_first, router_second, router_grad),
        (shrink_master, shrink_first, shrink_second, shrink_grad[None]),
    )
    fresh = []
    for (master, first_old, second, gradient), learn_rate in zip(states, rate_table):
        fresh.append(adam_update(master, first_old, second, gradient, counter, learn_rate))
    kept = adam_expand(scales, expand_states, expand_grads[1], expand_new, PARTS[0], PARTS[1])
    fresh.insert(5, tuple(value[None] for value in kept))
    fresh = [value for group in fresh for value in group]
    return (
        layer_out.reshape(MB, 1, length, width),
        token_grad.reshape(MB, 1, length, width),
        *fresh,
    )


def solution(mesh):
    sequences = P(None, ("dp", "expert"), None, None)
    over_rows = P("dp", None)
    over_columns = P(None, "dp")
    by_expert = P("expert", "dp", None)
    weights = (
        (over_rows,) * 9 + (over_columns,) * 3 + (over_rows,) * 3 + (by_expert,) * 6
    )
    return jax.shard_map(
        body,
        mesh=mesh,
        in_specs=(sequences, P(None, ("dp", "expert")), sequences, sequences, P()) + weights,
        out_specs=(sequences, sequences) + weights,
        check_vma=False,
    )
```

```python
import functools

import jax
import jax.numpy as jnp
import numpy as np
from jax import lax
from jax.experimental import pallas as pl
from jax.experimental.pallas import tpu as pltpu
from jax.sharding import PartitionSpec as P

HEAD = 64
FF = 2816
BUCKETS = 32
MB = 2
TILE = 256
PARTS = (7, 4)
RING_LIMIT = 8
GATE = 4

HIGHEST = lax.Precision.HIGHEST
f32 = jnp.float32
bf16 = jnp.bfloat16
epsilon_norm = 1e-06
beta_first = 0.9
beta_second = 0.95
adam_floor = 1e-08
decay_rate = 0.1
rate_table = (0.03, 0.1, 0.3, 0.1, 0.03, 0.03)
rate_expand = np.float32(0.03)
tanh_scale = 0.7978845608028654
tanh_cubic = 0.044715


def dot_nn(a, b):
    return lax.dot_general(a, b, (((1,), (0,)), ((), ())), preferred_element_type=f32)


def dot_nt(a, b):
    return lax.dot_general(a, b, (((1,), (1,)), ((), ())), preferred_element_type=f32)


def dot_tn(a, b):
    return lax.dot_general(a, b, (((0,), (0,)), ((), ())), preferred_element_type=f32)


def cost(seconds):
    return pl.CostEstimate(
        flops=int(seconds * 1e15), transcendentals=0, bytes_accessed=int(seconds * 3e12)
    )


def distance_buckets(length):
    spread = np.arange(length)
    exact_span = BUCKETS // 2
    scaled = np.log(np.maximum(spread, 1) / exact_span) / np.log(128.0 / exact_span)
    farther = np.minimum(
        exact_span + (scaled * (BUCKETS - exact_span)).astype(np.int64), BUCKETS - 1
    )
    return np.where(spread < exact_span, spread, farther).astype(np.int32)


def ring_order(count):
    if count % 2:
        return list(range(count))
    return list(range(0, count, 2)) + list(range(count - 1, 0, -2))


class Ring:
    def __init__(self):
        self.count = n = lax.axis_size("dp")
        self.order = ring_order(n)
        self.me = me = lax.axis_index("dp")
        if n % 2:
            place = me
        else:
            place = jnp.where(me % 2 == 0, me // 2, n - (me + 1) // 2)
        self.others = []
        for offset in range(1, n if n <= RING_LIMIT else 1):
            other = lax.rem(place + offset, n)
            if n % 2 == 0:
                other = jnp.where(other < n // 2, 2 * other, 2 * n - 1 - 2 * other)
            self.others.append(other)

    def member(self, offset):
        offset %= self.count
        return self.others[offset - 1] if offset else self.me

    def step(self, values, way):
        n, order = self.count, self.order
        pairs = [(order[i], order[(i + way) % n]) for i in range(n)]
        return lax.ppermute(values, "dp", pairs)


class Moving:
    def __init__(self, ring, blocks):
        self.ring = ring
        self.ahead, self.behind = list(blocks), list(blocks)
        self.hops = 0
        self.arrived = [[(0, 0, block)] for block in blocks]

    def advance(self, gate=None):
        self.hops += 1
        hop, count = self.hops, len(self.ahead)
        ahead, behind = self.ahead, self.behind
        cuts = [0] * count
        if hop == self.ring.count // 2:
            cuts = [block.shape[0] // 2 for block in ahead]
            ahead = [block[:cut] for block, cut in zip(ahead, cuts)]
            behind = [block[cut:] for block, cut in zip(behind, cuts)]
        blocks = (*ahead, *behind)
        if gate is not None:
            blocks = lax.optimization_barrier((*blocks, gate))[:-1]
        blocks = lax.optimization_barrier(
            tuple(self.ring.step(block, 1 if k < count else -1) for k, block in enumerate(blocks))
        )
        self.ahead, self.behind = blocks[:count], blocks[count:]
        for k in range(count):
            self.arrived[k].append((-hop, 0, self.ahead[k]))
            self.arrived[k].append((hop, cuts[k], self.behind[k]))
        return blocks[0]

    def placed(self, k):
        block = self.arrived[k][0][2]
        whole = jnp.zeros((self.ring.count,) + block.shape, block.dtype)
        for offset, row, block in self.arrived[k]:
            index = (self.ring.member(offset), row) + (0,) * (block.ndim - 1)
            whole = lax.dynamic_update_slice(
                whole, block[None], index, allow_negative_indices=False
            )
        return whole


class Scattering:
    def __init__(self, ring, top, bottom):
        self.ring, self.groups, self.hops = ring, (top, bottom), 0
        self.alone = ring.count > RING_LIMIT
        self.blocks = [top[0][0]]
        if not self.alone:
            self.add(None)

    def add(self, received, gates=()):
        self.blocks = add_shares(received, self.groups, self.hops, self.ring, gates)

    def start(self, *gates):
        if not self.alone:
            blocks = after(list(self.blocks), *gates)
            self.received = [self.ring.step(block, way) for block, way in zip(blocks, (1, -1))]

    def settle(self, *gates):
        if self.alone:
            return gates[0]
        self.hops += 1
        self.add(self.received, gates)
        return self.blocks[0]

    def finish(self):
        if not self.alone:
            return self.blocks
        return [
            jnp.concatenate(
                [
                    lax.psum_scatter(
                        shares[:, r * i : r * (i + 1), c * j : c * (j + 1)],
                        "dp",
                        scatter_dimension=0,
                    ).astype(f32)
                    for shares, r, c, i, j in group
                ],
                axis=1,
            )
            for group in self.groups
        ]


def add_kernel(members, *refs, counts, rows, hop, last):
    received, refs = (refs[:2], refs[2:]) if hop else ((), refs)
    ways = 1 if last else 2
    for way in range(ways):
        start_row = 0
        for g in range(2):
            if hop == 0 and g != way:
                continue
            windows, refs = refs[: counts[g]], refs[counts[g] :]
            start = 0
            for window in windows:
                span = pl.ds(start, window.shape[-1])
                value = window[0].astype(f32)
                for side in (0, 1) if last else (way,):
                    if hop > 1:
                        value = value + received[side][pl.ds(start_row, rows[g]), span].astype(f32)
                    elif hop == 1 and side == g:
                        value = value + received[side][:, span].astype(f32)
                if last:
                    out, r = refs_out(refs, 2)[g], pl.ds(0, rows[g])
                elif hop == 0:
                    out, r = refs_out(refs, 2)[way], pl.ds(0, rows[g])
                else:
                    out, r = refs_out(refs, 2)[way], pl.ds(start_row, rows[g])
                out[r, span] = value.astype(out.dtype)
                start += window.shape[-1]
            start_row += rows[g]


def refs_out(refs, count):
    return refs[len(refs) - count :]


def add_shares(received, groups, hop, ring, gates):
    last = hop == ring.count // 2
    rows = [group[0][1] for group in groups]
    widths = [sum(window[2] for window in group) for group in groups]
    distance = ring.count // 2 - hop
    members = [ring.member(distance), ring.member(-distance)]
    in_specs, operands = [], []
    for block in received or ():
        in_specs.append(pl.BlockSpec(block.shape, lambda i, _: (0, 0)))
        operands.append(block)
    for way in range(1 if last else 2):
        for g, group in enumerate(groups):
            if hop == 0 and g != way:
                continue
            for shares, r, c, row, column in group:
                in_specs.append(
                    pl.BlockSpec(
                        (1, r, c),
                        lambda i, members, way=way, row=row, column=column: (
                            members[way],
                            row,
                            column,
                        ),
                    )
                )
                operands.append(shares)
    in_specs += [pl.BlockSpec(memory_space=pl.ANY) for _ in gates]
    operands += gates
    if last:
        outs = [jax.ShapeDtypeStruct(shape, f32) for shape in zip(rows, widths)]
    elif hop == 0:
        outs = [jax.ShapeDtypeStruct(shape, bf16) for shape in zip(rows, widths)]
    else:
        outs = [jax.ShapeDtypeStruct((sum(rows), widths[0]), bf16)] * 2
    return pl.pallas_call(
        functools.partial(
            add_kernel, counts=[len(group) for group in groups], rows=rows, hop=hop, last=last
        ),
        grid_spec=pltpu.PrefetchScalarGridSpec(
            num_scalar_prefetch=1,
            grid=(1,),
            in_specs=in_specs,
            out_specs=[pl.BlockSpec(out.shape, lambda i, _: (0, 0)) for out in outs],
        ),
        out_shape=outs,
        cost_estimate=cost(3e-6),
        name="add_shares",
    )(jnp.stack(members), *operands)


def swap(values, axis, bit):
    count = lax.axis_size(axis)
    return lax.ppermute(values, axis, [(i, i ^ bit) for i in range(count)])


def gather_small(values):
    count = lax.axis_size("dp")
    rows = values[None]
    bit = 1
    marks = []
    while bit < count:
        rows = jnp.concatenate([rows, swap(rows, "dp", bit)], axis=0)
        marks.append(rows)
        bit *= 2
    return rows[jnp.arange(count) ^ lax.axis_index("dp")], marks


def sum_small(values):
    marks = []
    for axis in ("expert", "dp"):
        bit = 1
        while bit < lax.axis_size(axis):
            values = values + swap(values, axis, bit)
            marks.append(values)
            bit *= 2
    return values, marks


def head_probs(query, key, bias_row, length):
    seq = query.shape[0]
    scores = dot_nt(query, key) * HEAD ** (-0.5)
    bias = pltpu.roll(
        jnp.broadcast_to(bias_row, (seq, seq)), 0, 1, stride=1, stride_axis=0
    )
    row = lax.broadcasted_iota(jnp.int32, (seq, seq), 0)
    column = lax.broadcasted_iota(jnp.int32, (seq, seq), 1)
    scores = jnp.where((column <= row) & (column < length), scores + bias, -1e30)
    exps = jnp.exp(scores - jnp.max(scores, axis=1, keepdims=True))
    return exps / jnp.sum(exps, axis=1, keepdims=True)


def attend_kernel(info, query, key, value, bias_rows, mixed):
    length = info[0]
    for half in range(2):
        c = pl.ds(HEAD * half, HEAD)
        probs = head_probs(query[:, c], key[:, c], bias_rows[0, half : half + 1, :], length)
        mixed[:, c] = dot_nn(probs.astype(bf16), value[:, c]).astype(bf16)


def diagonal_sums(values):
    seq = values.shape[0]
    eight = values[0:8, :]
    for t in range(1, seq // 8):
        eight = eight + pltpu.roll(values[8 * t : 8 * t + 8, :], seq - 8 * t, 1)
    total = eight[0:1, :]
    for t in range(1, 8):
        total = total + pltpu.roll(eight, seq - t, 1)[t : t + 1, :]
    return total


def attend_back_kernel(info, query, key, value, bias_rows, grad, *refs):
    grad_packed, sums = refs[-2:]
    seq = query.shape[0]
    h = pl.program_id(0)
    length, core = info[0], info[1]
    places = packed_places(h, pl.num_programs(0), core)
    offsets = [pl.multiple_of(place * 2 * HEAD, 2 * HEAD) for place in places]
    parts = [[], [], []]
    for half in range(2):
        c = pl.ds(HEAD * half, HEAD)
        q, k, v, g = query[:, c], key[:, c], value[:, c], grad[:, c]
        probs = head_probs(q, k, bias_rows[0, half : half + 1, :], length)
        grad_probs = dot_nt(g, v)
        scores = probs * (grad_probs - jnp.sum(probs * grad_probs, axis=1, keepdims=True))
        rounded = scores.astype(bf16)
        parts[0].append((dot_nn(rounded, k) * HEAD ** (-0.5)).astype(bf16))
        parts[1].append((dot_tn(rounded, q) * HEAD ** (-0.5)).astype(bf16))
        parts[2].append(dot_tn(probs.astype(bf16), g).astype(bf16))
        sums[0, half : half + 1, :] = diagonal_sums(scores)
    sums[0, 2:8, :] = jnp.zeros((6, seq), f32)
    for offset, part in zip(offsets, parts):
        grad_packed[:, pl.ds(offset, 2 * HEAD)] = jnp.concatenate(part, axis=1)


def packed_places(h, pairs, core):
    half = pairs // 2
    first = jnp.where(h // half == core, 0, 3 * half) + lax.rem(h, half)
    return first, first + half, first + 2 * half


def pair_windows(m, seq, pairs):
    return [
        pl.BlockSpec(
            (seq, 2 * HEAD),
            lambda h, info, part=part: (m, packed_places(h, pairs, info[1])[part]),
        )
        for part in range(3)
    ]


def attend(m, info, packed, bias_rows, seq):
    width = packed.shape[1] // 3
    pairs = width // (2 * HEAD)
    return pl.pallas_call(
        attend_kernel,
        grid_spec=pltpu.PrefetchScalarGridSpec(
            num_scalar_prefetch=1,
            grid=(pairs,),
            in_specs=pair_windows(m, seq, pairs)
            + [pl.BlockSpec((1, 8, seq), lambda h, _: (h, 0, 0))],
            out_specs=pl.BlockSpec((seq, 2 * HEAD), lambda h, _: (0, h)),
        ),
        out_shape=jax.ShapeDtypeStruct((seq, width), bf16),
        cost_estimate=cost(10e-6),
        name="attend",
    )(info, packed, packed, packed, bias_rows)


def attend_back(m, info, packed, bias_rows, grad, kept):
    seq, width = grad.shape
    pairs = width // (2 * HEAD)

    return pl.pallas_call(
        attend_back_kernel,
        grid_spec=pltpu.PrefetchScalarGridSpec(
            num_scalar_prefetch=1,
            grid=(pairs,),
            in_specs=pair_windows(m, seq, pairs)
            + [
                pl.BlockSpec((1, 8, seq), lambda h, _: (h, 0, 0)),
                pl.BlockSpec((seq, 2 * HEAD), lambda h, _: (0, h)),
            ]
            + [pl.BlockSpec(memory_space=pl.ANY) for _ in kept],
            out_specs=[
                pl.BlockSpec((seq, 3 * width), lambda h, _: (m, 0)),
                pl.BlockSpec((1, 8, seq), lambda h, _: (h, 0, 0)),
            ],
        ),
        out_shape=[
            jax.ShapeDtypeStruct(packed.shape, bf16),
            jax.ShapeDtypeStruct((pairs, 8, seq), f32),
        ],
        input_output_aliases={6: 0} if kept else {},
        cost_estimate=cost(16e-6),
        name="attend_back",
    )(info, packed, packed, packed, bias_rows, grad, *kept)


SLOT_LANE, GATE_LANE = 16, 18


def halves(values, core):
    half = values.shape[1] // 2
    turned = jnp.concatenate([values[:, half:], values[:, :half]], axis=1)
    return jnp.where(core == 0, values, turned)


def pick_table(slot, slots):
    lane = lax.broadcasted_iota(jnp.int32, (slot.shape[0], slots), 1).astype(f32)
    return jnp.where(lane == slot, 1.0, 0.0).astype(bf16)


def route_kernel(info, inputs, mixed, *refs, capacity):
    pieces, refs = refs[:2], refs[2:]
    gain, router, routes, cotangent, state, normed, aux, out = refs
    length, core = info[0], info[1]
    seq = inputs.shape[0]
    experts = out.shape[0] // (2 * capacity)
    added = jnp.concatenate([dot_nn(mixed[...], piece[...]) for piece in pieces], axis=1)
    values = inputs[...].astype(f32) + halves(added, core)
    state[...] = values
    rows = (values * inverse_root(values) * gain[...]).astype(bf16)
    normed[...] = rows
    logits = dot_nn(rows, router[...])
    lane = lax.broadcasted_iota(jnp.int32, logits.shape, 1)
    logits = jnp.where(lane < experts, logits, -1e30)
    exps = jnp.exp(logits - jnp.max(logits, axis=1, keepdims=True))
    probs = exps / jnp.sum(exps, axis=1, keepdims=True)
    live = lax.broadcasted_iota(jnp.int32, (seq, 1), 0) < length
    named = [routes[:, k : k + 1] for k in range(2)]
    hits = [jnp.where((lane == name) & live, 1.0, 0.0) for name in named]
    before = lax.broadcasted_iota(jnp.int32, (seq, seq), 0) > lax.broadcasted_iota(
        jnp.int32, (seq, seq), 1
    )
    earlier = dot_nn(
        jnp.where(before, 1.0, 0.0).astype(bf16), (hits[0] + hits[1]).astype(bf16)
    )
    grad_out = jnp.where(live, cotangent[...], 0.0)
    kept = probs
    picks, grads = [], []
    for k in range(2):
        rank = jnp.sum(hits[k] * earlier, axis=1, keepdims=True)
        slot = (named[k] * capacity).astype(f32) + rank
        slot = jnp.where(live, slot, float(experts * capacity))
        gate = jnp.sum(hits[k] * probs, axis=1, keepdims=True)
        kept = jnp.where(lane == SLOT_LANE + k, slot, kept)
        kept = jnp.where(lane == GATE_LANE + k, gate, kept)
        picks.append(pick_table(slot, experts * capacity))
        grads.append((gate * grad_out).astype(bf16))
    aux[...] = kept
    sent = dot_tn(picks[0] + picks[1], rows).astype(bf16)
    sent_grads = (dot_tn(picks[0], grads[0]) + dot_tn(picks[1], grads[1])).astype(bf16)
    for e in range(experts):
        r = slice(e * capacity, (e + 1) * capacity)
        out[pl.ds(2 * e * capacity, capacity), :] = sent[r, :]
        out[pl.ds((2 * e + 1) * capacity, capacity), :] = sent_grads[r, :]


def whole(shape):
    return pl.BlockSpec(shape, lambda i, _: (0,) * len(shape))


def part(m, shape):
    return pl.BlockSpec(shape, lambda i, _: (m,) + (0,) * (len(shape) - 1))


def proj_part(pieces):
    width = pieces[0].shape[0]
    return [pl.BlockSpec((width, width // 2), lambda i, _: (0, 3)) for _ in pieces]


def route(m, info, inputs, mixed, pieces, gain, router, routes, cotangent, experts, capacity):
    width = inputs.shape[1]
    seq = inputs.shape[0] // MB
    big = (seq, width)
    outs = [
        jax.ShapeDtypeStruct(big, f32),
        jax.ShapeDtypeStruct(big, bf16),
        jax.ShapeDtypeStruct((seq, 128), f32),
        jax.ShapeDtypeStruct((2 * experts * capacity, width), bf16),
    ]
    return pl.pallas_call(
        functools.partial(route_kernel, capacity=capacity),
        grid_spec=pltpu.PrefetchScalarGridSpec(
            num_scalar_prefetch=1,
            grid=(1,),
            in_specs=[part(m, big), whole(big)]
            + proj_part(pieces)
            + [whole(gain.shape), whole(router.shape), part(m, (seq, 2)), part(m, big)],
            out_specs=[whole(out.shape) for out in outs],
        ),
        out_shape=outs,
        cost_estimate=cost(8e-6),
        name="route",
    )(info, inputs, mixed, *pieces, gain, router, routes, cotangent)


def combine_kernel(info, aux, routes, state, cotangent, gain, router_rows, *refs, experts):
    pieces, blocks, refs = refs[:2], refs[2], refs[3:]
    layer_out, grad_state, grad_attn, grad_mixed, grad_logits, gain_grad = refs
    length, core = info[0], info[1]
    seq = state.shape[0]
    capacity = blocks.shape[0] // (2 * experts)
    result, back = split_blocks(blocks, experts)
    lane = lax.broadcasted_iota(jnp.int32, aux.shape, 1)
    probs = jnp.where(lane < experts, aux[...], 0.0)
    live = lax.broadcasted_iota(jnp.int32, (seq, 1), 0) < length
    grad_out = jnp.where(live, cotangent[...], 0.0)
    picks, mixture, grad_probs = [], 0.0, 0.0
    for k in range(2):
        picks.append(pick_table(aux[:, SLOT_LANE + k : SLOT_LANE + k + 1], experts * capacity))
        picked = dot_nn(picks[k], result)
        mixture = mixture + aux[:, GATE_LANE + k : GATE_LANE + k + 1] * picked
        grad_gate = jnp.sum(grad_out * picked, axis=1, keepdims=True)
        grad_probs = grad_probs + jnp.where(lane == routes[:, k : k + 1], grad_gate, 0.0)
    values = state[...]
    layer_out[...] = jnp.where(live, values + mixture, 0.0).astype(bf16)
    logits = probs * (grad_probs - jnp.sum(probs * grad_probs, axis=1, keepdims=True))
    grad_logits[...] = logits
    grad = dot_nn(picks[0] + picks[1], back)
    for e in range(experts):
        grad = grad + logits[:, e : e + 1] * router_rows[e : e + 1, :]
    grad_norm, gain_sum = norm_back(values, gain[...], grad)
    gain_grad[...] = gain_sum
    total = grad_out + grad_norm
    grad_state[...] = total
    turned = halves(total.astype(bf16), core)
    grad_attn[...] = turned
    half = turned.shape[1] // 2
    grad_mixed[...] = (
        dot_nt(turned[:, :half], pieces[0][...]) + dot_nt(turned[:, half:], pieces[1][...])
    ).astype(bf16)


def combine(m, info, aux, routes, state, cotangent, gain, router_rows, pieces, blocks, experts):
    seq, width = state.shape
    big = (seq, width)
    outs = [
        jax.ShapeDtypeStruct(big, bf16),
        jax.ShapeDtypeStruct(big, f32),
        jax.ShapeDtypeStruct(big, bf16),
        jax.ShapeDtypeStruct(big, bf16),
        jax.ShapeDtypeStruct((seq, 128), f32),
        jax.ShapeDtypeStruct((1, width), f32),
    ]
    return pl.pallas_call(
        functools.partial(combine_kernel, experts=experts),
        grid_spec=pltpu.PrefetchScalarGridSpec(
            num_scalar_prefetch=1,
            grid=(1,),
            in_specs=[whole(aux.shape), part(m, (seq, 2)), whole(big), part(m, big)]
            + [whole(gain.shape), whole(router_rows.shape)]
            + proj_part(pieces)
            + [whole(blocks.shape)],
            out_specs=[whole(out.shape) for out in outs],
        ),
        out_shape=outs,
        cost_estimate=cost(8e-6),
        name="combine",
    )(info, aux, routes, state, cotangent, gain, router_rows, *pieces, blocks)


def enter_kernel(inputs, gain, *refs):
    pieces, (normed, packed) = refs[:2], refs[2:]
    values = inputs[...].astype(f32)
    rows = (values * inverse_root(values) * gain[...]).astype(bf16)
    normed[...] = rows
    span = pieces[0].shape[1] * 3 // 4
    for i, piece in enumerate(pieces):
        packed[:, i * span : (i + 1) * span] = dot_nn(rows, piece[:, :span]).astype(bf16)


def enter(inputs, gain, pieces):
    rows, width = inputs.shape
    return pl.pallas_call(
        enter_kernel,
        out_shape=[
            jax.ShapeDtypeStruct((rows, width), bf16),
            jax.ShapeDtypeStruct((rows, 3 * width), bf16),
        ],
        cost_estimate=cost(9e-6),
        compiler_params=pltpu.CompilerParams(vmem_limit_bytes=48 << 20),
        name="enter",
    )(inputs, gain, *pieces)


def leave_kernel(inputs, gain, *refs):
    pieces, (packed, *states), (_, out, gain_grad) = refs[:2], refs[2 : 3 + MB], refs[3 + MB :]
    seq = states[0].shape[0]
    span = pieces[0].shape[1] * 3 // 4
    total = 0.0
    for m in range(MB):
        r = pl.ds(m * seq, seq)
        grad = sum(
            dot_nt(packed[r, i * span : (i + 1) * span], piece[:, :span])
            for i, piece in enumerate(pieces)
        )
        grad_norm, gain_sum = norm_back(inputs[r, :].astype(f32), gain[...], grad)
        out[r, :] = states[m][...] + grad_norm
        total = total + gain_sum
    gain_grad[...] = total


def leave(inputs, gain, pieces, packed, states, gate):
    operands = (inputs, gain, *pieces, packed, *states)
    return pl.pallas_call(
        leave_kernel,
        in_specs=[pl.BlockSpec(memory_space=pltpu.VMEM) for _ in operands]
        + [pl.BlockSpec(memory_space=pl.ANY)],
        out_shape=[
            jax.ShapeDtypeStruct(inputs.shape, f32),
            jax.ShapeDtypeStruct(gain.shape, f32),
        ],
        cost_estimate=cost(12e-6),
        compiler_params=pltpu.CompilerParams(vmem_limit_bytes=48 << 20),
        name="leave",
    )(*operands, gate)


def activations(rows_in, grads_in, gate_mat, up_mat, shrink_mat):
    gate = dot_nn(rows_in, gate_mat[...])
    up = dot_nn(rows_in, up_mat[...])
    grad = dot_nt(grads_in, shrink_mat[...])
    bent = jnp.tanh(tanh_scale * (gate + tanh_cubic * (gate * gate * gate)))
    half = 0.5 * (1.0 + bent)
    gelu = gate * half
    slope = half + gate * (0.5 * (1.0 - bent * bent)) * (
        tanh_scale * (1.0 + 3.0 * tanh_cubic * gate * gate)
    )
    return (gelu * up).astype(bf16), (slope * up * grad).astype(bf16), (gelu * grad).astype(bf16)


def split_blocks(blocks, experts):
    cap = blocks.shape[0] // (2 * experts)
    return (
        jnp.concatenate(
            [blocks[pl.ds((2 * e + i) * cap, cap), :] for e in range(experts)], axis=0
        )
        for i in range(2)
    )


def weight_grads(turned, hidden, pre, grads_in):
    expand_grad = sum(dot_nn(turned[m][...], pre[m][...]) for m in range(MB))
    shrink_grad = sum(dot_tn(hidden[m][...], grads_in[m]) for m in range(MB))
    return expand_grad.astype(bf16), shrink_grad.astype(bf16)


def first_kernel(members, *refs, experts, pieces):
    blocks, refs = refs[:MB], refs[MB:]
    mats, refs = refs[:pieces], refs[pieces:]
    (shrink_mat, expand_grad, shrink_grad), refs = refs[:3], refs[3:]
    sums, turned, refs = refs[: 2 * MB], refs[2 * MB : 3 * MB], refs[3 * MB :]
    hidden, pre, mats_whole = refs[:MB], refs[MB : 2 * MB], refs[2 * MB :]
    cap = blocks[0].shape[0] // (2 * experts)
    if pieces == 2:
        gate_mat, up_mat = mats
    else:
        gate_mat, up_mat = mats_whole
        for k, piece in enumerate(mats):
            count = piece.shape[0]
            r = pl.ds(pl.multiple_of(members[k % (pieces // 2)], count), count)
            mats_whole[k // (pieces // 2)][r, :] = piece[...]

    @pl.when(pl.program_id(0) == 0)
    def _():
        for total in sums:
            total[...] = jnp.zeros_like(total)
        for m in range(MB):
            for e in range(experts):
                rows_now = blocks[m][pl.ds(2 * e * cap, cap), :]
                turned[m][:, e * cap : (e + 1) * cap] = rows_now.T

    grads_in = []
    for m in range(MB):
        rows_in, grads = split_blocks(blocks[m], experts)
        grads_in.append(grads)
        act, pre_gate, pre_up = activations(rows_in, grads, gate_mat, up_mat, shrink_mat)
        hidden[m][...] = act
        pre[m][:, :TILE] = pre_gate
        pre[m][:, TILE:] = pre_up
        sums[2 * m][...] += dot_nn(act, shrink_mat[...])
        sums[2 * m + 1][...] += dot_nt(pre_gate, gate_mat[...]) + dot_nt(pre_up, up_mat[...])
    expand_grad[...], shrink_grad[...] = weight_grads(turned, hidden, pre, grads_in)


def full(shape, **options):
    return pl.BlockSpec(shape, lambda j, *_: (0, 0), **options)


def once(shape):
    return full(shape, pipeline_mode=pl.Buffered(1))


def column_tiles(rows, place=0, size=TILE):
    return pl.BlockSpec((rows, size), lambda j, *_: (0, place + j))


def row_tiles(width, place):
    return pl.BlockSpec((TILE, width), lambda j, *_: (place + j, 0))


def expert_first(blocks, mat, members, shrink_mat, tiles, experts):
    height, width = blocks[0].shape
    size = height // 2
    if isinstance(mat, list):
        mat_specs = [
            column_tiles(piece.shape[0], place) for place in (0, tiles) for piece in mat
        ]
        mat, whole_mats = mat * 2, [pltpu.VMEM((width, TILE), bf16)] * 2
    else:
        mat_specs = [column_tiles(width), column_tiles(width, tiles)]
        mat, whole_mats = [mat, mat], []
    return pl.pallas_call(
        functools.partial(first_kernel, experts=experts, pieces=len(mat)),
        grid_spec=pltpu.PrefetchScalarGridSpec(
            num_scalar_prefetch=1,
            grid=(tiles,),
            in_specs=[once((height, width))] * MB + mat_specs + [row_tiles(width, 0)],
            out_specs=[column_tiles(width, 0, 2 * TILE), row_tiles(width, 0)]
            + [full((size, width))] * (2 * MB)
            + [full((width, size))] * MB,
            scratch_shapes=[pltpu.VMEM((size, TILE), bf16)] * MB
            + [pltpu.VMEM((size, 2 * TILE), bf16)] * MB
            + whole_mats,
        ),
        out_shape=[
            jax.ShapeDtypeStruct((width, 2 * tiles * TILE), bf16),
            jax.ShapeDtypeStruct((FF, width), bf16),
        ]
        + [jax.ShapeDtypeStruct((size, width), f32)] * (2 * MB)
        + [jax.ShapeDtypeStruct((width, size), bf16)] * MB,
        compiler_params=pltpu.CompilerParams(
            dimension_semantics=("arbitrary",), vmem_limit_bytes=58 << 20
        ),
        cost_estimate=cost(8.5e-6 * tiles),
        name="expert",
    )(members, *blocks, *mat, shrink_mat)


def last_kernel(*refs, experts):
    blocks, gate_mat, up_mat, shrink_mat, result_in, grad_in, out, hidden, pre, result, grad = refs
    cap = blocks.shape[0] // (2 * experts)
    j = pl.program_id(0)

    @pl.when(j == 0)
    def _():
        result[...] = result_in[...]
        grad[...] = grad_in[...]

    rows_in, grads = split_blocks(blocks, experts)
    act, pre_gate, pre_up = activations(rows_in, grads, gate_mat, up_mat, shrink_mat)
    hidden[...] = act
    pre[:, :TILE] = pre_gate
    pre[:, TILE:] = pre_up
    result[...] += dot_nn(act, shrink_mat[...])
    grad[...] += dot_nt(pre_gate, gate_mat[...]) + dot_nt(pre_up, up_mat[...])

    @pl.when(j == pl.num_programs(0) - 1)
    def _():
        for e in range(experts):
            r = pl.ds(e * cap, cap)
            out[pl.ds(2 * e * cap, cap), :] = result[r, :].astype(bf16)
            out[pl.ds((2 * e + 1) * cap, cap), :] = grad[r, :].astype(bf16)


def expert_last(blocks, mat, shrink_mat, sums, place, tiles, experts):
    height, width = blocks.shape
    size = height // 2
    return pl.pallas_call(
        functools.partial(last_kernel, experts=experts),
        grid=(tiles,),
        in_specs=[once((height, width))]
        + [column_tiles(width), column_tiles(width, tiles), row_tiles(width, place)]
        + [once((size, width))] * 2,
        out_specs=[
            full((height, width)),
            pl.BlockSpec((size, TILE), lambda j: (0, j)),
            pl.BlockSpec((size, 2 * TILE), lambda j: (0, j)),
        ],
        out_shape=[
            jax.ShapeDtypeStruct((height, width), bf16),
            jax.ShapeDtypeStruct((size, tiles * TILE), bf16),
            jax.ShapeDtypeStruct((size, 2 * tiles * TILE), bf16),
        ],
        scratch_shapes=[pltpu.VMEM((size, width), f32)] * 2,
        compiler_params=pltpu.CompilerParams(
            dimension_semantics=("arbitrary",), vmem_limit_bytes=40 << 20
        ),
        cost_estimate=cost(3.0e-6 * tiles),
        name="expert_last",
    )(blocks, mat, mat, shrink_mat, *sums)


def weights_kernel(*refs, experts):
    turned, hidden, pre, refs = refs[:MB], refs[MB : 2 * MB], refs[2 * MB : 3 * MB], refs[3 * MB :]
    blocks, (_, expand_grad, shrink_grad) = refs[:MB], refs[MB:]
    grads_in = []
    for m in range(MB):
        _, grads = split_blocks(blocks[m], experts)
        grads_in.append(grads)
    expand_grad[...], shrink_grad[...] = weight_grads(turned, hidden, pre, grads_in)


def expert_weights(turned, hidden, pre, blocks, shrink_grad, place, tiles, experts):
    height, width = blocks[0].shape
    size = height // 2
    return pl.pallas_call(
        functools.partial(weights_kernel, experts=experts),
        grid=(tiles,),
        in_specs=[once((width, size))] * MB
        + [column_tiles(size)] * MB
        + [column_tiles(size, 0, 2 * TILE)] * MB
        + [once((height, width))] * MB
        + [pl.BlockSpec(memory_space=pl.ANY)],
        out_specs=[column_tiles(width, 0, 2 * TILE), row_tiles(width, place)],
        out_shape=[
            jax.ShapeDtypeStruct((width, 2 * tiles * TILE), bf16),
            jax.ShapeDtypeStruct((FF, width), bf16),
        ],
        input_output_aliases={4 * MB: 1},
        compiler_params=pltpu.CompilerParams(
            dimension_semantics=("arbitrary",), vmem_limit_bytes=40 << 20
        ),
        cost_estimate=cost(3.0e-6 * tiles),
        name="expert_weights",
    )(*turned, *hidden, *pre, *blocks, shrink_grad)


def adam_kernel(scales, master, first_old, second, gradient, *refs):
    master_out, first_out, second_out = refs[-3:]
    grad = gradient[...].astype(f32)
    first_new = beta_first * first_old[...] + (1.0 - beta_first) * grad
    second_new = beta_second * second[...] + (1.0 - beta_second) * grad * grad
    step = (first_new / scales[0]) / (jnp.sqrt(second_new / scales[1]) + adam_floor)
    master_out[...] = master[...] - scales[2] * (step + decay_rate * master[...])
    first_out[...] = first_new
    second_out[...] = second_new


def adam_expand(scales, states, gradient, kept, place, tiles):
    rows = states[0].shape[0]
    window = pl.BlockSpec((rows, TILE), lambda h, j, _: (0, h * (FF // TILE) + place + j))
    first = kept is None
    return pl.pallas_call(
        adam_kernel,
        grid_spec=pltpu.PrefetchScalarGridSpec(
            num_scalar_prefetch=1,
            grid=(2, tiles),
            in_specs=[window] * 3
            + [pl.BlockSpec((rows, TILE), lambda h, j, _: (0, 2 * j + h))]
            + ([] if first else [pl.BlockSpec(memory_space=pl.ANY)] * 3),
            out_specs=[window] * 3,
        ),
        out_shape=[jax.ShapeDtypeStruct(states[0].shape, f32)] * 3,
        input_output_aliases={} if first else {5: 0, 6: 1, 7: 2},
        cost_estimate=cost(1.5e-6 * tiles),
        name="adam",
    )(scales, *states, gradient, *(() if first else kept))


def inverse_root(values):
    return lax.rsqrt(jnp.mean(values * values, axis=-1, keepdims=True) + epsilon_norm)


def norm_back(values, gain, grad):
    root = inverse_root(values)
    scaled = grad * gain
    inner = jnp.mean(scaled * values, axis=-1, keepdims=True)
    grad_values = root * scaled - values * (root * root * root * inner)
    return grad_values, jnp.sum(grad * values * root, axis=0, keepdims=True)


def adam_update(master, first_old, second, gradient, counter, learn_rate):
    first_new = beta_first * first_old + (1.0 - beta_first) * gradient
    second_new = beta_second * second + (1.0 - beta_second) * gradient * gradient
    first_hat = first_new / (1.0 - beta_first**counter)
    second_hat = second_new / (1.0 - beta_second**counter)
    master_new = master - learn_rate * (
        first_hat / (jnp.sqrt(second_hat) + adam_floor) + decay_rate * master
    )
    return (master_new, first_new, second_new)


def after(values, *earlier):
    if isinstance(values, list):
        return list(lax.optimization_barrier((*values, *earlier))[: len(values)])
    return lax.optimization_barrier((values,) + earlier)[0]


def body(
    tokens,
    lengths,
    routes,
    cotangent,
    step_count,
    qkv_master,
    qkv_first,
    qkv_second,
    proj_master,
    proj_first,
    proj_second,
    table_master,
    table_first,
    table_second,
    gains_master,
    gains_first,
    gains_second,
    router_master,
    router_first,
    router_second,
    expand_master,
    expand_first,
    expand_second,
    shrink_master,
    shrink_first,
    shrink_second,
):
    experts = lax.axis_size("expert")
    devices = lax.axis_size("dp")
    length, width = tokens.shape[2], tokens.shape[3]
    heads = width // HEAD
    capacity = 5 * length // (2 * experts)
    slots = experts * capacity
    rows = MB * length
    ring = Ring()
    lower = lax.axis_index("expert") % 2 == 0

    def mine(values):
        half = values.shape[-1] // 2
        return jnp.where(lower, values[..., :half], values[..., half:])

    def joined(own, others):
        return [jnp.where(lower, own, others), jnp.where(lower, others, own)]

    small = jnp.concatenate(
        [table_master.reshape(-1), gains_master.reshape(-1), router_master.reshape(-1)]
    ).astype(bf16)
    small, small_marks = gather_small(small)
    cut_one = table_master.size
    cut_two = cut_one + gains_master.size
    table_vals = small[:, :cut_one].reshape(BUCKETS, heads).astype(f32)
    gains = small[:, cut_one:cut_two].reshape(devices, 2, width // devices)
    gains = gains.transpose(1, 0, 2).reshape(2, width).astype(f32)
    router_mat = small[:, cut_two:].reshape(width, experts)

    half = width // 2
    dense_half = jnp.concatenate(
        [mine(qkv_master[:, i * width : (i + 1) * width]) for i in range(3)] + [mine(proj_master)],
        axis=1,
    ).astype(bf16)
    if devices > RING_LIMIT:
        dense_own = lax.all_gather(dense_half, "dp", axis=0, tiled=True)
    else:
        moving = Moving(ring, [dense_half])
        for hop in range(devices // 2):
            moving.advance(small_marks[hop - 1] if 0 < hop <= len(small_marks) else None)
        dense_own = moving.placed(0).reshape(width, 2 * width)
    dense = [dense_own, swap(dense_own, "expert", 1)]

    ends = np.cumsum((0, *PARTS)) * TILE

    def expand_part(p):
        start, stop = ends[p], ends[p + 1]
        return [
            expand_master[0][:, start + shift : stop + shift].astype(bf16) for shift in (0, FF)
        ]

    shrink_rows = shrink_master.shape[1]
    cut = shrink_rows // 2
    first_local, last_local = (jnp.concatenate(expand_part(p), axis=1) for p in range(2))
    shrink_local = shrink_master[0].astype(bf16)
    mark = dense[1]
    if devices <= RING_LIMIT:
        moving = Moving(ring, [first_local, shrink_local])
        mark = moving.advance(mark)

    distance = (-np.arange(length)) % length
    onehot = jnp.asarray(
        (distance_buckets(length)[distance][:, None] == np.arange(BUCKETS)).astype(np.float32)
    )
    bias_rows = jnp.einsum("cb,bh->hc", onehot, table_vals, precision=HIGHEST)
    bias_rows = jnp.pad(
        bias_rows.reshape(heads // 2, 2, length), ((0, 0), (0, 6), (0, 0))
    )
    length_now = lengths[:, 0]
    me = lax.axis_index("expert")
    core = lax.rem(me, 2)
    infos = [jnp.stack([length_now[m], core]) for m in range(MB)]
    inputs = tokens.reshape(rows, width)
    normed_one, packed = enter(inputs, gains[0:1], dense)

    route_rows = routes.reshape(rows, 2)
    gradient = cotangent.reshape(rows, width)
    router_lanes = jnp.pad(router_mat, ((0, 0), (0, 128 - experts)))

    def exchange(blocks):
        blocks = blocks.reshape(experts, 2 * capacity, width)
        blocks = lax.all_to_all(blocks, "expert", split_axis=0, concat_axis=0, tiled=True)
        return blocks.reshape(2 * slots, width)

    mixed, state, normed_two, aux, expert_rows = [], [], [], [], []
    for m in range(MB):
        source = packed if m == 0 else after(packed, state[-1], mark)
        mixed.append(attend(m, infos[m], source, bias_rows, length))
        state_now, normed_now, aux_now, sent = route(
            m,
            infos[m],
            inputs,
            mixed[m],
            dense,
            gains[1:2],
            router_lanes,
            route_rows,
            gradient,
            experts,
            capacity,
        )
        state.append(state_now)
        normed_two.append(normed_now)
        aux.append(aux_now)
        if m > 0 and devices <= RING_LIMIT:
            sent = after(sent, moving.advance(state[0]), expert_rows[0])
        expert_rows.append(exchange(sent))

    if devices > RING_LIMIT:
        first_mat = lax.all_gather(first_local, "dp", axis=0, tiled=True)
        members = jnp.zeros((1,), jnp.int32)
        shrink_mat = lax.all_gather(shrink_local, "dp", axis=0, tiled=True)
    else:
        for hop in range(3, devices // 2 + 1):
            mark = moving.advance({3: state[1], 4: expert_rows[1]}.get(hop))
            if hop == GATE:
                last_local = after(last_local, mark)
        first_mat = [piece for _, _, piece in moving.arrived[0]]
        members = jnp.stack(
            [
                ring.member(offset) * first_local.shape[0] + row
                for offset, row, _ in moving.arrived[0]
            ]
        )
        shrink_mat = moving.placed(1).reshape(FF, width)
    last_mat = lax.all_gather(last_local, "dp", axis=0, tiled=True)

    block = width // devices
    share, shrink_grad, *middle = expert_first(
        expert_rows, first_mat, members, shrink_mat, PARTS[0], experts
    )
    expand_grads = [lax.psum_scatter(share, "dp", scatter_dimension=0, tiled=True)]
    returned, hidden, pre = [], [], []
    for m in range(MB):
        blocks, hidden_now, pre_now = expert_last(
            expert_rows[m] if m == 0 else after(expert_rows[m], returned[-1]),
            last_mat,
            shrink_mat,
            middle[2 * m : 2 * m + 2],
            PARTS[0],
            PARTS[1],
            experts,
        )
        hidden.append(hidden_now)
        pre.append(pre_now)
        returned.append(blocks)
    returned = [exchange(blocks) for blocks in returned]
    share, shrink_grad = expert_weights(
        middle[2 * MB :], hidden, pre, expert_rows, shrink_grad, *PARTS, experts
    )
    shrink_grad = shrink_grad.reshape(devices, 2 * cut, width)

    router_rows = router_mat.astype(f32).T
    counter = step_count[0].astype(f32)
    scales = jnp.stack([1.0 - beta_first**counter, 1.0 - beta_second**counter, rate_expand])
    expand_states = (expand_master[0], expand_first[0], expand_second[0])
    def shared(left, right):
        middle = right.shape[1] // 2
        sent = swap(dot_tn(left, right[:, middle:]).astype(bf16), "expert", 1)
        share = dot_tn(left, right[:, :middle]) + sent.astype(f32)
        return share.astype(bf16).reshape(devices, block, middle)

    last_share = share.reshape(devices, block, -1)
    scattering = Scattering(
        ring,
        [(last_share, block, last_share.shape[2], 0, 0)],
        [(shrink_grad, cut, width, i, 0) for i in range(2)],
    )
    combined, sums = [], []
    grad_packed = ()
    scattering.start(share, returned[0])
    mark = share
    for m in range(MB):
        blocks = after(returned[m], mark)
        combined.append(
            combine(
                m,
                infos[m],
                aux[m],
                route_rows,
                state[m],
                gradient,
                gains[1:2],
                router_rows,
                dense,
                blocks,
                experts,
            )
        )
        grad_mixed = combined[m][3]
        if m == MB - 1:
            grad_attn = jnp.concatenate([values[2] for values in combined], axis=0)
            proj_share = shared(jnp.concatenate(mixed, axis=0), grad_attn)
            grad_mixed = after(grad_mixed, proj_share)
        *grad_packed, sums_now = attend_back(
            m, infos[m], packed, bias_rows, grad_mixed, grad_packed
        )
        sums.append(sums_now)
        if m == 0:
            mark = scattering.settle(sums_now)
            scattering.start(returned[1])
    (grad_packed,) = grad_packed
    layer_out, _, _, _, grad_logits, gain_sums = (jnp.stack(values) for values in zip(*combined))
    gains_two_grad = jnp.sum(gain_sums, axis=(0, 1))
    router_grad = jnp.einsum(
        "mtd,mte->de",
        jnp.stack(normed_two).astype(f32),
        grad_logits[:, :, :experts],
        precision=HIGHEST,
    )
    qkv_share = shared(normed_one, grad_packed)
    expand_new = adam_expand(
        scales, expand_states, after(expand_grads[0], qkv_share), None, 0, PARTS[0]
    )
    dense_scattering = Scattering(
        ring,
        *(
            [
                (qkv_share, block // 2, 3 * half, i, 0),
                (proj_share, block // 2, half, i, 0),
            ]
            for i in range(2)
        ),
    )
    dense_scattering.start()
    table_grad = jnp.einsum(
        "hc,cb->bh",
        (sums[0] + sums[1])[:, :2].reshape(heads, length),
        onehot,
        precision=HIGHEST,
    )
    token_grad, gains_one_grad = leave(
        inputs,
        gains[0:1],
        dense,
        grad_packed,
        [values[1] for values in combined],
        dense_scattering.blocks[0],
    )

    flat = jnp.concatenate(
        [
            table_grad.reshape(devices, -1),
            jnp.stack([gains_one_grad[0], gains_two_grad])
            .reshape(2, devices, block)
            .transpose(1, 0, 2)
            .reshape(devices, -1),
            router_grad.reshape(devices, -1),
        ],
        axis=1,
    )
    flat, small_marks = sum_small(flat)
    flat = flat[ring.me]
    table_grad = flat[:cut_one].reshape(table_master.shape)
    gains_grad = flat[cut_one:cut_two].reshape(gains_master.shape)
    router_grad = flat[cut_two:].reshape(router_master.shape)

    if devices <= RING_LIMIT:
        scattering.settle(dense_scattering.blocks[0])
        scattering.start()
        mark = dense_scattering.settle(token_grad)
        scattering.settle(mark)
        scattering.start()
        for hop in range(2, devices // 2 + 1):
            dense_scattering.start(small_marks[hop - 2])
            if hop == 4:
                scattering.settle(mark)
            mark = dense_scattering.settle(*expand_new[:1] if hop == 2 else ())
    done = dense_scattering.finish()
    done = jnp.concatenate(done, axis=0)
    last_grad, shrink_grad = scattering.finish()
    expand_grads.append(last_grad)
    shrink_grad = jnp.concatenate([shrink_grad[:, :width], shrink_grad[:, width:]], axis=0)
    bit = 2
    while bit < experts:
        done = done.astype(bf16)
        done = done.astype(f32) + swap(done, "expert", bit).astype(f32)
        bit *= 2
    others = swap(done, "expert", 1)

    parts = [
        joined(done[:, i * half : (i + 1) * half], others[:, i * half : (i + 1) * half])
        for i in range(4)
    ]
    qkv_grad = jnp.concatenate(parts[0] + parts[1] + parts[2], axis=1)
    proj_grad = jnp.concatenate(parts[3], axis=1)

    states = (
        (qkv_master, qkv_first, qkv_second, qkv_grad),
        (proj_master, proj_first, proj_second, proj_grad),
        (table_master, table_first, table_second, table_grad),
        (gains_master, gains_first, gains_second, gains_grad),
        (router_master, router_first, router_second, router_grad),
        (shrink_master, shrink_first, shrink_second, shrink_grad[None]),
    )
    fresh = []
    for (master, first_old, second, gradient), learn_rate in zip(states, rate_table):
        fresh.append(adam_update(master, first_old, second, gradient, counter, learn_rate))
    kept = adam_expand(
        scales,
        expand_states,
        after(expand_grads[1], fresh[0][1], fresh[1][1]),
        expand_new,
        PARTS[0],
        PARTS[1],
    )
    fresh.insert(5, tuple(value[None] for value in kept))
    fresh = [value for group in fresh for value in group]
    return (
        layer_out.reshape(MB, 1, length, width),
        token_grad.reshape(MB, 1, length, width),
        *fresh,
    )


def solution(mesh):
    sequences = P(None, ("dp", "expert"), None, None)
    over_rows = P("dp", None)
    over_columns = P(None, "dp")
    by_expert = P("expert", "dp", None)
    weights = (
        (over_rows,) * 9 + (over_columns,) * 3 + (over_rows,) * 3 + (by_expert,) * 6
    )
    return jax.shard_map(
        body,
        mesh=mesh,
        in_specs=(sequences, P(None, ("dp", "expert")), sequences, sequences, P()) + weights,
        out_specs=(sequences, sequences) + weights,
        check_vma=False,
    )
```
